32 devices in a mesh: gx: 4 (over x, core), gy: 8 (over z, y).
Axes of the slice: x: 2, y: 2, z: 4, core: 2. Of those that a mesh axis runs over, the one named last changes fastest.
Arguments:
- rock_type: int32 [64, 256, 512], P('gx', 'gy'), may hold values from 0 to 7
- rock_perm: float32 [8], replicated, may hold values from 0.05 to 0.5
- rock_poro: float32 [8], replicated, may hold values from 0.1 to 0.35
- base_flux: float32 [64, 256, 512], P('gx', 'gy'), may hold values from 0.5 to 2
- initial_pressure: float32 [64, 256, 512], P('gx', 'gy'), may hold values from -6 to 6
- old_saturation: float32 [64, 256, 512], P('gx', 'gy'), may hold values from 0 to 1
- well_cells: int32 [3, 128], replicated, may hold values from 0 to 511, as said below
- well_rates: float32 [128], replicated, may hold values from -2 to 2
Outputs:
- pressure: float32 [64, 256, 512], P('gx', 'gy')
- saturation: float32 [64, 256, 512], P('gx', 'gy')
The draws below stay inside these ranges and needn't reach their ends.
Inputs may be any that keep to these rules, and one draw needn't show every extreme that they name: `well_cells`: row 0 holds first coordinates below 64, row 1 second coordinates below 256, row 2 third coordinates below 512. The first well lies in the last cell of the grid and the second in the first cell; wells may share a cell.
All inputs are finite; a program needn't handle non-finite values.
Results may differ from the reference program's by a relative error of at most 0.0003.
Values sent between devices are 32-bit elements; how exact they have to be, the bound alone decides.
No kernel may reach another device: no remote copies, remote signals or barrier semaphores. Data moves between devices by JAX's collectives and lax.ppermute only.
A program may use at most 64 MiB of HBM per device.

```python
import math
import jax
import jax.numpy as jnp
from jax import lax

PASSES = 4
NEWTON = 3
ROCKS = 8
NX = 64
NY = 256
NZ = 512
WELLS = 128


def draw_well_cells(key, part):
    first_key, second_key, third_key = jax.random.split(jax.random.fold_in(key, 17), 3)
    coord_x = jax.random.randint(first_key, (WELLS,), 0, NX)
    coord_y = jax.random.randint(second_key, (WELLS,), 0, NY)
    coord_z = jax.random.randint(third_key, (WELLS,), 0, NZ)
    coord_x = coord_x.at[0].set(NX - 1).at[1].set(0)
    coord_y = coord_y.at[0].set(NY - 1).at[1].set(0)
    coord_z = coord_z.at[0].set(NZ - 1).at[1].set(0)
    return jnp.stack([coord_x, coord_y, coord_z]).astype(jnp.int32)


def place_ends(array, rng, smallest, high):
    shape = array.shape
    index_at = [jax.random.randint(jax.random.fold_in(rng, axis), (), 0, shape[axis]) for axis in range(len(shape))]
    array = array.at[tuple(index_at)].set(smallest)
    longest = shape.index(max(shape))
    index_at[longest] = (index_at[longest] + 1) % shape[longest]
    return array.at[tuple(index_at)].set(high)


def steps_of(rng, shape, cuts, smallest, high):
    gain = 1.0
    for dim, shards_of in cuts:
        heights = jax.random.uniform(jax.random.fold_in(jax.random.fold_in(rng, 6), dim), (shards_of,), jnp.float32, smallest / len(cuts), high / len(cuts))
        gain = gain * jnp.repeat(jnp.exp(heights), shape[dim] // shards_of).reshape((-1,) + (1,) * (len(shape) - 1 - dim))
    return gain


def noise(stream_key, dims, scale, most, shards=(), kind=jnp.bfloat16):
    entries = scale * jax.random.normal(stream_key, dims, jnp.float32)
    if shards:
        entries = entries * steps_of(stream_key, dims, shards, -0.22, 0.18)
    return jnp.clip(entries, -most, most).astype(kind)


def setup_inputs(seed: int = 0) -> dict:
    keys = jax.random.split(jax.random.key(seed), 9)
    rock_type = place_ends(jax.random.randint(keys[0], (NX, NY, NZ), 0, ROCKS), jax.random.fold_in(keys[0], 1), 0, ROCKS - 1).astype(jnp.int32)
    rock_perm = jnp.clip(jnp.exp(jax.random.uniform(keys[1], (ROCKS,), jnp.float32, math.log(0.05), math.log(0.5))), 0.05, 0.5)
    rock_poro = jnp.clip(jax.random.uniform(keys[2], (ROCKS,), jnp.float32, 0.1, 0.35), 0.1, 0.35)
    base_flux = jnp.clip(jnp.exp(math.log(2.0) - 1.3862944 * jax.random.uniform(keys[3], (NX, NY, NZ), jnp.float32) ** steps_of(keys[3], (NX, NY, NZ), ((0, 4), (1, 8)), -0.2, 0.2)), 0.5, 2.0)
    initial_pressure = noise(keys[4], (NX, NY, NZ), 1.0, 6.0, ((0, 4), (1, 8)), jnp.float32)
    old_saturation = jnp.clip(1.0 * jax.random.uniform(keys[5], (NX, NY, NZ), jnp.float32) ** steps_of(keys[5], (NX, NY, NZ), ((0, 4), (1, 8)), -0.2, 0.2), 0.0, 1.0)
    well_cells = draw_well_cells(jax.random.fold_in(keys[8], 71), 0)
    well_rates = jnp.clip(jax.random.uniform(keys[7], (WELLS,), jnp.float32, -2.0, 2.0), -2.0, 2.0)
    return dict(rock_type=rock_type, rock_perm=rock_perm, rock_poro=rock_poro, base_flux=base_flux, initial_pressure=initial_pressure, old_saturation=old_saturation, well_cells=well_cells, well_rates=well_rates)


MOBILITY = 0.5
OMEGA = 0.8
VOLUME = 4.0
COMPRESS = 0.5


def fraction(water):
    denom = water * water + MOBILITY * (1.0 - water) ** 2
    return water * water / denom


def fraction_slope(water):
    denom = water * water + MOBILITY * (1.0 - water) ** 2
    return 2.0 * MOBILITY * water * (1.0 - water) / (denom * denom)


def transmit(left, right):
    total = left + right
    return 2.0 * left * right / jnp.where(total > 0, total, 1.0)


def along_depth(field):
    deeper = jnp.pad(field[:, :, 1:], ((0, 0), (0, 0), (0, 1)))
    shallower = jnp.pad(field[:, :, :-1], ((0, 0), (0, 0), (1, 0)))
    return deeper, shallower


def links(perm_ext):
    center = perm_ext[1:-1, 1:-1]
    deeper, shallower = along_depth(center)
    return (transmit(center, perm_ext[2:, 1:-1]), transmit(center, perm_ext[:-2, 1:-1]),
            transmit(center, perm_ext[1:-1, 2:]), transmit(center, perm_ext[1:-1, :-2]),
            transmit(center, deeper), transmit(center, shallower))


def jacobi(press_ext, perm_ext, storage, source):
    east, west, north, south, below, above = links(perm_ext)
    center = press_ext[1:-1, 1:-1]
    deeper, shallower = along_depth(center)
    flow = (east * (center - press_ext[2:, 1:-1]) + west * (center - press_ext[:-2, 1:-1])
            + north * (center - press_ext[1:-1, 2:]) + south * (center - press_ext[1:-1, :-2])
            + below * (center - deeper) + above * (center - shallower))
    outside = jnp.where(perm_ext[1:-1, 1:-1] > 0, 0.0, 1.0)
    diagonal = storage + east + west + north + south + below + above + outside
    return center + OMEGA * (source - storage * center - flow) / diagonal


def upwind(flux, own, other):
    return jnp.maximum(flux, 0.0) * own + jnp.minimum(flux, 0.0) * other


def water_terms(press_ext, perm_ext, frac_old, frac_side, base_flux, rates_field):
    east, west, north, south, below, above = links(perm_ext)
    center = press_ext[1:-1, 1:-1]
    deeper, shallower = along_depth(center)
    frac_deep, frac_shallow = along_depth(frac_old)
    through = jnp.maximum(base_flux + east * (center - press_ext[2:, 1:-1]), 0.0)
    leaving = (upwind(north * (center - press_ext[1:-1, 2:]), frac_old, frac_side[:, 2:])
               + upwind(south * (center - press_ext[1:-1, :-2]), frac_old, frac_side[:, :-2])
               + upwind(below * (center - deeper), frac_old, frac_deep)
               + upwind(above * (center - shallower), frac_old, frac_shallow))
    explicit = jnp.maximum(rates_field, 0.0) + jnp.minimum(rates_field, 0.0) * frac_old - leaving
    return through, explicit


def sweep(inflow, volume, through, explicit, old_sat):
    def advance(incoming, items):
        vol_row, flux_row, extra_row, start_row = items
        water = start_row
        for _ in range(NEWTON):
            misfit = vol_row * (water - start_row) + flux_row * fraction(water) - incoming - extra_row
            water = jnp.clip(water - misfit / (vol_row + flux_row * fraction_slope(water)), 0.0, 1.0)
        return flux_row * fraction(water), water

    outgoing, saturation = lax.scan(advance, inflow, (volume, through, explicit, old_sat))
    return saturation, outgoing


def lookup(rock_type, table):
    result = jnp.zeros(rock_type.shape, table.dtype)
    for kind in range(table.shape[0]):
        result = jnp.where(rock_type == kind, table[kind], result)
    return result


def well_field(well_cells, well_rates, shape, anchor_x, anchor_y):
    local_x = well_cells[0] - anchor_x
    local_y = well_cells[1] - anchor_y
    local_z = well_cells[2]
    inside = (local_x >= 0) & (local_x < shape[0]) & (local_y >= 0) & (local_y < shape[1]) & (local_z >= 0) & (local_z < shape[2])
    count = shape[0] * shape[1] * shape[2]
    flat = jnp.where(inside, (local_x * shape[1] + local_y) * shape[2] + local_z, count).astype(jnp.int32)
    return jnp.zeros((count,), well_rates.dtype).at[flat].add(well_rates, mode="drop").reshape(shape)


def widen(field):
    return jnp.pad(field, ((1, 1), (1, 1), (0, 0)))


def reference(rock_type, rock_perm, rock_poro, base_flux, initial_pressure, old_saturation, well_cells, well_rates):
    perm = lookup(rock_type, rock_perm)
    volume = VOLUME * lookup(rock_type, rock_poro)
    storage = COMPRESS * volume
    rates_field = well_field(well_cells, well_rates, rock_type.shape, 0, 0)
    source = storage * initial_pressure + rates_field
    perm_ext = widen(perm)
    pressure = initial_pressure
    for _ in range(PASSES):
        pressure = jacobi(widen(pressure), perm_ext, storage, source)
    frac_old = fraction(old_saturation)
    frac_side = jnp.pad(frac_old, ((0, 0), (1, 1), (0, 0)))
    through, explicit = water_terms(widen(pressure), perm_ext, frac_old, frac_side, base_flux, rates_field)
    saturation, _ = sweep(base_flux[0], volume, through, explicit, old_saturation)
    return pressure, saturation
```

```python
import functools

import jax
import jax.numpy as jnp
from jax import lax
from jax.experimental import pallas as pl
from jax.experimental.pallas import tpu as pltpu
from jax.sharding import PartitionSpec as P

PASSES = 4
NEWTON = 3

MOBILITY = 0.5
OMEGA = 0.8
VOLUME = 4.0
COMPRESS = 0.5

LANES = 128
REACH = PASSES + 1
PAD = 8
ANY = pl.BlockSpec(memory_space=pl.ANY)
VMEM = pl.BlockSpec(memory_space=pltpu.VMEM)
SMEM = pl.BlockSpec(memory_space=pltpu.SMEM)


def swap_pairs(axis):
    count = lax.axis_size(axis)
    pairs = []
    for first in (0, 1):
        ups = [(i, i + 1) for i in range(first, count - 1, 2)]
        pairs.append(ups + [(j, i) for i, j in ups])
    return pairs


def swap(value_a, value_b, axis):
    pairs_a, pairs_b = swap_pairs(axis)
    return lax.ppermute(value_a, axis, pairs_a), lax.ppermute(value_b, axis, pairs_b)


def chunks_of(ref):
    return ref.shape[-1] // LANES


def fetch(source, target, sems, start):
    for c in range(target.shape[0]):
        copy = pltpu.make_async_copy(source.at[:, :, pl.ds(c * LANES, LANES)], target.at[c], sems.at[c])
        copy.start() if start else copy.wait()


def pack_kernel(p_ref, rock_ref, sat_ref, ya_ref, yb_ref, xa_ref, xb_ref, p, rock, sat, sems):
    chunks, nx, ny, _ = p.shape
    for i, (source, target) in enumerate(((p_ref, p), (rock_ref, rock), (sat_ref, sat))):
        fetch(source, target, sems.at[i], True)
    for i, (source, target) in enumerate(((p_ref, p), (rock_ref, rock), (sat_ref, sat))):
        fetch(source, target, sems.at[i], False)
    even_y = lax.rem(lax.axis_index("gy"), 2) == 0
    even_x = lax.rem(lax.axis_index("gx"), 2) == 0
    p2, rock2, sat2 = (f.reshape(chunks * nx * ny, LANES) for f in (p, rock, sat))
    rows = (2 * REACH + 1) * nx
    for out, high in ((ya_ref, even_y), (yb_ref, jnp.logical_not(even_y))):
        first = jnp.where(high, ny - REACH, 0)
        edge = jnp.where(high, ny - 1, 0)
        for c in range(chunks):
            base = c * nx * ny
            for j in range(REACH):
                out[pl.ds(c * rows + j * nx, nx), :] = p2[pl.ds(base + first + j, nx, stride=ny), :]
                kinds = rock2[pl.ds(base + first + j, nx, stride=ny), :]
                out[pl.ds(c * rows + (REACH + j) * nx, nx), :] = kinds.astype(jnp.float32) + 1.0
            out[pl.ds(c * rows + 2 * REACH * nx, nx), :] = sat2[pl.ds(base + edge, nx, stride=ny), :]
    for out, high in ((xa_ref, even_x), (xb_ref, jnp.logical_not(even_x))):
        first = jnp.where(high, nx - REACH, 0)
        for c in range(chunks):
            for j in range(REACH):
                out[j, :, pl.ds(c * LANES, LANES)] = p[c, first + j]
                out[REACH + j, :, pl.ds(c * LANES, LANES)] = rock[c, first + j].astype(jnp.float32) + 1.0


def pack(pressure, rock_type, saturation):
    nx, ny, nz = pressure.shape
    chunks = nz // LANES
    side = jax.ShapeDtypeStruct((chunks * (2 * REACH + 1) * nx, LANES), jnp.float32)
    end = jax.ShapeDtypeStruct((2 * REACH, ny, nz), jnp.float32)
    block = (chunks, nx, ny, LANES)
    return pl.pallas_call(
        pack_kernel,
        name="pack",
        out_shape=(side, side, end, end),
        in_specs=[ANY] * 3,
        out_specs=(VMEM,) * 4,
        scratch_shapes=[
            pltpu.VMEM(block, jnp.float32),
            pltpu.VMEM(block, jnp.int32),
            pltpu.VMEM(block, jnp.float32),
            pltpu.SemaphoreType.DMA((3, chunks)),
        ],
    )(pressure, rock_type, saturation)


def corner_kernel(nx, ya_ref, yb_ref, ca_ref, cb_ref):
    rows = (2 * REACH + 1) * nx
    chunks = ya_ref.shape[0] // rows
    even_y = lax.rem(lax.axis_index("gy"), 2) == 0
    even_x = lax.rem(lax.axis_index("gx"), 2) == 0
    for out, high in ((ca_ref, even_x), (cb_ref, jnp.logical_not(even_x))):
        layer = jnp.where(high, nx - PASSES, 0)
        for c in range(chunks):
            for kind in range(2):
                for i in range(PASSES):
                    for side in range(2):
                        start = c * rows + (kind * REACH + 1 - side) * nx + layer + i
                        from_a = ya_ref[pl.ds(start, PASSES, stride=nx), :]
                        from_b = yb_ref[pl.ds(start, PASSES, stride=nx), :]
                        mine = jnp.where(even_y, from_b, from_a) if side == 0 else jnp.where(even_y, from_a, from_b)
                        at = ((c * 2 + kind) * PASSES + i) * 2 + side
                        out[pl.ds(at * PASSES, PASSES), :] = mine


def corners(side_a, side_b, nx):
    chunks = side_a.shape[0] // ((2 * REACH + 1) * nx)
    shape = jax.ShapeDtypeStruct((chunks * 4 * PASSES * PASSES, LANES), jnp.float32)
    return pl.pallas_call(
        functools.partial(corner_kernel, nx),
        name="corners",
        out_shape=(shape, shape),
        in_specs=[VMEM] * 2,
        out_specs=(VMEM,) * 2,
    )(side_a, side_b)


def fraction(water):
    denom = water * water + MOBILITY * (1.0 - water) ** 2
    return water * water / denom


def transmit(left, right):
    return 2.0 * left * right / jnp.maximum(left + right, 1e-30)


def look_up(table, kinds):
    return jnp.take_along_axis(table, kinds, axis=1, mode="promise_in_bounds")


def deeper(values):
    turned = [pltpu.roll(v, LANES - 1, 1) for v in values]
    last = lax.broadcasted_iota(jnp.int32, turned[0].shape, 1) == LANES - 1
    return [jnp.where(last, turned[(c + 1) % len(values)], turned[c]) for c in range(len(values))]


def shallower(values):
    turned = [pltpu.roll(v, 1, 1) for v in values]
    first = lax.broadcasted_iota(jnp.int32, turned[0].shape, 1) == 0
    return [jnp.where(first, turned[c - 1], turned[c]) for c in range(len(values))]


def flow_kernel(
    p_ref, rock_ref, flux_ref, sat_ref, ya_ref, yb_ref, xa_ref, xb_ref, ca_ref, cb_ref, tables_ref, cells_ref, rates_ref,
    press_ref, prep_ref, inlet_ref,
    press, other, kinds, perms, rates, trans_x, trans_y, trans_z, scale, drive, rock, flux, sat, frac, sems,
):
    chunks, layers, pitch, _ = press.shape
    _, nx, ny, _ = rock.shape
    low, depth = PASSES, layers * pitch
    tiles = (ny + 2 * PASSES) // 8
    side_rows = (2 * REACH + 1) * nx
    rank_x, rank_y = lax.axis_index("gx"), lax.axis_index("gy")
    even_x, even_y = lax.rem(rank_x, 2) == 0, lax.rem(rank_y, 2) == 0
    flat = lambda f: f.reshape(chunks * f.shape[1] * f.shape[2], LANES)
    press2, other2, kinds2, perms2, rates2, frac2, rock2, flux2, sat2 = map(flat, (press, other, kinds, perms, rates, frac, rock, flux, sat))

    own_p = press.at[:, pl.ds(low, nx), pl.ds(PAD, ny), :]
    fetch(p_ref, own_p, sems.at[0], True)
    fetch(rock_ref, rock, sems.at[1], True)

    def ends(start, from_low, from_high):
        for c in range(chunks):
            lanes = pl.ds(c * LANES, LANES)
            for i, target in enumerate((press, kinds)):
                a = pltpu.make_async_copy(
                    from_low.at[pl.ds(i * REACH + REACH - low, low), :, lanes],
                    target.at[c, pl.ds(0, low), pl.ds(PAD, ny), :], sems.at[2 + i, c])
                b = pltpu.make_async_copy(
                    from_high.at[pl.ds(i * REACH, REACH), :, lanes],
                    target.at[c, pl.ds(low + nx, REACH), pl.ds(PAD, ny), :], sems.at[4 + i, c])
                for copy in (a, b):
                    copy.start() if start else copy.wait()

    @pl.when(even_x)
    def _():
        ends(True, xb_ref, xa_ref)

    @pl.when(jnp.logical_not(even_x))
    def _():
        ends(True, xa_ref, xb_ref)

    fetch(flux_ref, flux, sems.at[6], True)
    fetch(sat_ref, sat, sems.at[7], True)

    zero = jnp.zeros((8, LANES), jnp.float32)
    sub = lax.broadcasted_iota(jnp.int32, (8, LANES), 0)
    lane = lax.broadcasted_iota(jnp.int32, (8, LANES), 1)

    def clear(layer, _):
        for c in range(chunks):
            for t in range(pitch // 8):
                rates[c, layer, pl.ds(t * 8, 8), :] = zero
            for t in (0, pitch // 8 - 1):
                press[c, layer, pl.ds(t * 8, 8), :] = zero
                kinds[c, layer, pl.ds(t * 8, 8), :] = zero
        return 0

    lax.fori_loop(0, layers, clear, 0)

    def add_well(w, _):
        x = cells_ref[0, w] - rank_x * nx + low
        y = cells_ref[1, w] - rank_y * ny + PAD
        z = cells_ref[2, w]

        @pl.when((x >= 0) & (x < layers) & (y >= 0) & (y < pitch))
        def _():
            row = (lax.shift_right_logical(z, 7) * layers + x) * pitch + y
            tile = pl.multiple_of(lax.shift_left(lax.shift_right_logical(row, 3), 3), 8)
            here = (sub == row - tile) & (lane == lax.bitwise_and(z, LANES - 1))
            rates2[pl.ds(tile, 8), :] = rates2[pl.ds(tile, 8), :] + jnp.where(here, rates_ref[w], 0.0)

        return 0

    lax.fori_loop(0, cells_ref.shape[1], add_well, 0)

    for c in range(chunks):
        for j in range(REACH):
            for i, target in enumerate((press2, kinds2)):
                start = c * side_rows + (i * REACH + j) * nx
                a, b = ya_ref[pl.ds(start, nx), :], yb_ref[pl.ds(start, nx), :]
                at = c * depth + low * pitch + j
                target[pl.ds(at + PAD - REACH, nx, stride=pitch), :] = jnp.where(even_y, b, a)
                target[pl.ds(at + PAD + ny, nx, stride=pitch), :] = jnp.where(even_y, a, b)
        start = c * side_rows + 2 * REACH * nx
        a, b = fraction(ya_ref[pl.ds(start, nx), :]), fraction(yb_ref[pl.ds(start, nx), :])
        at = c * nx * pitch
        frac2[pl.ds(at + PAD - 1, nx, stride=pitch), :] = jnp.where(even_y, b, a)
        frac2[pl.ds(at + PAD + ny, nx, stride=pitch), :] = jnp.where(even_y, a, b)
        for i, target in enumerate((press2, kinds2)):
            for k in range(PASSES):
                for side in range(2):
                    start = (((c * 2 + i) * PASSES + k) * 2 + side) * PASSES
                    a, b = ca_ref[pl.ds(start, PASSES), :], cb_ref[pl.ds(start, PASSES), :]
                    row = PAD - PASSES if side == 0 else PAD + ny
                    at = c * depth + row
                    target[pl.ds(at + k * pitch, PASSES), :] = jnp.where(even_x, b, a)
                    target[pl.ds(at + (low + nx + k) * pitch, PASSES), :] = jnp.where(even_x, a, b)

    fetch(rock_ref, rock, sems.at[1], False)

    def encode(layer, _):
        for c in range(chunks):
            kinds[c, low + layer, pl.ds(PAD, ny), :] = rock[c, layer].astype(jnp.float32) + 1.0
        return 0

    lax.fori_loop(0, nx, encode, 0)
    fetch(p_ref, own_p, sems.at[0], False)
    ends(False, xa_ref, xb_ref)
    perm_table, store_table, volume_table = tables_ref[0], tables_ref[1], tables_ref[2]

    def look(layer, _):
        for c in range(chunks):
            for t in range(pitch // 8):
                kind = kinds[c, layer, pl.ds(t * 8, 8), :].astype(jnp.int32)
                perms[c, layer, pl.ds(t * 8, 8), :] = look_up(perm_table, kind)
        return 0

    lax.fori_loop(0, layers, look, 0)

    def rows_of(ref, layer, k):
        return [ref[pl.ds(c * depth + layer * pitch + PAD - PASSES + k, 8, stride=tiles), :] for c in range(chunks)]

    def tile_of(layer, k):
        return pl.ds(pl.multiple_of((layer * (tiles + 1) + k) * 8, 8), 8)

    def prepare(layer, _):
        perm = {k: rows_of(perms2, layer, k) for k in range(-1, tiles + 1)}
        for k in range(-1, tiles):
            for c in range(chunks):
                trans_y[c, tile_of(layer, k + 1), :] = transmit(perm[k][c], perm[k + 1][c])
        for k in range(tiles):
            ahead = rows_of(perms2, layer + 1, k)
            deep = deeper(perm[k])
            t_z = [transmit(perm[k][c], deep[c]) for c in range(chunks)]
            t_z[-1] = jnp.where(lane == LANES - 1, 0.0, t_z[-1])
            above = shallower(t_z)
            kind = rows_of(kinds2, layer, k)
            start = rows_of(press2, layer, k)
            rate = rows_of(rates2, layer, k)
            for c in range(chunks):
                t_x = transmit(perm[k][c], ahead[c])
                trans_x[c, tile_of(layer, k), :] = t_x
                trans_z[c, tile_of(layer, k), :] = t_z[c]
                t_w = trans_x[c, tile_of(jnp.maximum(layer - 1, 0), k), :]
                t_n, t_s = trans_y[c, tile_of(layer, k + 1), :], trans_y[c, tile_of(layer, k), :]
                store = look_up(store_table, kind[c].astype(jnp.int32))
                factor = OMEGA / (store + ((t_x + t_w) + (t_n + t_s) + (t_z[c] + above[c])))
                scale[c, tile_of(layer, k), :] = factor
                drive[c, tile_of(layer, k), :] = factor * (store * start[c] + rate[c])
        return 0

    lax.fori_loop(0, layers - 1, prepare, 0)

    def sweep_pass(source, target, number):
        def one(layer, _):
            now = {k: rows_of(source, layer, k) for k in range(-1, tiles + 1)}
            for k in range(tiles):
                here = now[k]
                t_z = [trans_z[c, tile_of(layer, k), :] for c in range(chunks)]
                deep = deeper(here)
                shallow = shallower([t_z[c] * here[c] for c in range(chunks)])
                east, west = rows_of(source, layer + 1, k), rows_of(source, layer - 1, k)
                for c in range(chunks):
                    total = (
                        (trans_x[c, tile_of(layer, k), :] * east[c] + trans_x[c, tile_of(layer - 1, k), :] * west[c])
                        + (trans_y[c, tile_of(layer, k + 1), :] * now[k + 1][c] + trans_y[c, tile_of(layer, k), :] * now[k - 1][c])
                        + (t_z[c] * deep[c] + shallow[c])
                    )
                    new = (1.0 - OMEGA) * here[c] + (drive[c, tile_of(layer, k), :] + scale[c, tile_of(layer, k), :] * total)
                    at = c * depth + layer * pitch + PAD - PASSES + k
                    target[pl.ds(at, 8, stride=tiles), :] = new
            return 0

        lax.fori_loop(number, layers - number, one, 0)

    for number in range(1, PASSES + 1):
        source, target = (press2, other2) if number % 2 else (other2, press2)
        sweep_pass(source, target, number)
    final, final2 = (press, press2) if PASSES % 2 == 0 else (other, other2)

    def send_out(start):
        for c in range(chunks):
            copy = pltpu.make_async_copy(
                final.at[c, pl.ds(low, nx), pl.ds(PAD, ny), :], press_ref.at[:, :, pl.ds(c * LANES, LANES)], sems.at[0, c]
            )
            copy.start() if start else copy.wait()

    send_out(True)
    fetch(flux_ref, flux, sems.at[6], False)
    fetch(sat_ref, sat, sems.at[7], False)
    for c in range(chunks):
        inlet_ref[pl.ds(c * ny, ny), :] = flux[c, 0]

    def old_fraction(layer, _):
        for c in range(chunks):
            frac[c, layer, pl.ds(PAD, ny), :] = fraction(sat[c, layer])
        return 0

    lax.fori_loop(0, nx, old_fraction, 0)
    step = ny // 8

    def upwind(flow, own, far):
        return jnp.maximum(flow, 0.0) * own + jnp.minimum(flow, 0.0) * far

    def fluxes(layer, _):
        def rows(ref, k, at=low, span=layers, pad=PAD, width=pitch):
            return [ref[pl.ds((c * span + layer + at) * width + pad + k, 8, stride=step), :] for c in range(chunks)]

        perm = {k: rows(perms2, k) for k in range(-1, step + 1)}
        here = {k: rows(final2, k) for k in range(-1, step + 1)}
        old = {k: rows(frac2, k, 0, nx) for k in range(-1, step + 1)}
        for k in range(step):
            deep = deeper(perm[k])
            t_z = [transmit(perm[k][c], deep[c]) for c in range(chunks)]
            t_z[-1] = jnp.where(lane == LANES - 1, 0.0, t_z[-1])
            below, old_below = deeper(here[k]), deeper(old[k])
            down = [upwind(t_z[c] * (here[k][c] - below[c]), old[k][c], old_below[c]) for c in range(chunks)]
            from_above = shallower(down)
            east, perm_east = rows(final2, k, low + 1), rows(perms2, k, low + 1)
            kind, rate = rows(kinds2, k), rows(rates2, k)
            imposed, water = rows(flux2, k, 0, nx, 0, ny), rows(sat2, k, 0, nx, 0, ny)
            for c in range(chunks):
                north = transmit(perm[k][c], perm[k + 1][c]) * (here[k][c] - here[k + 1][c])
                south = transmit(perm[k][c], perm[k - 1][c]) * (here[k][c] - here[k - 1][c])
                own = old[k][c]
                leaving = (upwind(north, own, old[k + 1][c]) + upwind(south, own, old[k - 1][c])) + (down[c] - from_above[c])
                explicit = jnp.maximum(rate[c], 0.0) + jnp.minimum(rate[c], 0.0) * own - leaving
                t_x = transmit(perm[k][c], perm_east[c])
                through = jnp.maximum(imposed[c] + t_x * (here[k][c] - east[c]), 0.0)
                s = water[c]
                volume = look_up(volume_table, kind[c].astype(jnp.int32))
                denom = s * s + MOBILITY * (1.0 - s) ** 2
                gain = 1.0 / (volume + through * (2.0 * MOBILITY * s * (1.0 - s) / (denom * denom)))
                first = s - (through * own - explicit) * gain
                for i, value in enumerate((first, gain, through, volume, volume * s + explicit)):
                    prep_ref[layer, pl.ds((i * chunks + c) * ny + k, 8, stride=step), :] = value
        return 0

    lax.fori_loop(0, nx, fluxes, 0)
    send_out(False)


def flow(pressure, rock_type, base_flux, saturation, sides, ends, ends_corner, tables, well_cells, well_rates):
    nx, ny, nz = pressure.shape
    chunks = nz // LANES
    layers, pitch = PASSES + nx + REACH, ny + 2 * PAD
    assert ny % 8 == 0 and nz % LANES == 0
    tiles = (ny + 2 * PASSES) // 8
    wide = pltpu.VMEM((chunks, layers, pitch, LANES), jnp.float32)
    packed = pltpu.VMEM((chunks, layers * (tiles + 1) * 8, LANES), jnp.float32)
    block = (chunks, nx, ny, LANES)
    return pl.pallas_call(
        flow_kernel,
        name="flow",
        out_shape=(
            jax.ShapeDtypeStruct(pressure.shape, jnp.float32),
            jax.ShapeDtypeStruct((nx, 5 * chunks * ny, LANES), jnp.float32),
            jax.ShapeDtypeStruct((chunks * ny, LANES), jnp.float32),
        ),
        in_specs=[ANY] * 4 + [VMEM] * 2 + [ANY] * 2 + [VMEM] * 2 + [VMEM, SMEM, SMEM],
        out_specs=(ANY, VMEM, VMEM),
        scratch_shapes=[wide] * 5 + [packed] * 5
        + [pltpu.VMEM(block, jnp.int32)] + [pltpu.VMEM(block, jnp.float32)] * 2
        + [pltpu.VMEM((chunks, nx, pitch, LANES), jnp.float32), pltpu.SemaphoreType.DMA((8, chunks))],
        compiler_params=pltpu.CompilerParams(vmem_limit_bytes=60 << 20),
    )(pressure, rock_type, base_flux, saturation, *sides, *ends, *ends_corner, tables, well_cells, well_rates)


def stage_kernel(stage, inflow_ref, prep_ref, *refs):
    sat_ref, out_ref, prep, sat, sems, out_sems = refs[-6:]
    nx, rows, _ = prep.shape
    plane = rows // 5
    chunks, _, ny, _ = sat.shape

    @pl.when(lax.axis_index("gx") == stage)
    def _():
        def bring(layer):
            return pltpu.make_async_copy(prep_ref.at[layer], prep.at[layer], sems.at[layer])

        def send(layer):
            return [
                pltpu.make_async_copy(sat.at[c, layer], sat_ref.at[layer, :, pl.ds(c * LANES, LANES)], out_sems.at[layer, c])
                for c in range(chunks)
            ]

        for layer in range(nx):
            bring(layer).start()

        def advance(layer, incoming):
            bring(layer).wait()
            first, gain, through, volume, held = (prep[layer, pl.ds(i * plane, plane), :] for i in range(5))
            known = held + incoming
            water = jnp.clip(first + gain * incoming, 0.0, 1.0)
            for _ in range(NEWTON - 1):
                dry = 1.0 - water
                square = water * water
                denom = square + MOBILITY * (dry * dry)
                top = denom * (denom * (volume * water - known) + through * square)
                bottom = denom * denom * volume + through * (2.0 * MOBILITY * (water * dry))
                water = jnp.clip(water - top / bottom, 0.0, 1.0)
            for c in range(chunks):
                sat[c, layer] = water[c * ny : (c + 1) * ny]
            for copy in send(layer):
                copy.start()
            return through * fraction(water)

        out_ref[...] = lax.fori_loop(0, nx, advance, inflow_ref[...])

        def finish(layer, _):
            for copy in send(layer):
                copy.wait()
            return 0

        lax.fori_loop(0, nx, finish, 0)


def run_stage(stage, inflow, prep, shape, saturation):
    nx, ny, nz = shape
    chunks = nz // LANES
    block = jax.ShapeDtypeStruct(shape, jnp.float32)
    return pl.pallas_call(
        functools.partial(stage_kernel, stage),
        name="stage",
        out_shape=(block, jax.ShapeDtypeStruct(inflow.shape, jnp.float32)),
        in_specs=[VMEM, ANY] + [ANY] * len(saturation),
        out_specs=(ANY, VMEM),
        input_output_aliases={2: 0} if saturation else {},
        scratch_shapes=[
            pltpu.VMEM(prep.shape, jnp.float32),
            pltpu.VMEM((chunks, nx, ny, LANES), jnp.float32),
            pltpu.SemaphoreType.DMA((nx,)),
            pltpu.SemaphoreType.DMA((nx, chunks)),
        ],
    )(inflow, prep, *saturation)


def shards(rock_type, rock_perm, rock_poro, base_flux, initial_pressure, old_saturation, well_cells, well_rates):
    nx = rock_type.shape[0]
    volume = VOLUME * rock_poro
    tables = jnp.stack([
        jnp.pad(rock_perm, (1, LANES - 1 - rock_perm.shape[0])),
        jnp.pad(COMPRESS * volume, (1, LANES - 1 - volume.shape[0]), constant_values=1.0),
        jnp.pad(volume, (1, LANES - 1 - volume.shape[0]), constant_values=1.0),
    ])
    tables = jnp.broadcast_to(tables[:, None, :], (3, 8, LANES))

    side_a, side_b, end_a, end_b = pack(initial_pressure, rock_type, old_saturation)
    sides = swap(side_a, side_b, "gy")
    ends = swap(end_a, end_b, "gx")
    ends_corner = swap(*corners(*sides, nx), "gx")
    pressure, prep, inflow = flow(
        initial_pressure, rock_type, base_flux, old_saturation, sides, ends, ends_corner, tables, well_cells, well_rates
    )
    saturation = ()
    count = lax.axis_size("gx")
    for stage in range(count):
        *saturation, outflow = run_stage(stage, inflow, prep, rock_type.shape, saturation)
        if stage < count - 1:
            inflow = lax.ppermute(outflow, "gx", [(stage, stage + 1)])
    return pressure, saturation[0]


def solution(mesh):
    return jax.shard_map(
        shards,
        mesh=mesh,
        in_specs=(
            P("gx", "gy", None),
            P(),
            P(),
            P("gx", "gy", None),
            P("gx", "gy", None),
            P("gx", "gy", None),
            P(),
            P(),
        ),
        out_specs=(P("gx", "gy", None), P("gx", "gy", None)),
        check_vma=False,
    )
```

```python
import functools
import math

import jax
import jax.numpy as jnp
from jax import lax
from jax.experimental import pallas as pl
from jax.experimental.pallas import tpu as pltpu
from jax.sharding import PartitionSpec as P


PASSES = 4
NEWTON = 3

MOBILITY = 0.5
OMEGA = 0.8
VOLUME = 4.0
COMPRESS = 0.5

LANES = 128
UNROLL = 2
REACH = PASSES + 1
PAD = 8
HBM = pl.BlockSpec(memory_space=pltpu.MemorySpace.HBM)
VMEM = pl.BlockSpec(memory_space=pltpu.VMEM)
SMEM = pl.BlockSpec(memory_space=pltpu.SMEM)


def swap_pairs(axis):
    count = lax.axis_size(axis)
    pairs = []
    for first in (0, 1):
        ups = [(i, i + 1) for i in range(first, count - 1, 2)]
        pairs.append(ups + [(j, i) for i, j in ups])
    return pairs


def swap(value_a, value_b, axis):
    pairs_a, pairs_b = swap_pairs(axis)
    got_a = lax.ppermute(value_a, axis, pairs_a)
    got_b = lax.ppermute(value_b, axis, pairs_b)
    return got_a, got_b


def fetch(source, target, sems, start):
    for c in range(target.shape[0]):
        copy = pltpu.make_async_copy(source.at[:, :, pl.ds(c * LANES, LANES)], target.at[c], sems.at[c])
        copy.start() if start else copy.wait()


def pack_sides_kernel(p_ref, rock_ref, sat_ref, ya_ref, yb_ref, p, rock, sat, sems):
    chunks, nx = p.shape[1], p.shape[2]
    ny = p_ref.shape[1]
    even = lax.rem(lax.axis_index("gy"), 2) == 0
    outs = ((ya_ref, even), (yb_ref, jnp.logical_not(even)))

    def copies(i):
        _, high = outs[i]
        tile = pl.ds(pl.multiple_of(jnp.where(high, ny - 8, 0), 8), 8)
        return [
            pltpu.make_async_copy(source.at[:, tile, pl.ds(c * LANES, LANES)], target.at[i, c], sems.at[i, n, c])
            for n, (source, target) in enumerate(((p_ref, p), (rock_ref, rock), (sat_ref, sat)))
            for c in range(chunks)
        ]

    for i in range(2):
        for copy in copies(i):
            copy.start()
    p2, rock2, sat2 = (f.reshape(2 * chunks * nx * 8, LANES) for f in (p, rock, sat))
    rows = (2 * REACH + 1) * nx
    for i, (out, high) in enumerate(outs):
        for copy in copies(i):
            copy.wait()
        first = jnp.where(high, 8 - REACH, 0)
        edge = jnp.where(high, 7, 0)
        for c in range(chunks):
            base = (i * chunks + c) * nx * 8
            for j in range(REACH):
                out[pl.ds(c * rows + j * nx, nx), :] = p2[pl.ds(base + first + j, nx, stride=8), :]
                kinds = rock2[pl.ds(base + first + j, nx, stride=8), :]
                out[pl.ds(c * rows + (REACH + j) * nx, nx), :] = kinds.astype(jnp.float32) + 1.0
            out[pl.ds(c * rows + 2 * REACH * nx, nx), :] = sat2[pl.ds(base + edge, nx, stride=8), :]


def pack_sides(pressure, rock_type, saturation):
    nx, _, nz = pressure.shape
    chunks = nz // LANES
    side = jax.ShapeDtypeStruct((chunks * (2 * REACH + 1) * nx, LANES), jnp.float32)
    block = (2, chunks, nx, 8, LANES)
    return pl.pallas_call(
        pack_sides_kernel,
        name="pack_sides",
        out_shape=(side, side),
        in_specs=[HBM] * 3,
        out_specs=(VMEM,) * 2,
        scratch_shapes=[
            pltpu.VMEM(block, jnp.float32),
            pltpu.VMEM(block, jnp.int32),
            pltpu.VMEM(block, jnp.float32),
            pltpu.SemaphoreType.DMA((2, 3, chunks)),
        ],
        compiler_params=pltpu.CompilerParams(vmem_limit_bytes=63 << 20),
    )(pressure, rock_type, saturation)


def pack_ends_kernel(p_ref, rock_ref, _, xa_ref, xb_ref, rock, sems):
    nx = p_ref.shape[0]
    even = lax.rem(lax.axis_index("gx"), 2) == 0
    copies = []
    for i, (out, high) in enumerate(((xa_ref, even), (xb_ref, jnp.logical_not(even)))):
        layers = pl.ds(jnp.where(high, nx - REACH, 0), REACH)
        copies.append((
            pltpu.make_async_copy(p_ref.at[layers], out.at[pl.ds(0, REACH)], sems.at[i, 0]),
            pltpu.make_async_copy(rock_ref.at[layers], rock.at[i], sems.at[i, 1]),
        ))
    for pair in copies:
        for copy in pair:
            copy.start()
    for i, out in enumerate((xa_ref, xb_ref)):
        copies[i][1].wait()
        for j in range(REACH):
            out[REACH + j] = rock[i, j].astype(jnp.float32) + 1.0
        copies[i][0].wait()


def pack_ends(pressure, rock_type, after):
    _, ny, nz = pressure.shape
    end = jax.ShapeDtypeStruct((2 * REACH, ny, nz), jnp.float32)
    return pl.pallas_call(
        pack_ends_kernel,
        name="pack_ends",
        out_shape=(end, end),
        in_specs=[HBM] * 2 + [pl.BlockSpec(memory_space=pl.ANY)],
        out_specs=(VMEM,) * 2,
        scratch_shapes=[pltpu.VMEM((2, REACH, ny, nz), jnp.int32), pltpu.SemaphoreType.DMA((2, 2))],
        compiler_params=pltpu.CompilerParams(vmem_limit_bytes=60 << 20),
    )(pressure, rock_type, after)


def corner_kernel(nx, ya_ref, yb_ref, _, ca_ref, cb_ref):
    rows = (2 * REACH + 1) * nx
    chunks = ya_ref.shape[0] // rows
    even_y = lax.rem(lax.axis_index("gy"), 2) == 0
    even_x = lax.rem(lax.axis_index("gx"), 2) == 0
    for out, high in ((ca_ref, even_x), (cb_ref, jnp.logical_not(even_x))):
        layer = jnp.where(high, nx - PASSES, 0)
        for c in range(chunks):
            for kind in range(2):
                for i in range(PASSES):
                    for side in range(2):
                        start = c * rows + (kind * REACH + 1 - side) * nx + layer + i
                        from_a = ya_ref[pl.ds(start, PASSES, stride=nx), :]
                        from_b = yb_ref[pl.ds(start, PASSES, stride=nx), :]
                        mine = jnp.where(even_y, from_b, from_a) if side == 0 else jnp.where(even_y, from_a, from_b)
                        at = ((c * 2 + kind) * PASSES + i) * 2 + side
                        out[pl.ds(at * PASSES, PASSES), :] = mine


def corners(side_a, side_b, nx, after):
    chunks = side_a.shape[0] // ((2 * REACH + 1) * nx)
    shape = jax.ShapeDtypeStruct((chunks * 4 * PASSES * PASSES, LANES), jnp.float32)
    return pl.pallas_call(
        functools.partial(corner_kernel, nx),
        name="corners",
        out_shape=(shape, shape),
        in_specs=[VMEM] * 2 + [pl.BlockSpec(memory_space=pl.ANY)],
        out_specs=(VMEM,) * 2,
        compiler_params=pltpu.CompilerParams(vmem_limit_bytes=4 << 20),
    )(side_a, side_b, after)


def fraction(water):
    denom = water * water + MOBILITY * (1.0 - water) ** 2
    return water * water / denom


def transmit(left, right):
    return 2.0 * left * right / jnp.maximum(left + right, 1e-30)


def look_up(table, kinds):
    return jnp.take_along_axis(table, kinds, axis=1, mode="promise_in_bounds")


def deeper(values):
    turned = [pltpu.roll(v, LANES - 1, 1) for v in values]
    last = lax.broadcasted_iota(jnp.int32, turned[0].shape, 1) == LANES - 1
    return [jnp.where(last, turned[(c + 1) % len(values)], turned[c]) for c in range(len(values))]


def shallower(values):
    turned = [pltpu.roll(v, 1, 1) for v in values]
    first = lax.broadcasted_iota(jnp.int32, turned[0].shape, 1) == 0
    return [jnp.where(first, turned[c - 1], turned[c]) for c in range(len(values))]


def upwind(flow, own, far):
    return jnp.maximum(flow, 0.0) * own + jnp.minimum(flow, 0.0) * far


def flat(ref):
    return ref.reshape(math.prod(ref.shape[:-1]), LANES)


def rock_tables(perm_ref, poro_ref):
    lane = lax.broadcasted_iota(jnp.int32, (8, LANES), 1)
    perm, poro = jnp.zeros((8, LANES), jnp.float32), jnp.zeros((8, LANES), jnp.float32)
    for kind in range(perm_ref.shape[0]):
        perm = jnp.where(lane == kind + 1, perm_ref[kind], perm)
        poro = jnp.where(lane == kind + 1, poro_ref[kind], poro)
    return perm, jnp.where(lane == 0, 1.0, COMPRESS * (VOLUME * poro))


def rates_kernel(nx, ny, cells_ref, rates_ref, out_ref):
    chunks, layers, pitch, _ = out_ref.shape
    rank_x, rank_y = lax.axis_index("gx"), lax.axis_index("gy")
    sub = lax.broadcasted_iota(jnp.int32, (8, LANES), 0)
    lane = lax.broadcasted_iota(jnp.int32, (8, LANES), 1)
    out2 = flat(out_ref)

    def clear(layer, _):
        for c in range(chunks):
            out_ref[c, layer] = jnp.zeros((pitch, LANES), jnp.float32)
        return 0

    lax.fori_loop(0, layers, clear, 0)

    def add_well(w, _):
        x = cells_ref[0, w] - rank_x * nx + REACH
        y = cells_ref[1, w] - rank_y * ny + PAD
        z = cells_ref[2, w]

        @pl.when((x >= 0) & (x < layers) & (y >= 0) & (y < pitch))
        def _():
            row = (lax.shift_right_logical(z, 7) * layers + x) * pitch + y
            tile = pl.multiple_of(lax.shift_left(lax.shift_right_logical(row, 3), 3), 8)
            here = (sub == row - tile) & (lane == lax.bitwise_and(z, LANES - 1))
            out2[pl.ds(tile, 8), :] = out2[pl.ds(tile, 8), :] + jnp.where(here, rates_ref[w], 0.0)

        return 0

    lax.fori_loop(0, cells_ref.shape[1], add_well, 0)


def wide_shape(block):
    nx, ny, nz = block
    return (nz // LANES, nx + 2 * REACH, ny + 2 * PAD, LANES)


def rates_field(block, well_cells, well_rates):
    return pl.pallas_call(
        functools.partial(rates_kernel, *block[:2]),
        name="rates",
        out_shape=jax.ShapeDtypeStruct(wide_shape(block), jnp.float32),
        in_specs=[SMEM] * 2,
        out_specs=VMEM,
        cost_estimate=pl.CostEstimate(flops=0, bytes_accessed=12 << 20, transcendentals=0),
        compiler_params=pltpu.CompilerParams(vmem_limit_bytes=4 << 20),
    )(well_cells, well_rates)


def ready_kernel(
    p_ref, rock_ref, sat_ref, xa_ref, xb_ref, rates_ref, perm_ref, poro_ref,
    press, perms, stores, trans_x, trans_y, trans_z, scale, drive, frac, slope, rock, sat, sems,
):
    chunks, layers, pitch, _ = press.shape
    _, nx, ny, _ = rock.shape
    depth, step = layers * pitch, ny // 8
    even_x = lax.rem(lax.axis_index("gx"), 2) == 0
    own_p = press.at[:, pl.ds(REACH, nx), pl.ds(PAD, ny), :]
    fetch(rock_ref, rock, sems.at[0], True)
    fetch(p_ref, own_p, sems.at[1], True)
    fetch(sat_ref, sat, sems.at[2], True)
    perm_table, store_table = rock_tables(perm_ref, poro_ref)
    zero = jnp.zeros((8, LANES), jnp.float32)
    lane = lax.broadcasted_iota(jnp.int32, (8, LANES), 1)

    def clear(layer, _):
        for c in range(chunks):
            for ref in (press, perms, stores):
                for t in (0, pitch // 8 - 1):
                    ref[c, layer, pl.ds(t * 8, 8), :] = zero
        return 0

    lax.fori_loop(0, layers, clear, 0)

    def look(layer, kinds_of):
        for c in range(chunks):
            for t in range(ny // 8):
                kind = kinds_of(c, t)
                perms[c, layer, pl.ds(PAD + t * 8, 8), :] = look_up(perm_table, kind)
                stores[c, layer, pl.ds(PAD + t * 8, 8), :] = look_up(store_table, kind)

    def look_ends(j, _):
        for c in range(chunks):
            a, b = (ref[j, :, pl.ds(c * LANES, LANES)] for ref in (xa_ref, xb_ref))
            press[c, j, pl.ds(PAD, ny), :] = jnp.where(even_x, b, a)
            press[c, REACH + nx + j, pl.ds(PAD, ny), :] = jnp.where(even_x, a, b)

        def side(low):
            def kinds_of(c, t):
                a, b = (ref[REACH + j, pl.ds(t * 8, 8), pl.ds(c * LANES, LANES)] for ref in (xa_ref, xb_ref))
                return (jnp.where(even_x, b, a) if low else jnp.where(even_x, a, b)).astype(jnp.int32)

            return kinds_of

        look(j, side(True))
        look(REACH + nx + j, side(False))
        return 0

    lax.fori_loop(0, REACH, look_ends, 0)
    fetch(rock_ref, rock, sems.at[0], False)

    def look_own(layer, _):
        look(REACH + layer, lambda c, t: rock[c, layer, pl.ds(t * 8, 8), :] + 1)
        return 0

    lax.fori_loop(0, nx, look_own, 0)
    fetch(p_ref, own_p, sems.at[1], False)

    press2, perms2, stores2, rates2 = map(flat, (press, perms, stores, rates_ref))
    tx2, ty2, tz2, scale2, drive2 = map(flat, (trans_x, trans_y, trans_z, scale, drive))

    def rows(layer, k, c):
        return pl.ds(c * depth + layer * pitch + PAD + k, 8, stride=step)

    def prepare(layer, _):
        perm = {k: [perms2[rows(layer, k, c), :] for c in range(chunks)] for k in range(-1, step + 1)}
        t_s = [transmit(perm[-1][c], perm[0][c]) for c in range(chunks)]
        for k in range(step):
            deep = deeper(perm[k])
            t_z = [transmit(perm[k][c], deep[c]) for c in range(chunks)]
            t_z[-1] = jnp.where(lane == LANES - 1, 0.0, t_z[-1])
            above = shallower(t_z)
            for c in range(chunks):
                at = rows(layer, k, c)
                t_x = transmit(perm[k][c], perms2[rows(layer + 1, k, c), :])
                t_n = transmit(perm[k][c], perm[k + 1][c])
                t_w = tx2[rows(jnp.maximum(layer - 1, 0), k, c), :]
                tx2[at, :], ty2[at, :], tz2[at, :] = t_x, t_n, t_z[c]
                store = stores2[at, :]
                factor = OMEGA / (store + ((t_x + t_w) + (t_n + t_s[c]) + (t_z[c] + above[c])))
                scale2[at, :] = factor
                drive2[at, :] = factor * (store * press2[at, :] + rates2[at, :])
                t_s[c] = t_n
        return 0

    lax.fori_loop(0, layers - 1, prepare, 0)
    fetch(sat_ref, sat, sems.at[2], False)

    def old_fraction(layer, _):
        for c in range(chunks):
            s = sat[c, layer]
            inverse = 1.0 / (s * s + MOBILITY * (1.0 - s) ** 2)
            frac[c, layer, pl.ds(PAD, ny), :] = s * s * inverse
            slope[c, layer] = 2.0 * MOBILITY * s * (1.0 - s) * (inverse * inverse)
        return 0

    lax.fori_loop(0, nx, old_fraction, 0)


def ready(pressure, rock_type, saturation, ends, rates, rock_perm, rock_poro):
    nx, ny, nz = pressure.shape
    chunks = nz // LANES
    assert ny % 8 == 0 and nz % LANES == 0
    wide = jax.ShapeDtypeStruct(wide_shape(pressure.shape), jnp.float32)
    block = (chunks, nx, ny, LANES)
    return pl.pallas_call(
        ready_kernel,
        name="ready",
        out_shape=(wide,) * 8 + (jax.ShapeDtypeStruct((chunks, nx, ny + 2 * PAD, LANES), jnp.float32), jax.ShapeDtypeStruct(block, jnp.float32)),
        in_specs=[HBM] * 3 + [VMEM] * 3 + [SMEM] * 2,
        out_specs=(VMEM,) * 10,
        scratch_shapes=[pltpu.VMEM(block, jnp.int32), pltpu.VMEM(block, jnp.float32), pltpu.SemaphoreType.DMA((3, chunks))],
        cost_estimate=pl.CostEstimate(flops=0, bytes_accessed=24 << 20, transcendentals=0),
        compiler_params=pltpu.CompilerParams(vmem_limit_bytes=4 << 20),
    )(pressure, rock_type, saturation, *ends, rates, rock_perm, rock_poro)


def flow_kernel(
    flux_ref, sat_ref, ya_ref, yb_ref, ca_ref, cb_ref, rates_ref, slope_ref, perm_ref, poro_ref, *refs
):
    press, perms, stores, trans_x, trans_y, trans_z, scale, drive, frac = refs[9:18]
    press_ref, prep_ref, inlet_ref, other, flux, sat, sems = refs[18:]
    chunks, layers, pitch, _ = press.shape
    _, nx, ny, _ = flux.shape
    depth, step = layers * pitch, ny // 8
    tiles = (ny + 2 * PASSES) // 8
    side_rows = (2 * REACH + 1) * nx
    even_x, even_y = lax.rem(lax.axis_index("gx"), 2) == 0, lax.rem(lax.axis_index("gy"), 2) == 0
    press2, other2, perms2, stores2, rates2, frac2 = map(flat, (press, other, perms, stores, rates_ref, frac))
    tx2, ty2, tz2, scale2, drive2 = map(flat, (trans_x, trans_y, trans_z, scale, drive))
    flux2, sat2, slope2 = map(flat, (flux, sat, slope_ref))
    fetch(flux_ref, flux, sems.at[0], True)
    fetch(sat_ref, sat, sems.at[1], True)
    perm_table, store_table = rock_tables(perm_ref, poro_ref)
    lane = lax.broadcasted_iota(jnp.int32, (8, LANES), 1)

    for c in range(chunks):
        for j in range(REACH):
            for half in range(nx // 8):
                start = c * side_rows + j * nx + half * 8
                at = c * depth + (REACH + half * 8) * pitch + j
                low = pl.ds(at + PAD - REACH, 8, stride=pitch)
                high = pl.ds(at + PAD + ny, 8, stride=pitch)
                a, b = ya_ref[pl.ds(start, 8), :], yb_ref[pl.ds(start, 8), :]
                press2[low, :], press2[high, :] = jnp.where(even_y, b, a), jnp.where(even_y, a, b)
                a, b = (ref[pl.ds(start + REACH * nx, 8), :].astype(jnp.int32) for ref in (ya_ref, yb_ref))
                for where, kind in ((low, jnp.where(even_y, b, a)), (high, jnp.where(even_y, a, b))):
                    perms2[where, :], stores2[where, :] = look_up(perm_table, kind), look_up(store_table, kind)
        start = c * side_rows + 2 * REACH * nx
        a, b = fraction(ya_ref[pl.ds(start, nx), :]), fraction(yb_ref[pl.ds(start, nx), :])
        at = c * nx * pitch
        frac2[pl.ds(at + PAD - 1, nx, stride=pitch), :] = jnp.where(even_y, b, a)
        frac2[pl.ds(at + PAD + ny, nx, stride=pitch), :] = jnp.where(even_y, a, b)
        both = 2 * PASSES
        for k in range(PASSES):
            start = (c * 2 * PASSES + k) * both
            a, b = ca_ref[pl.ds(start, both), :], cb_ref[pl.ds(start, both), :]
            ends = ((1 + k, jnp.where(even_x, b, a)), (REACH + nx + k, jnp.where(even_x, a, b)))
            start += PASSES * both
            a, b = (ref[pl.ds(start, both), :].astype(jnp.int32) for ref in (ca_ref, cb_ref))
            kinds = (jnp.where(even_x, b, a), jnp.where(even_x, a, b))
            for (layer, value), kind in zip(ends, kinds):
                for ref, new in ((press2, value), (perms2, look_up(perm_table, kind)), (stores2, look_up(store_table, kind))):
                    at = c * depth + layer * pitch + PAD
                    ref[pl.ds(at - PASSES, PASSES), :] = new[:PASSES]
                    ref[pl.ds(at + ny, PASSES), :] = new[PASSES:]

    def complete(group, _):
        for first in (PAD - PASSES, PAD + ny - 1):
            def rows(k, by, c):
                return pl.ds(c * depth + (1 + group * 8 + by) * pitch + first + k, 8, stride=pitch)

            perm = {k: [perms2[rows(k, 0, c), :] for c in range(chunks)] for k in range(-1, PASSES + 2)}
            t_s = [transmit(perm[-1][c], perm[0][c]) for c in range(chunks)]
            for c in range(chunks):
                ty2[rows(-1, 0, c), :] = t_s[c]
            for k in range(PASSES + 1):
                deep = deeper(perm[k])
                t_z = [transmit(perm[k][c], deep[c]) for c in range(chunks)]
                t_z[-1] = jnp.where(lane == LANES - 1, 0.0, t_z[-1])
                above = shallower(t_z)
                for c in range(chunks):
                    at = rows(k, 0, c)
                    t_x = transmit(perm[k][c], perms2[rows(k, 1, c), :])
                    t_w = transmit(perm[k][c], perms2[rows(k, -1, c), :])
                    t_n = transmit(perm[k][c], perm[k + 1][c])
                    tx2[at, :], ty2[at, :], tz2[at, :] = t_x, t_n, t_z[c]
                    store = stores2[at, :]
                    factor = OMEGA / (store + ((t_x + t_w) + (t_n + t_s[c]) + (t_z[c] + above[c])))
                    scale2[at, :] = factor
                    drive2[at, :] = factor * (store * press2[at, :] + rates2[at, :])
                    t_s[c] = t_n
        return 0

    lax.fori_loop(0, (layers - 2) // 8, complete, 0)

    def relax(source, target, number):
        def one(layer, _):
            def rows(k, c, by=0):
                return pl.ds(c * depth + (layer + by) * pitch + PAD - PASSES + k, 8, stride=tiles)

            now = {k: [source[rows(k, c), :] for c in range(chunks)] for k in range(-1, tiles + 1)}
            for k in range(tiles):
                here = now[k]
                t_z = [tz2[rows(k, c), :] for c in range(chunks)]
                deep = deeper(here)
                shallow = shallower([t_z[c] * here[c] for c in range(chunks)])
                for c in range(chunks):
                    at = rows(k, c)
                    total = (
                        (tx2[at, :] * source[rows(k, c, 1), :] + tx2[rows(k, c, -1), :] * source[rows(k, c, -1), :])
                        + (ty2[at, :] * now[k + 1][c] + ty2[rows(k - 1, c), :] * now[k - 1][c])
                        + (t_z[c] * deep[c] + shallow[c])
                    )
                    target[at, :] = (1.0 - OMEGA) * here[c] + (drive2[at, :] + scale2[at, :] * total)
            return 0

        lax.fori_loop(min(number + 1, REACH), layers - number, one, 0, unroll=UNROLL)

    for number in range(1, PASSES + 1):
        source, target = (press2, other2) if number % 2 else (other2, press2)
        relax(source, target, number)
    final, final2 = (press, press2) if PASSES % 2 == 0 else (other, other2)

    def send_out(start):
        for c in range(chunks):
            copy = pltpu.make_async_copy(
                final.at[c, pl.ds(REACH, nx), pl.ds(PAD, ny), :], press_ref.at[:, :, pl.ds(c * LANES, LANES)], sems.at[2, c]
            )
            copy.start() if start else copy.wait()

    send_out(True)
    fetch(flux_ref, flux, sems.at[0], False)
    fetch(sat_ref, sat, sems.at[1], False)
    for c in range(chunks):
        inlet_ref[pl.ds(c * ny, ny), :] = flux[c, 0]

    def fluxes(layer, _):
        def wide(ref, k, by=0):
            return [ref[pl.ds(c * depth + (REACH + layer + by) * pitch + PAD + k, 8, stride=step), :] for c in range(chunks)]

        def own(ref, k):
            return [ref[pl.ds((c * nx + layer) * ny + k, 8, stride=step), :] for c in range(chunks)]

        here = {k: wide(final2, k) for k in range(-1, step + 1)}
        old = {
            k: [frac2[pl.ds((c * nx + layer) * pitch + PAD + k, 8, stride=step), :] for c in range(chunks)]
            for k in range(-1, step + 1)
        }
        south = None
        for k in range(-1, step):
            t_y = wide(ty2, k)
            north = [upwind(t_y[c] * (here[k][c] - here[k + 1][c]), old[k][c], old[k + 1][c]) for c in range(chunks)]
            if k >= 0:
                t_z, below, old_below = wide(tz2, k), deeper(here[k]), deeper(old[k])
                down = [upwind(t_z[c] * (here[k][c] - below[c]), old[k][c], old_below[c]) for c in range(chunks)]
                from_above = shallower(down)
                east, t_x, rate, store = wide(final2, k, 1), wide(tx2, k), wide(rates2, k), wide(stores2, k)
                imposed, water, bend = own(flux2, k), own(sat2, k), own(slope2, k)
                for c in range(chunks):
                    leaving = (north[c] - south[c]) + (down[c] - from_above[c])
                    explicit = jnp.maximum(rate[c], 0.0) + jnp.minimum(rate[c], 0.0) * old[k][c] - leaving
                    through = jnp.maximum(imposed[c] + t_x[c] * (here[k][c] - east[c]), 0.0)
                    volume = store[c] * (1.0 / COMPRESS)
                    gain = 1.0 / (volume + through * bend[c])
                    first = water[c] - (through * old[k][c] - explicit) * gain
                    for i, value in enumerate((first, gain, through, volume, volume * water[c] + explicit)):
                        prep_ref[layer, pl.ds((i * chunks + c) * ny + k, 8, stride=step), :] = value
            south = north
        return 0

    lax.fori_loop(0, nx, fluxes, 0)
    send_out(False)


def flow(base_flux, saturation, sides, ends_corner, rates, made, rock_perm, rock_poro):
    nx, ny, nz = base_flux.shape
    chunks = nz // LANES
    *fields, slope = made
    block = pltpu.VMEM((chunks, nx, ny, LANES), jnp.float32)
    inputs = (base_flux, saturation, *sides, *ends_corner, rates, slope, rock_perm, rock_poro, *fields)
    first = len(inputs) - len(fields)
    return pl.pallas_call(
        flow_kernel,
        name="flow",
        out_shape=tuple(jax.ShapeDtypeStruct(f.shape, f.dtype) for f in fields) + (
            jax.ShapeDtypeStruct(base_flux.shape, jnp.float32),
            jax.ShapeDtypeStruct((nx, 5 * chunks * ny, LANES), jnp.float32),
            jax.ShapeDtypeStruct((chunks * ny, LANES), jnp.float32),
        ),
        in_specs=[HBM] * 2 + [VMEM] * 6 + [SMEM] * 2 + [VMEM] * len(fields),
        out_specs=(VMEM,) * len(fields) + (HBM, VMEM, VMEM),
        input_output_aliases={first + i: i for i in range(len(fields))},
        scratch_shapes=[pltpu.VMEM(wide_shape(base_flux.shape), jnp.float32), block, block, pltpu.SemaphoreType.DMA((3, chunks))],
        compiler_params=pltpu.CompilerParams(vmem_limit_bytes=8 << 20),
    )(*inputs)[-3:]


def stage_kernel(stage, inflow_ref, prep_ref, *refs):
    sat_ref, out_ref, sat, out_sems = refs[-4:]
    nx, rows, _ = prep_ref.shape
    plane = rows // 5
    chunks, _, ny, _ = sat.shape

    @pl.when(lax.axis_index("gx") == stage)
    def _():
        def send(layer):
            return [
                pltpu.make_async_copy(sat.at[c, layer], sat_ref.at[layer, :, pl.ds(c * LANES, LANES)], out_sems.at[layer, c])
                for c in range(chunks)
            ]

        def advance(layer, incoming):
            first, gain, through, volume, held = (prep_ref[layer, pl.ds(i * plane, plane), :] for i in range(5))
            known = held + incoming
            water = jnp.clip(first + gain * incoming, 0.0, 1.0)
            for _ in range(NEWTON - 1):
                square = water * water
                part = 1.5 * square
                denom = part + (0.5 - water)
                denom = denom * denom
                top = denom * known + through * (square * (0.5 - part))
                bottom = denom * volume + through * (water - square)
                water = jnp.clip(top / bottom, 0.0, 1.0)
            for c in range(chunks):
                sat[c, layer] = water[c * ny : (c + 1) * ny]
            for copy in send(layer):
                copy.start()
            square = water * water
            return (through * square) / (1.5 * square + (0.5 - water))

        out_ref[...] = lax.fori_loop(0, nx, advance, inflow_ref[...])

        def finish(layer, _):
            for copy in send(layer):
                copy.wait()
            return 0

        lax.fori_loop(0, nx, finish, 0)


def run_stage(stage, inflow, prep, shape, saturation):
    nx, ny, nz = shape
    chunks = nz // LANES
    block = jax.ShapeDtypeStruct(shape, jnp.float32)
    return pl.pallas_call(
        functools.partial(stage_kernel, stage),
        name="stage",
        out_shape=(block, jax.ShapeDtypeStruct(inflow.shape, jnp.float32)),
        in_specs=[VMEM, VMEM] + [HBM] * len(saturation),
        out_specs=(HBM, VMEM),
        input_output_aliases={2: 0} if saturation else {},
        scratch_shapes=[
            pltpu.VMEM((chunks, nx, ny, LANES), jnp.float32),
            pltpu.SemaphoreType.DMA((nx, chunks)),
        ],
        compiler_params=pltpu.CompilerParams(vmem_limit_bytes=12 << 20),
    )(inflow, prep, *saturation)


def step(rock_type, rock_perm, rock_poro, base_flux, initial_pressure, old_saturation, well_cells, well_rates):
    nx = rock_type.shape[0]
    sides = pack_sides(initial_pressure, rock_type, old_saturation)
    sides_got = swap(*sides, "gy")
    ends = swap(*pack_ends(initial_pressure, rock_type, sides[0]), "gx")
    rates = rates_field(rock_type.shape, well_cells, well_rates)
    made = ready(initial_pressure, rock_type, old_saturation, ends, rates, rock_perm, rock_poro)
    ends_corner = swap(*corners(*sides_got, nx, made[-1]), "gx")
    pressure, prep, inflow = flow(base_flux, old_saturation, sides_got, ends_corner, rates, made, rock_perm, rock_poro)
    saturation = ()
    count = lax.axis_size("gx")
    for stage in range(count):
        *saturation, outflow = run_stage(stage, inflow, prep, rock_type.shape, saturation)
        if stage < count - 1:
            inflow = lax.ppermute(outflow, "gx", [(stage, stage + 1)])
    return pressure, saturation[0]


def solution(mesh):
    return jax.shard_map(
        step,
        mesh=mesh,
        in_specs=(
            P("gx", "gy", None),
            P(),
            P(),
            P("gx", "gy", None),
            P("gx", "gy", None),
            P("gx", "gy", None),
            P(),
            P(),
        ),
        out_specs=(P("gx", "gy", None), P("gx", "gy", None)),
        check_vma=False,
    )
```

```python
import functools
import math

import jax
import jax.numpy as jnp
from jax import lax
from jax.experimental import pallas as pl
from jax.experimental.pallas import tpu as pltpu
from jax.sharding import PartitionSpec as P


PASSES = 4
NEWTON = 3

MOBILITY = 0.5
OMEGA = 0.8
VOLUME = 4.0
COMPRESS = 0.5

LANES = 128
UNROLL = 2
ENDS_LIMIT = 59 << 20
SIDES_LIMIT = 62 << 20
REACH = PASSES + 1
PAD = REACH + 1
HBM = pl.BlockSpec(memory_space=pltpu.MemorySpace.HBM)
VMEM = pl.BlockSpec(memory_space=pltpu.VMEM)
SMEM = pl.BlockSpec(memory_space=pltpu.SMEM)


def swap_pairs(axis):
    count = lax.axis_size(axis)
    pairs = []
    for first in (0, 1):
        ups = [(i, i + 1) for i in range(first, count - 1, 2)]
        pairs.append(ups + [(j, i) for i, j in ups])
    return pairs


def swap(value_a, value_b, axis):
    pairs_a, pairs_b = swap_pairs(axis)
    got_a = lax.ppermute(value_a, axis, pairs_a)
    got_b = lax.ppermute(value_b, axis, pairs_b)
    return got_a, got_b


def fetch(source, target, sems, start):
    for c in range(target.shape[0]):
        copy = pltpu.make_async_copy(source.at[:, :, pl.ds(c * LANES, LANES)], target.at[c], sems.at[c])
        copy.start() if start else copy.wait()


def pack_sides_kernel(p_ref, rock_ref, sat_ref, ya_ref, yb_ref, p, rock, sat, sems):
    chunks, nx = p.shape[1], p.shape[2]
    ny = p_ref.shape[1]
    even = lax.rem(lax.axis_index("gy"), 2) == 0
    outs = ((ya_ref, even), (yb_ref, jnp.logical_not(even)))

    def copies(i):
        _, high = outs[i]
        tile = pl.ds(pl.multiple_of(jnp.where(high, ny - 8, 0), 8), 8)
        return [
            pltpu.make_async_copy(source.at[:, tile, pl.ds(c * LANES, LANES)], target.at[i, c], sems.at[i, n, c])
            for n, (source, target) in enumerate(((p_ref, p), (rock_ref, rock), (sat_ref, sat)))
            for c in range(chunks)
        ]

    for i in range(2):
        for copy in copies(i):
            copy.start()
    p2, rock2, sat2 = (f.reshape(2 * chunks * nx * 8, LANES) for f in (p, rock, sat))
    rows = (2 * REACH + 1) * nx
    for i, (out, high) in enumerate(outs):
        for copy in copies(i):
            copy.wait()
        first = jnp.where(high, 8 - REACH, 0)
        edge = jnp.where(high, 7, 0)
        for c in range(chunks):
            base = (i * chunks + c) * nx * 8
            for j in range(REACH):
                out[pl.ds(c * rows + j * nx, nx), :] = p2[pl.ds(base + first + j, nx, stride=8), :]
                kinds = rock2[pl.ds(base + first + j, nx, stride=8), :]
                out[pl.ds(c * rows + (REACH + j) * nx, nx), :] = kinds.astype(jnp.float32) + 1.0
            out[pl.ds(c * rows + 2 * REACH * nx, nx), :] = sat2[pl.ds(base + edge, nx, stride=8), :]


def pack_sides(pressure, rock_type, saturation):
    nx, _, nz = pressure.shape
    chunks = nz // LANES
    side = jax.ShapeDtypeStruct((chunks * (2 * REACH + 1) * nx, LANES), jnp.float32)
    block = (2, chunks, nx, 8, LANES)
    return pl.pallas_call(
        pack_sides_kernel,
        name="pack_sides",
        out_shape=(side, side),
        in_specs=[HBM] * 3,
        out_specs=(VMEM,) * 2,
        scratch_shapes=[
            pltpu.VMEM(block, jnp.float32),
            pltpu.VMEM(block, jnp.int32),
            pltpu.VMEM(block, jnp.float32),
            pltpu.SemaphoreType.DMA((2, 3, chunks)),
        ],
        compiler_params=pltpu.CompilerParams(vmem_limit_bytes=SIDES_LIMIT),
    )(pressure, rock_type, saturation)


def pack_ends_kernel(p_ref, rock_ref, _, xa_ref, xb_ref, rock, sems):
    nx = p_ref.shape[0]
    even = lax.rem(lax.axis_index("gx"), 2) == 0
    copies = []
    for i, (out, high) in enumerate(((xa_ref, even), (xb_ref, jnp.logical_not(even)))):
        layers = pl.ds(jnp.where(high, nx - REACH, 0), REACH)
        copies.append((
            pltpu.make_async_copy(p_ref.at[layers], out.at[pl.ds(0, REACH)], sems.at[i, 0]),
            pltpu.make_async_copy(rock_ref.at[layers], rock.at[i], sems.at[i, 1]),
        ))
    for pair in copies:
        for copy in pair:
            copy.start()
    for i, out in enumerate((xa_ref, xb_ref)):
        copies[i][1].wait()
        for j in range(REACH):
            out[REACH + j] = rock[i, j].astype(jnp.float32) + 1.0
        copies[i][0].wait()


def pack_ends(pressure, rock_type, after):
    _, ny, nz = pressure.shape
    end = jax.ShapeDtypeStruct((2 * REACH, ny, nz), jnp.float32)
    return pl.pallas_call(
        pack_ends_kernel,
        name="pack_ends",
        out_shape=(end, end),
        in_specs=[HBM] * 2 + [pl.BlockSpec(memory_space=pl.ANY)],
        out_specs=(VMEM,) * 2,
        scratch_shapes=[pltpu.VMEM((2, REACH, ny, nz), jnp.int32), pltpu.SemaphoreType.DMA((2, 2))],
        compiler_params=pltpu.CompilerParams(vmem_limit_bytes=ENDS_LIMIT),
    )(pressure, rock_type, after)


def corner_kernel(nx, ya_ref, yb_ref, _, ca_ref, cb_ref):
    rows = (2 * REACH + 1) * nx
    chunks = ya_ref.shape[0] // rows
    even_y = lax.rem(lax.axis_index("gy"), 2) == 0
    even_x = lax.rem(lax.axis_index("gx"), 2) == 0
    for out, high in ((ca_ref, even_x), (cb_ref, jnp.logical_not(even_x))):
        layer = jnp.where(high, nx - PASSES, 0)
        for c in range(chunks):
            for kind in range(2):
                for i in range(PASSES):
                    for side in range(2):
                        start = c * rows + (kind * REACH + 1 - side) * nx + layer + i
                        from_a = ya_ref[pl.ds(start, PASSES, stride=nx), :]
                        from_b = yb_ref[pl.ds(start, PASSES, stride=nx), :]
                        mine = jnp.where(even_y, from_b, from_a) if side == 0 else jnp.where(even_y, from_a, from_b)
                        at = ((c * 2 + kind) * PASSES + i) * 2 + side
                        out[pl.ds(at * PASSES, PASSES), :] = mine


def corners(side_a, side_b, nx, after):
    chunks = side_a.shape[0] // ((2 * REACH + 1) * nx)
    shape = jax.ShapeDtypeStruct((chunks * 4 * PASSES * PASSES, LANES), jnp.float32)
    return pl.pallas_call(
        functools.partial(corner_kernel, nx),
        name="corners",
        out_shape=(shape, shape),
        in_specs=[VMEM] * 2 + [pl.BlockSpec(memory_space=pl.ANY)],
        out_specs=(VMEM,) * 2,
        compiler_params=pltpu.CompilerParams(vmem_limit_bytes=4 << 20),
    )(side_a, side_b, after)


def fraction(water):
    denom = water * water + MOBILITY * (1.0 - water) ** 2
    return water * water / denom


def transmit(left, right):
    return 2.0 * left * right / jnp.maximum(left + right, 1e-30)


def look_up(table, kinds):
    return jnp.take_along_axis(table, kinds, axis=1, mode="promise_in_bounds")


def deeper(values):
    turned = [pltpu.roll(v, LANES - 1, 1) for v in values]
    last = lax.broadcasted_iota(jnp.int32, turned[0].shape, 1) == LANES - 1
    return [jnp.where(last, turned[(c + 1) % len(values)], turned[c]) for c in range(len(values))]


def shallower(values):
    turned = [pltpu.roll(v, 1, 1) for v in values]
    first = lax.broadcasted_iota(jnp.int32, turned[0].shape, 1) == 0
    return [jnp.where(first, turned[c - 1], turned[c]) for c in range(len(values))]


def upwind(flow, own, far):
    return jnp.maximum(flow, 0.0) * own + jnp.minimum(flow, 0.0) * far


def flat(ref):
    return ref.reshape(math.prod(ref.shape[:-1]), LANES)


def rock_tables(perm_ref, poro_ref):
    lane = lax.broadcasted_iota(jnp.int32, (8, LANES), 1)
    perm, poro = jnp.zeros((8, LANES), jnp.float32), jnp.zeros((8, LANES), jnp.float32)
    for kind in range(perm_ref.shape[0]):
        perm = jnp.where(lane == kind + 1, perm_ref[kind], perm)
        poro = jnp.where(lane == kind + 1, poro_ref[kind], poro)
    return perm, jnp.where(lane == 0, 1.0, COMPRESS * (VOLUME * poro))


def rates_kernel(block, cells_ref, rates_ref, out_ref):
    (nx, ny, _), (_, layers, pitch) = block, wide_sizes(block)
    rank_x, rank_y = lax.axis_index("gx"), lax.axis_index("gy")
    sub = lax.broadcasted_iota(jnp.int32, (8, LANES), 0)
    lane = lax.broadcasted_iota(jnp.int32, (8, LANES), 1)
    share = out_ref.shape[0] // layers
    low_x, low_y = rank_x * nx - REACH, rank_y * ny - PAD

    def clear(i, _):
        out_ref[pl.ds(pl.multiple_of(i * share, 8), share), :] = jnp.zeros((share, LANES), jnp.float32)
        return 0

    lax.fori_loop(0, layers, clear, 0)

    def some_wells(first, count):
        def place(w):
            return cells_ref[0, w] - low_x, cells_ref[1, w] - low_y

        near = [(x >= 0) & (x < layers) & (y >= 0) & (y < pitch) for x, y in map(place, (first + i for i in range(count)))]

        @pl.when(functools.reduce(jnp.logical_or, near))
        def _():
            for i in range(count):
                @pl.when(near[i])
                def _(w=first + i):
                    (x, y), z = place(w), cells_ref[2, w]
                    row = (lax.shift_right_logical(z, 7) * layers + x) * pitch + y
                    tile = pl.multiple_of(lax.shift_left(lax.shift_right_logical(row, 3), 3), 8)
                    here = (sub == row - tile) & (lane == lax.bitwise_and(z, LANES - 1))
                    out_ref[pl.ds(tile, 8), :] = out_ref[pl.ds(tile, 8), :] + jnp.where(here, rates_ref[w], 0.0)

    wells, batch = cells_ref.shape[1], 8

    def wells_of(i, _):
        some_wells(i * batch, batch)
        return 0

    lax.fori_loop(0, wells // batch, wells_of, 0)
    if wells % batch:
        some_wells(wells - wells % batch, wells % batch)


def wide_sizes(block):
    nx, ny, nz = block
    return nz // LANES, nx + 2 * REACH, ny + 2 * PAD


def wide_shape(block):
    rows = math.prod(wide_sizes(block))
    assert block[0] % 8 == 0 and block[1] % 8 == 0 and block[2] % LANES == 0
    return jax.ShapeDtypeStruct((rows, LANES), jnp.float32)


def rates_field(block, well_cells, well_rates):
    return pl.pallas_call(
        functools.partial(rates_kernel, block),
        name="rates",
        out_shape=wide_shape(block),
        in_specs=[SMEM] * 2,
        out_specs=VMEM,
        cost_estimate=pl.CostEstimate(flops=0, bytes_accessed=6 << 20, transcendentals=0),
        compiler_params=pltpu.CompilerParams(vmem_limit_bytes=4 << 20),
    )(well_cells, well_rates)


def prepare_layers(block, fields, rates, first, last):
    press, perms, stores, trans_x, trans_y, trans_z, scale, drive = fields
    chunks, layers, pitch = wide_sizes(block)
    step = block[1] // 8
    lane = lax.broadcasted_iota(jnp.int32, (8, LANES), 1)

    def rows(layer, k, c):
        return pl.ds((c * layers + layer) * pitch + PAD + k, 8, stride=step)

    def prepare(layer, _):
        perm = {k: [perms[rows(layer, k, c), :] for c in range(chunks)] for k in range(-1, step + 1)}
        t_s = [transmit(perm[-1][c], perm[0][c]) for c in range(chunks)]
        for k in range(step):
            deep = deeper(perm[k])
            t_z = [transmit(perm[k][c], deep[c]) for c in range(chunks)]
            t_z[-1] = jnp.where(lane == LANES - 1, 0.0, t_z[-1])
            above = shallower(t_z)
            for c in range(chunks):
                at = rows(layer, k, c)
                t_x = transmit(perm[k][c], perms[rows(layer + 1, k, c), :])
                t_n = transmit(perm[k][c], perm[k + 1][c])
                t_w = trans_x[rows(jnp.maximum(layer - 1, 0), k, c), :]
                trans_x[at, :], trans_y[at, :], trans_z[at, :] = t_x, t_n, t_z[c]
                store = stores[at, :]
                factor = OMEGA / (store + ((t_x + t_w) + (t_n + t_s[c]) + (t_z[c] + above[c])))
                scale[at, :] = factor
                drive[at, :] = factor * (store * press[at, :] + rates[at, :])
                t_s[c] = t_n
        return 0

    lax.fori_loop(first, last, prepare, 0)


def ready_own_kernel(block, p_ref, rock_ref, sat_ref, rates_ref, perm_ref, poro_ref, *refs):
    fields, (frac, slope, p, rock, sat, sems) = refs[:8], refs[8:]
    press, perms, stores = fields[:3]
    (nx, ny, _), (chunks, layers, pitch) = block, wide_sizes(block)
    step = ny // 8
    fetch(rock_ref, rock, sems.at[0], True)
    fetch(p_ref, p, sems.at[1], True)
    fetch(sat_ref, sat, sems.at[2], True)
    perm_table, store_table = rock_tables(perm_ref, poro_ref)
    p2, rock2, sat2, slope2 = map(flat, (p, rock, sat, slope))
    fetch(rock_ref, rock, sems.at[0], False)
    fetch(p_ref, p, sems.at[1], False)

    def look(layer, _):
        for c in range(chunks):
            for k in range(step):
                own = pl.ds((c * nx + layer) * ny + k, 8, stride=step)
                at = pl.ds((c * layers + REACH + layer) * pitch + PAD + k, 8, stride=step)
                kind = rock2[own, :] + 1
                perms[at, :], stores[at, :] = look_up(perm_table, kind), look_up(store_table, kind)
                press[at, :] = p2[own, :]
        return 0

    lax.fori_loop(0, nx, look, 0)
    prepare_layers(block, fields, rates_ref, REACH, REACH + nx)
    fetch(sat_ref, sat, sems.at[2], False)

    def old_fraction(layer, _):
        for c in range(chunks):
            for k in range(step):
                own = pl.ds((c * nx + layer) * ny + k, 8, stride=step)
                s = sat2[own, :]
                inverse = 1.0 / (s * s + MOBILITY * (1.0 - s) ** 2)
                frac[pl.ds((c * nx + layer) * pitch + PAD + k, 8, stride=step), :] = s * s * inverse
                slope2[own, :] = 2.0 * MOBILITY * s * (1.0 - s) * (inverse * inverse)
        return 0

    lax.fori_loop(0, nx, old_fraction, 0)


def ready_own(pressure, rock_type, saturation, rates, rock_perm, rock_poro):
    block = pressure.shape
    (nx, ny, _), (chunks, _, pitch) = block, wide_sizes(block)
    own = (chunks, nx, ny, LANES)
    return pl.pallas_call(
        functools.partial(ready_own_kernel, block),
        name="ready_own",
        out_shape=(wide_shape(block),) * 8
        + (jax.ShapeDtypeStruct((chunks * nx * pitch, LANES), jnp.float32), jax.ShapeDtypeStruct(own, jnp.float32)),
        in_specs=[HBM] * 3 + [VMEM] + [SMEM] * 2,
        out_specs=(VMEM,) * 10,
        scratch_shapes=[
            pltpu.VMEM(own, jnp.float32),
            pltpu.VMEM(own, jnp.int32),
            pltpu.VMEM(own, jnp.float32),
            pltpu.SemaphoreType.DMA((3, chunks)),
        ],
        cost_estimate=pl.CostEstimate(flops=0, bytes_accessed=18 << 20, transcendentals=0),
        compiler_params=pltpu.CompilerParams(vmem_limit_bytes=5 << 20),
    )(pressure, rock_type, saturation, rates, rock_perm, rock_poro)


def ready_ends_kernel(block, xa_ref, xb_ref, rates_ref, perm_ref, poro_ref, *refs):
    fields, (ends_a, ends_b, sems) = refs[8:16], refs[16:]
    press, perms, stores = fields[:3]
    (nx, ny, _), (chunks, layers, pitch) = block, wide_sizes(block)
    step = ny // 8
    even = lax.rem(lax.axis_index("gx"), 2) == 0
    fetch(xa_ref, ends_a, sems.at[0], True)
    fetch(xb_ref, ends_b, sems.at[1], True)
    perm_table, store_table = rock_tables(perm_ref, poro_ref)
    fetch(xa_ref, ends_a, sems.at[0], False)
    fetch(xb_ref, ends_b, sems.at[1], False)
    a2, b2 = flat(ends_a), flat(ends_b)

    def look(j, _):
        for c in range(chunks):
            for k in range(step):
                got = pl.ds((c * 2 * REACH + j) * ny + k, 8, stride=step)
                kinds_got = pl.ds((c * 2 * REACH + REACH + j) * ny + k, 8, stride=step)
                for low in (True, False):
                    at = pl.ds((c * layers + j + (0 if low else REACH + nx)) * pitch + PAD + k, 8, stride=step)
                    one, two = (b2, a2) if low else (a2, b2)
                    press[at, :] = jnp.where(even, one[got, :], two[got, :])
                    kind = jnp.where(even, one[kinds_got, :], two[kinds_got, :]).astype(jnp.int32)
                    perms[at, :], stores[at, :] = look_up(perm_table, kind), look_up(store_table, kind)
        return 0

    lax.fori_loop(0, REACH, look, 0)
    prepare_layers(block, fields, rates_ref, 0, REACH + 1)
    prepare_layers(block, fields, rates_ref, REACH + nx - 1, layers - 1)


def ready_ends(block, ends, rates, rock_perm, rock_poro, fields):
    (_, ny, _), (chunks, _, _) = block, wide_sizes(block)
    inputs = (*ends, rates, rock_perm, rock_poro, *fields)
    end = pltpu.VMEM((chunks, 2 * REACH, ny, LANES), jnp.float32)
    return pl.pallas_call(
        functools.partial(ready_ends_kernel, block),
        name="ready_ends",
        out_shape=tuple(jax.ShapeDtypeStruct(f.shape, f.dtype) for f in fields),
        in_specs=[VMEM] * 3 + [SMEM] * 2 + [VMEM] * len(fields),
        out_specs=(VMEM,) * len(fields),
        input_output_aliases={5 + i: i for i in range(len(fields))},
        scratch_shapes=[end, end, pltpu.SemaphoreType.DMA((2, chunks))],
        cost_estimate=pl.CostEstimate(flops=0, bytes_accessed=9 << 20, transcendentals=0),
        compiler_params=pltpu.CompilerParams(vmem_limit_bytes=4 << 20),
    )(*inputs)


def flow_kernel(
    block, flux_ref, sat_ref, ya_ref, yb_ref, ca_ref, cb_ref, rates_ref, slope_ref, perm_ref, poro_ref, *refs
):
    press, perms, stores, trans_x, trans_y, trans_z, scale, drive, frac = refs[9:18]
    press_ref, prep_ref, inlet_ref, other, flux, sat, leave, sems = refs[18:]
    (nx, ny, _), (chunks, layers, pitch) = block, wide_sizes(block)
    depth, step = layers * pitch, ny // 8
    tiles = (ny + 2 * PASSES) // 8
    side_rows = (2 * REACH + 1) * nx
    even_x, even_y = lax.rem(lax.axis_index("gx"), 2) == 0, lax.rem(lax.axis_index("gy"), 2) == 0
    press2, other2, perms2, stores2, rates2, frac2 = press, other, perms, stores, rates_ref, frac
    tx2, ty2, tz2, scale2, drive2 = trans_x, trans_y, trans_z, scale, drive
    flux2, sat2, slope2, leave2 = map(flat, (flux, sat, slope_ref, leave))
    fetch(flux_ref, flux, sems.at[0], True)
    fetch(sat_ref, sat, sems.at[1], True)
    perm_table, store_table = rock_tables(perm_ref, poro_ref)
    lane = lax.broadcasted_iota(jnp.int32, (8, LANES), 1)

    for c in range(chunks):
        for j in range(REACH):
            for half in range(nx // 8):
                start = c * side_rows + j * nx + half * 8
                at = c * depth + (REACH + half * 8) * pitch + j
                low = pl.ds(at + PAD - REACH, 8, stride=pitch)
                high = pl.ds(at + PAD + ny, 8, stride=pitch)
                a, b = ya_ref[pl.ds(start, 8), :], yb_ref[pl.ds(start, 8), :]
                press2[low, :], press2[high, :] = jnp.where(even_y, b, a), jnp.where(even_y, a, b)
                a, b = (ref[pl.ds(start + REACH * nx, 8), :].astype(jnp.int32) for ref in (ya_ref, yb_ref))
                for where, kind in ((low, jnp.where(even_y, b, a)), (high, jnp.where(even_y, a, b))):
                    perms2[where, :], stores2[where, :] = look_up(perm_table, kind), look_up(store_table, kind)
        start = c * side_rows + 2 * REACH * nx
        a, b = fraction(ya_ref[pl.ds(start, nx), :]), fraction(yb_ref[pl.ds(start, nx), :])
        at = c * nx * pitch
        frac2[pl.ds(at + PAD - 1, nx, stride=pitch), :] = jnp.where(even_y, b, a)
        frac2[pl.ds(at + PAD + ny, nx, stride=pitch), :] = jnp.where(even_y, a, b)
        both = 2 * PASSES
        for k in range(PASSES):
            start = (c * 2 * PASSES + k) * both
            a, b = ca_ref[pl.ds(start, both), :], cb_ref[pl.ds(start, both), :]
            ends = ((1 + k, jnp.where(even_x, b, a)), (REACH + nx + k, jnp.where(even_x, a, b)))
            start += PASSES * both
            a, b = (ref[pl.ds(start, both), :].astype(jnp.int32) for ref in (ca_ref, cb_ref))
            kinds = (jnp.where(even_x, b, a), jnp.where(even_x, a, b))
            for (layer, value), kind in zip(ends, kinds):
                for ref, new in ((press2, value), (perms2, look_up(perm_table, kind)), (stores2, look_up(store_table, kind))):
                    at = c * depth + layer * pitch + PAD
                    ref[pl.ds(at - PASSES, PASSES), :] = new[:PASSES]
                    ref[pl.ds(at + ny, PASSES), :] = new[PASSES:]

    def complete(group, _):
        for first in (PAD - PASSES, PAD + ny - 1):
            def rows(k, by, c):
                return pl.ds(c * depth + (1 + group * 8 + by) * pitch + first + k, 8, stride=pitch)

            perm = {k: [perms2[rows(k, 0, c), :] for c in range(chunks)] for k in range(-1, PASSES + 2)}
            t_s = [transmit(perm[-1][c], perm[0][c]) for c in range(chunks)]
            for c in range(chunks):
                ty2[rows(-1, 0, c), :] = t_s[c]
            for k in range(PASSES + 1):
                deep = deeper(perm[k])
                t_z = [transmit(perm[k][c], deep[c]) for c in range(chunks)]
                t_z[-1] = jnp.where(lane == LANES - 1, 0.0, t_z[-1])
                above = shallower(t_z)
                for c in range(chunks):
                    at = rows(k, 0, c)
                    t_x = transmit(perm[k][c], perms2[rows(k, 1, c), :])
                    t_w = transmit(perm[k][c], perms2[rows(k, -1, c), :])
                    t_n = transmit(perm[k][c], perm[k + 1][c])
                    tx2[at, :], ty2[at, :], tz2[at, :] = t_x, t_n, t_z[c]
                    store = stores2[at, :]
                    factor = OMEGA / (store + ((t_x + t_w) + (t_n + t_s[c]) + (t_z[c] + above[c])))
                    scale2[at, :] = factor
                    drive2[at, :] = factor * (store * press2[at, :] + rates2[at, :])
                    t_s[c] = t_n
        return 0

    lax.fori_loop(0, (layers - 2) // 8, complete, 0)

    def relax(source, target, number):
        def one(layer, _):
            def rows(k, c, by=0):
                return pl.ds(c * depth + (layer + by) * pitch + PAD - PASSES + k, 8, stride=tiles)

            now = {k: [source[rows(k, c), :] for c in range(chunks)] for k in range(-1, tiles + 1)}
            for k in range(tiles):
                here = now[k]
                t_z = [tz2[rows(k, c), :] for c in range(chunks)]
                deep = deeper(here)
                shallow = shallower([t_z[c] * here[c] for c in range(chunks)])
                for c in range(chunks):
                    at = rows(k, c)
                    total = (
                        (tx2[at, :] * source[rows(k, c, 1), :] + tx2[rows(k, c, -1), :] * source[rows(k, c, -1), :])
                        + (ty2[at, :] * now[k + 1][c] + ty2[rows(k - 1, c), :] * now[k - 1][c])
                        + (t_z[c] * deep[c] + shallow[c])
                    )
                    target[at, :] = (1.0 - OMEGA) * here[c] + (drive2[at, :] + scale2[at, :] * total)
            return 0

        lax.fori_loop(min(number + 1, REACH), layers - number, one, 0, unroll=UNROLL)

    for number in range(1, PASSES + 1):
        source, target = (press2, other2) if number % 2 else (other2, press2)
        relax(source, target, number)
    final2 = press2 if PASSES % 2 == 0 else other2

    def send_out(start):
        for c in range(chunks):
            copy = pltpu.make_async_copy(leave.at[c], press_ref.at[:, :, pl.ds(c * LANES, LANES)], sems.at[2, c])
            copy.start() if start else copy.wait()

    def gather(layer, _):
        for c in range(chunks):
            for k in range(step):
                at = pl.ds(c * depth + (REACH + layer) * pitch + PAD + k, 8, stride=step)
                leave2[pl.ds((c * nx + layer) * ny + k, 8, stride=step), :] = final2[at, :]
        return 0

    step = ny // 8
    lax.fori_loop(0, nx, gather, 0)
    send_out(True)
    fetch(flux_ref, flux, sems.at[0], False)
    fetch(sat_ref, sat, sems.at[1], False)
    for c in range(chunks):
        inlet_ref[pl.ds(c * ny, ny), :] = flux[c, 0]

    def fluxes(layer, _):
        def wide(ref, k, by=0):
            return [ref[pl.ds(c * depth + (REACH + layer + by) * pitch + PAD + k, 8, stride=step), :] for c in range(chunks)]

        def own(ref, k):
            return [ref[pl.ds((c * nx + layer) * ny + k, 8, stride=step), :] for c in range(chunks)]

        here = {k: wide(final2, k) for k in range(-1, step + 1)}
        old = {
            k: [frac2[pl.ds((c * nx + layer) * pitch + PAD + k, 8, stride=step), :] for c in range(chunks)]
            for k in range(-1, step + 1)
        }
        south = None
        for k in range(-1, step):
            t_y = wide(ty2, k)
            north = [upwind(t_y[c] * (here[k][c] - here[k + 1][c]), old[k][c], old[k + 1][c]) for c in range(chunks)]
            if k >= 0:
                t_z, below, old_below = wide(tz2, k), deeper(here[k]), deeper(old[k])
                down = [upwind(t_z[c] * (here[k][c] - below[c]), old[k][c], old_below[c]) for c in range(chunks)]
                from_above = shallower(down)
                east, t_x, rate, store = wide(final2, k, 1), wide(tx2, k), wide(rates2, k), wide(stores2, k)
                imposed, water, bend = own(flux2, k), own(sat2, k), own(slope2, k)
                for c in range(chunks):
                    leaving = (north[c] - south[c]) + (down[c] - from_above[c])
                    explicit = jnp.maximum(rate[c], 0.0) + jnp.minimum(rate[c], 0.0) * old[k][c] - leaving
                    through = jnp.maximum(imposed[c] + t_x[c] * (here[k][c] - east[c]), 0.0)
                    volume = store[c] * (1.0 / COMPRESS)
                    gain = 1.0 / (volume + through * bend[c])
                    first = water[c] - (through * old[k][c] - explicit) * gain
                    for i, value in enumerate((first, gain, through, volume, volume * water[c] + explicit)):
                        prep_ref[layer, pl.ds((i * chunks + c) * ny + k, 8, stride=step), :] = value
            south = north
        return 0

    lax.fori_loop(0, nx, fluxes, 0)
    send_out(False)


def flow(base_flux, saturation, sides, ends_corner, rates, made, rock_perm, rock_poro):
    nx, ny, nz = base_flux.shape
    chunks = nz // LANES
    *fields, slope = made
    own = pltpu.VMEM((chunks, nx, ny, LANES), jnp.float32)
    inputs = (base_flux, saturation, *sides, *ends_corner, rates, slope, rock_perm, rock_poro, *fields)
    first = len(inputs) - len(fields)
    return pl.pallas_call(
        functools.partial(flow_kernel, base_flux.shape),
        name="flow",
        out_shape=tuple(jax.ShapeDtypeStruct(f.shape, f.dtype) for f in fields) + (
            jax.ShapeDtypeStruct(base_flux.shape, jnp.float32),
            jax.ShapeDtypeStruct((nx, 5 * chunks * ny, LANES), jnp.float32),
            jax.ShapeDtypeStruct((chunks * ny, LANES), jnp.float32),
        ),
        in_specs=[HBM] * 2 + [VMEM] * 6 + [SMEM] * 2 + [VMEM] * len(fields),
        out_specs=(VMEM,) * len(fields) + (HBM, VMEM, VMEM),
        input_output_aliases={first + i: i for i in range(len(fields))},
        scratch_shapes=[pltpu.VMEM(wide_shape(base_flux.shape).shape, jnp.float32), own, own, own, pltpu.SemaphoreType.DMA((3, chunks))],
        compiler_params=pltpu.CompilerParams(vmem_limit_bytes=8 << 20),
    )(*inputs)[-3:]


def stage_kernel(stage, inflow_ref, prep_ref, *refs):
    sat_ref, out_ref, sat, out_sems = refs[-4:]
    nx, rows, _ = prep_ref.shape
    plane = rows // 5
    chunks, _, ny, _ = sat.shape

    @pl.when(lax.axis_index("gx") == stage)
    def _():
        def send(layer):
            return [
                pltpu.make_async_copy(sat.at[c, layer], sat_ref.at[layer, :, pl.ds(c * LANES, LANES)], out_sems.at[layer, c])
                for c in range(chunks)
            ]

        def advance(layer, incoming):
            first, gain, through, volume, held = (prep_ref[layer, pl.ds(i * plane, plane), :] for i in range(5))
            known = held + incoming
            water = jnp.clip(first + gain * incoming, 0.0, 1.0)
            for _ in range(NEWTON - 1):
                square = water * water
                part = 1.5 * square
                denom = part + (0.5 - water)
                denom = denom * denom
                top = denom * known + through * (square * (0.5 - part))
                bottom = denom * volume + through * (water - square)
                water = jnp.clip(top / bottom, 0.0, 1.0)
            for c in range(chunks):
                sat[c, layer] = water[c * ny : (c + 1) * ny]
            for copy in send(layer):
                copy.start()
            square = water * water
            return (through * square) / (1.5 * square + (0.5 - water))

        out_ref[...] = lax.fori_loop(0, nx, advance, inflow_ref[...])

        def finish(layer, _):
            for copy in send(layer):
                copy.wait()
            return 0

        lax.fori_loop(0, nx, finish, 0)


def run_stage(stage, inflow, prep, shape, saturation):
    nx, ny, nz = shape
    chunks = nz // LANES
    block = jax.ShapeDtypeStruct(shape, jnp.float32)
    return pl.pallas_call(
        functools.partial(stage_kernel, stage),
        name="stage",
        out_shape=(block, jax.ShapeDtypeStruct(inflow.shape, jnp.float32)),
        in_specs=[VMEM, VMEM] + [HBM] * len(saturation),
        out_specs=(HBM, VMEM),
        input_output_aliases={2: 0} if saturation else {},
        scratch_shapes=[
            pltpu.VMEM((chunks, nx, ny, LANES), jnp.float32),
            pltpu.SemaphoreType.DMA((nx, chunks)),
        ],
        compiler_params=pltpu.CompilerParams(vmem_limit_bytes=12 << 20),
    )(inflow, prep, *saturation)


def step(rock_type, rock_perm, rock_poro, base_flux, initial_pressure, old_saturation, well_cells, well_rates):
    nx = rock_type.shape[0]
    sides = pack_sides(initial_pressure, rock_type, old_saturation)
    sides_got = swap(*sides, "gy")
    ends = swap(*pack_ends(initial_pressure, rock_type, sides[0]), "gx")
    rates = rates_field(rock_type.shape, well_cells, well_rates)
    *fields, frac, slope = ready_own(initial_pressure, rock_type, old_saturation, rates, rock_perm, rock_poro)
    ends_corner = swap(*corners(*sides_got, nx, slope), "gx")
    fields = ready_ends(rock_type.shape, ends, rates, rock_perm, rock_poro, fields)
    made = (*fields, frac, slope)
    pressure, prep, inflow = flow(base_flux, old_saturation, sides_got, ends_corner, rates, made, rock_perm, rock_poro)
    saturation = ()
    count = lax.axis_size("gx")
    for stage in range(count):
        *saturation, outflow = run_stage(stage, inflow, prep, rock_type.shape, saturation)
        if stage < count - 1:
            inflow = lax.ppermute(outflow, "gx", [(stage, stage + 1)])
    return pressure, saturation[0]


def solution(mesh):
    return jax.shard_map(
        step,
        mesh=mesh,
        in_specs=(
            P("gx", "gy", None),
            P(),
            P(),
            P("gx", "gy", None),
            P("gx", "gy", None),
            P("gx", "gy", None),
            P(),
            P(),
        ),
        out_specs=(P("gx", "gy", None), P("gx", "gy", None)),
        check_vma=False,
    )
```

```python
import functools
import math

import jax
import jax.numpy as jnp
from jax import lax
from jax.experimental import pallas as pl
from jax.experimental.pallas import tpu as pltpu
from jax.sharding import PartitionSpec as P


PASSES = 4
NEWTON = 3

MOBILITY = 0.5
OMEGA = 0.8
VOLUME = 4.0
COMPRESS = 0.5

LANES = 128
STAGE_UNROLL = 2
UNROLL = 4
ENDS_LIMIT = 59 << 20
SIDES_LIMIT = 62 << 20
OWN_LIMIT = 5 << 20
FLOW_LIMIT = 8 << 20
REACH = PASSES + 1
PAD = REACH + 1
HBM = pl.BlockSpec(memory_space=pltpu.MemorySpace.HBM)
VMEM = pl.BlockSpec(memory_space=pltpu.VMEM)
SMEM = pl.BlockSpec(memory_space=pltpu.SMEM)


def swap_pairs(axis):
    count = lax.axis_size(axis)
    pairs = []
    for first in (0, 1):
        ups = [(i, i + 1) for i in range(first, count - 1, 2)]
        pairs.append(ups + [(j, i) for i, j in ups])
    return pairs


def swap(value_a, value_b, axis):
    pairs_a, pairs_b = swap_pairs(axis)
    got_a = lax.ppermute(value_a, axis, pairs_a)
    got_b = lax.ppermute(value_b, axis, pairs_b)
    return got_a, got_b


def fetch(source, target, sems, start):
    for c in range(target.shape[0]):
        copy = pltpu.make_async_copy(source.at[:, :, pl.ds(c * LANES, LANES)], target.at[c], sems.at[c])
        copy.start() if start else copy.wait()


def pack_sides_kernel(p_ref, rock_ref, sat_ref, ya_ref, yb_ref, p, rock, sat, sems):
    chunks, nx = p.shape[1], p.shape[2]
    ny = p_ref.shape[1]
    even = lax.rem(lax.axis_index("gy"), 2) == 0
    outs = ((ya_ref, even), (yb_ref, jnp.logical_not(even)))

    def copies(i):
        _, high = outs[i]
        tile = pl.ds(pl.multiple_of(jnp.where(high, ny - 8, 0), 8), 8)
        return [
            pltpu.make_async_copy(source.at[:, tile, pl.ds(c * LANES, LANES)], target.at[i, c], sems.at[i, n, c])
            for n, (source, target) in enumerate(((p_ref, p), (rock_ref, rock), (sat_ref, sat)))
            for c in range(chunks)
        ]

    for i in range(2):
        for copy in copies(i):
            copy.start()
    p2, rock2, sat2 = (f.reshape(2 * chunks * nx * 8, LANES) for f in (p, rock, sat))
    rows = (2 * REACH + 1) * nx
    for i, (out, high) in enumerate(outs):
        for copy in copies(i):
            copy.wait()
        first = jnp.where(high, 8 - REACH, 0)
        edge = jnp.where(high, 7, 0)
        for c in range(chunks):
            base = (i * chunks + c) * nx * 8
            for j in range(REACH):
                out[pl.ds(c * rows + j * nx, nx), :] = p2[pl.ds(base + first + j, nx, stride=8), :]
                kinds = rock2[pl.ds(base + first + j, nx, stride=8), :]
                out[pl.ds(c * rows + (REACH + j) * nx, nx), :] = kinds.astype(jnp.float32) + 1.0
            out[pl.ds(c * rows + 2 * REACH * nx, nx), :] = sat2[pl.ds(base + edge, nx, stride=8), :]


def pack_sides(pressure, rock_type, saturation):
    nx, _, nz = pressure.shape
    chunks = nz // LANES
    side = jax.ShapeDtypeStruct((chunks * (2 * REACH + 1) * nx, LANES), jnp.float32)
    block = (2, chunks, nx, 8, LANES)
    return pl.pallas_call(
        pack_sides_kernel,
        name="pack_sides",
        out_shape=(side, side),
        in_specs=[HBM] * 3,
        out_specs=(VMEM,) * 2,
        scratch_shapes=[
            pltpu.VMEM(block, jnp.float32),
            pltpu.VMEM(block, jnp.int32),
            pltpu.VMEM(block, jnp.float32),
            pltpu.SemaphoreType.DMA((2, 3, chunks)),
        ],
        compiler_params=pltpu.CompilerParams(vmem_limit_bytes=SIDES_LIMIT),
    )(pressure, rock_type, saturation)


def pack_ends_kernel(p_ref, rock_ref, _, xa_ref, xb_ref, rock, sems):
    nx = p_ref.shape[0]
    chunks = xa_ref.shape[0]
    even = lax.rem(lax.axis_index("gx"), 2) == 0
    outs = (xa_ref, xb_ref)
    copies = []
    for i, high in enumerate((even, jnp.logical_not(even))):
        layers = pl.ds(jnp.where(high, nx - REACH, 0), REACH)
        for c in range(chunks):
            lanes = pl.ds(c * LANES, LANES)
            copies.append((
                pltpu.make_async_copy(rock_ref.at[layers, :, lanes], rock.at[i, c], sems.at[i, c, 0]),
                pltpu.make_async_copy(p_ref.at[layers, :, lanes], outs[i].at[c, pl.ds(0, REACH)], sems.at[i, c, 1]),
            ))
    for pair in copies:
        for copy in pair:
            copy.start()
    for i in range(2):
        for c in range(chunks):
            copies[i * chunks + c][0].wait()
            outs[i][c, pl.ds(REACH, REACH)] = rock[i, c].astype(jnp.float32) + 1.0
    for pair in copies:
        pair[1].wait()


def pack_ends(pressure, rock_type, after):
    _, ny, nz = pressure.shape
    chunks = nz // LANES
    end = jax.ShapeDtypeStruct((chunks, 2 * REACH, ny, LANES), jnp.float32)
    return pl.pallas_call(
        pack_ends_kernel,
        name="pack_ends",
        out_shape=(end, end),
        in_specs=[HBM] * 2 + [pl.BlockSpec(memory_space=pl.ANY)],
        out_specs=(VMEM,) * 2,
        scratch_shapes=[pltpu.VMEM((2, chunks, REACH, ny, LANES), jnp.int32), pltpu.SemaphoreType.DMA((2, chunks, 2))],
        compiler_params=pltpu.CompilerParams(vmem_limit_bytes=ENDS_LIMIT),
    )(pressure, rock_type, after)


def corner_kernel(nx, ya_ref, yb_ref, _, ca_ref, cb_ref):
    rows = (2 * REACH + 1) * nx
    chunks = ya_ref.shape[0] // rows
    even_y = lax.rem(lax.axis_index("gy"), 2) == 0
    even_x = lax.rem(lax.axis_index("gx"), 2) == 0
    for out, high in ((ca_ref, even_x), (cb_ref, jnp.logical_not(even_x))):
        layer = jnp.where(high, nx - PASSES, 0)
        for c in range(chunks):
            for kind in range(2):
                for i in range(PASSES):
                    for side in range(2):
                        start = c * rows + (kind * REACH + 1 - side) * nx + layer + i
                        from_a = ya_ref[pl.ds(start, PASSES, stride=nx), :]
                        from_b = yb_ref[pl.ds(start, PASSES, stride=nx), :]
                        mine = jnp.where(even_y, from_b, from_a) if side == 0 else jnp.where(even_y, from_a, from_b)
                        at = ((c * 2 + kind) * PASSES + i) * 2 + side
                        out[pl.ds(at * PASSES, PASSES), :] = mine


def corners(side_a, side_b, nx, after):
    chunks = side_a.shape[0] // ((2 * REACH + 1) * nx)
    shape = jax.ShapeDtypeStruct((chunks * 4 * PASSES * PASSES, LANES), jnp.float32)
    return pl.pallas_call(
        functools.partial(corner_kernel, nx),
        name="corners",
        out_shape=(shape, shape),
        in_specs=[VMEM] * 2 + [pl.BlockSpec(memory_space=pl.ANY)],
        out_specs=(VMEM,) * 2,
        compiler_params=pltpu.CompilerParams(vmem_limit_bytes=4 << 20),
    )(side_a, side_b, after)


def fraction(water):
    denom = water * water + MOBILITY * (1.0 - water) ** 2
    return water * water / denom


def transmit(left, right):
    return 2.0 * left * right / jnp.maximum(left + right, 1e-30)


def look_up(table, kinds):
    return jnp.take_along_axis(table, kinds, axis=1, mode="promise_in_bounds")


def deeper(values):
    turned = [pltpu.roll(v, LANES - 1, 1) for v in values]
    last = lax.broadcasted_iota(jnp.int32, turned[0].shape, 1) == LANES - 1
    return [jnp.where(last, turned[(c + 1) % len(values)], turned[c]) for c in range(len(values))]


def shallower(values):
    turned = [pltpu.roll(v, 1, 1) for v in values]
    first = lax.broadcasted_iota(jnp.int32, turned[0].shape, 1) == 0
    return [jnp.where(first, turned[c - 1], turned[c]) for c in range(len(values))]


def upwind(flow, own, far):
    return jnp.maximum(flow, 0.0) * own + jnp.minimum(flow, 0.0) * far


def flat(ref):
    return ref.reshape(math.prod(ref.shape[:-1]), LANES)


def rock_tables(perm_ref, poro_ref):
    lane = lax.broadcasted_iota(jnp.int32, (8, LANES), 1)
    table = jnp.zeros((8, LANES), jnp.float32)
    for kind in range(perm_ref.shape[0]):
        table = jnp.where(lane == kind + 1, perm_ref[kind], table)
    return table, [COMPRESS * (VOLUME * poro_ref[kind]) for kind in range(perm_ref.shape[0])]


def rock_of(kind, tables):
    table, stores = tables
    store = jnp.ones(kind.shape, jnp.float32)
    for i, value in enumerate(stores):
        store = jnp.where(kind == i + 1, value, store)
    return look_up(table, kind), store


def fill_rates(block, cells_ref, rates_ref, out_ref):
    (nx, ny, _), (_, layers, pitch) = block, wide_sizes(block)
    rank_x, rank_y = lax.axis_index("gx"), lax.axis_index("gy")
    sub = lax.broadcasted_iota(jnp.int32, (8, LANES), 0)
    lane = lax.broadcasted_iota(jnp.int32, (8, LANES), 1)
    share = out_ref.shape[0] // layers
    low_x, low_y = rank_x * nx - REACH, rank_y * ny - PAD

    def clear(i, _):
        out_ref[pl.ds(pl.multiple_of(i * share, 8), share), :] = jnp.zeros((share, LANES), jnp.float32)
        return 0

    lax.fori_loop(0, layers, clear, 0)

    def some_wells(first, count):
        def place(w):
            return cells_ref[0, w] - low_x, cells_ref[1, w] - low_y

        near = [(x >= 0) & (x < layers) & (y >= 0) & (y < pitch) for x, y in map(place, (first + i for i in range(count)))]

        @pl.when(functools.reduce(jnp.logical_or, near))
        def _():
            for i in range(count):
                @pl.when(near[i])
                def _(w=first + i):
                    (x, y), z = place(w), cells_ref[2, w]
                    row = (lax.shift_right_logical(z, 7) * layers + x) * pitch + y
                    tile = pl.multiple_of(lax.shift_left(lax.shift_right_logical(row, 3), 3), 8)
                    here = (sub == row - tile) & (lane == lax.bitwise_and(z, LANES - 1))
                    out_ref[pl.ds(tile, 8), :] = out_ref[pl.ds(tile, 8), :] + jnp.where(here, rates_ref[w], 0.0)

    wells, batch = cells_ref.shape[1], 8

    def wells_of(i, _):
        some_wells(i * batch, batch)
        return 0

    lax.fori_loop(0, wells // batch, wells_of, 0)
    if wells % batch:
        some_wells(wells - wells % batch, wells % batch)


def wide_sizes(block):
    nx, ny, nz = block
    return nz // LANES, nx + 2 * REACH, ny + 2 * PAD


def wide_shape(block):
    rows = math.prod(wide_sizes(block))
    assert block[0] % 8 == 0 and block[1] % 8 == 0 and block[2] % LANES == 0
    return jax.ShapeDtypeStruct((rows, LANES), jnp.float32)


def prepare_layers(block, fields, rates, first, last):
    press, perms, stores, trans_x, trans_y, trans_z, scale, drive = fields
    chunks, layers, pitch = wide_sizes(block)
    step = block[1] // 8
    lane = lax.broadcasted_iota(jnp.int32, (8, LANES), 1)

    def rows(layer, k, c):
        return pl.ds((c * layers + layer) * pitch + PAD + k, 8, stride=step)

    def prepare(layer, _):
        perm = {k: [perms[rows(layer, k, c), :] for c in range(chunks)] for k in range(-1, step + 1)}
        t_s = [transmit(perm[-1][c], perm[0][c]) for c in range(chunks)]
        for k in range(step):
            deep = deeper(perm[k])
            t_z = [transmit(perm[k][c], deep[c]) for c in range(chunks)]
            t_z[-1] = jnp.where(lane == LANES - 1, 0.0, t_z[-1])
            above = shallower(t_z)
            for c in range(chunks):
                at = rows(layer, k, c)
                t_x = transmit(perm[k][c], perms[rows(layer + 1, k, c), :])
                t_n = transmit(perm[k][c], perm[k + 1][c])
                t_w = trans_x[rows(jnp.maximum(layer - 1, 0), k, c), :]
                trans_x[at, :], trans_y[at, :], trans_z[at, :] = t_x, t_n, t_z[c]
                store = stores[at, :]
                factor = OMEGA / (store + ((t_x + t_w) + (t_n + t_s[c]) + (t_z[c] + above[c])))
                scale[at, :] = factor
                drive[at, :] = factor * (store * press[at, :] + rates[at, :])
                t_s[c] = t_n
        return 0

    lax.fori_loop(first, last, prepare, 0, unroll=2)


def ready_own_kernel(block, rock_ref, p_ref, sat_ref, cells_ref, well_ref, perm_ref, poro_ref, *refs):
    fields, (frac, slope, sat, rates_ref, rock, p, sems) = refs[:8], refs[8:]
    sources = ((rock_ref, rock), (p_ref, p), (sat_ref, sat))
    for i, (source, target) in enumerate(sources):
        fetch(source, target, sems.at[i], True)
    fill_rates(block, cells_ref, well_ref, rates_ref)
    press, perms, stores = fields[:3]
    (nx, ny, _), (chunks, layers, pitch) = block, wide_sizes(block)
    step = ny // 8
    tables = rock_tables(perm_ref, poro_ref)
    p2, rock2, sat2, slope2 = map(flat, (p, rock, sat, slope))
    for i, (source, target) in enumerate(sources):
        fetch(source, target, sems.at[i], False)

    def look(layer, _):
        for c in range(chunks):
            for k in range(step):
                own = pl.ds((c * nx + layer) * ny + k, 8, stride=step)
                at = pl.ds((c * layers + REACH + layer) * pitch + PAD + k, 8, stride=step)
                kind = rock2[own, :] + 1
                perms[at, :], stores[at, :] = rock_of(kind, tables)
                press[at, :] = p2[own, :]
        return 0

    lax.fori_loop(0, nx, look, 0, unroll=4)
    prepare_layers(block, fields, rates_ref, REACH, REACH + nx)

    def old_fraction(layer, _):
        for c in range(chunks):
            for k in range(step):
                own = pl.ds((c * nx + layer) * ny + k, 8, stride=step)
                s = sat2[own, :]
                inverse = 1.0 / (s * s + MOBILITY * (1.0 - s) ** 2)
                frac[pl.ds((c * nx + layer) * pitch + PAD + k, 8, stride=step), :] = s * s * inverse
                slope2[own, :] = 2.0 * MOBILITY * s * (1.0 - s) * (inverse * inverse)
        return 0

    lax.fori_loop(0, nx, old_fraction, 0, unroll=4)


def ready_own(pressure, rock_type, saturation, well_cells, well_rates, rock_perm, rock_poro):
    block = pressure.shape
    (nx, ny, _), (chunks, _, pitch) = block, wide_sizes(block)
    own = (chunks, nx, ny, LANES)
    return pl.pallas_call(
        functools.partial(ready_own_kernel, block),
        name="ready_own",
        out_shape=(wide_shape(block),) * 8
        + tuple(jax.ShapeDtypeStruct(shape, jnp.float32) for shape in ((chunks * nx * pitch, LANES), own, own))
        + (wide_shape(block),),
        in_specs=[HBM] * 3 + [SMEM] * 4,
        out_specs=(VMEM,) * 12,
        scratch_shapes=[
            pltpu.VMEM(own, jnp.int32),
            pltpu.VMEM(own, jnp.float32),
            pltpu.SemaphoreType.DMA((3, chunks)),
        ],
        cost_estimate=pl.CostEstimate(flops=0, bytes_accessed=24 << 20, transcendentals=0),
        compiler_params=pltpu.CompilerParams(vmem_limit_bytes=OWN_LIMIT),
    )(rock_type, pressure, saturation, well_cells, well_rates, rock_perm, rock_poro)


def ready_ends_kernel(block, xa_ref, xb_ref, rates_ref, perm_ref, poro_ref, *refs):
    fields = refs[8:16]
    press, perms, stores = fields[:3]
    (nx, ny, _), (chunks, layers, pitch) = block, wide_sizes(block)
    step = ny // 8
    even = lax.rem(lax.axis_index("gx"), 2) == 0
    tables = rock_tables(perm_ref, poro_ref)
    a2, b2 = flat(xa_ref), flat(xb_ref)

    def look(j, _):
        for c in range(chunks):
            for k in range(step):
                got = pl.ds((c * 2 * REACH + j) * ny + k, 8, stride=step)
                kinds_got = pl.ds((c * 2 * REACH + REACH + j) * ny + k, 8, stride=step)
                for low in (True, False):
                    at = pl.ds((c * layers + j + (0 if low else REACH + nx)) * pitch + PAD + k, 8, stride=step)
                    one, two = (b2, a2) if low else (a2, b2)
                    press[at, :] = jnp.where(even, one[got, :], two[got, :])
                    kind = jnp.where(even, one[kinds_got, :], two[kinds_got, :]).astype(jnp.int32)
                    perms[at, :], stores[at, :] = rock_of(kind, tables)
        return 0

    lax.fori_loop(0, REACH, look, 0, unroll=True)
    prepare_layers(block, fields, rates_ref, 0, REACH + 1)
    prepare_layers(block, fields, rates_ref, REACH + nx - 1, layers - 1)


def ready_ends(block, ends, rates, rock_perm, rock_poro, fields):
    inputs = (*ends, rates, rock_perm, rock_poro, *fields)
    return pl.pallas_call(
        functools.partial(ready_ends_kernel, block),
        name="ready_ends",
        out_shape=tuple(jax.ShapeDtypeStruct(f.shape, f.dtype) for f in fields),
        in_specs=[VMEM] * 3 + [SMEM] * 2 + [VMEM] * len(fields),
        out_specs=(VMEM,) * len(fields),
        input_output_aliases={5 + i: i for i in range(len(fields))},
        cost_estimate=pl.CostEstimate(flops=0, bytes_accessed=9 << 20, transcendentals=0),
        compiler_params=pltpu.CompilerParams(vmem_limit_bytes=4 << 20),
    )(*inputs)


def flow_kernel(
    block, flux_ref, sat, ya_ref, yb_ref, ca_ref, cb_ref, rates_ref, slope_ref, perm_ref, poro_ref, *refs
):
    press, perms, stores, trans_x, trans_y, trans_z, scale, drive, frac = refs[9:18]
    press_ref, prep_ref, inlet_ref, other, leave, flux, sems = refs[18:]
    (nx, ny, _), (chunks, layers, pitch) = block, wide_sizes(block)
    depth, step = layers * pitch, ny // 8
    tiles = (ny + 2 * PASSES) // 8
    side_rows = (2 * REACH + 1) * nx
    even_x, even_y = lax.rem(lax.axis_index("gx"), 2) == 0, lax.rem(lax.axis_index("gy"), 2) == 0
    press2, other2, perms2, stores2, rates2, frac2 = press, other, perms, stores, rates_ref, frac
    tx2, ty2, tz2, scale2, drive2 = trans_x, trans_y, trans_z, scale, drive
    flux2, sat2, slope2, leave2 = map(flat, (flux, sat, slope_ref, leave))
    fetch(flux_ref, flux, sems.at[0], True)
    tables = rock_tables(perm_ref, poro_ref)
    lane = lax.broadcasted_iota(jnp.int32, (8, LANES), 1)

    for c in range(chunks):
        for j in range(REACH):
            for half in range(nx // 8):
                start = c * side_rows + j * nx + half * 8
                at = c * depth + (REACH + half * 8) * pitch + j
                low = pl.ds(at + PAD - REACH, 8, stride=pitch)
                high = pl.ds(at + PAD + ny, 8, stride=pitch)
                a, b = ya_ref[pl.ds(start, 8), :], yb_ref[pl.ds(start, 8), :]
                press2[low, :], press2[high, :] = jnp.where(even_y, b, a), jnp.where(even_y, a, b)
                a, b = (ref[pl.ds(start + REACH * nx, 8), :].astype(jnp.int32) for ref in (ya_ref, yb_ref))
                for where, kind in ((low, jnp.where(even_y, b, a)), (high, jnp.where(even_y, a, b))):
                    perms2[where, :], stores2[where, :] = rock_of(kind, tables)
        start = c * side_rows + 2 * REACH * nx
        a, b = fraction(ya_ref[pl.ds(start, nx), :]), fraction(yb_ref[pl.ds(start, nx), :])
        at = c * nx * pitch
        frac2[pl.ds(at + PAD - 1, nx, stride=pitch), :] = jnp.where(even_y, b, a)
        frac2[pl.ds(at + PAD + ny, nx, stride=pitch), :] = jnp.where(even_y, a, b)
        both = 2 * PASSES
        for k in range(PASSES):
            start = (c * 2 * PASSES + k) * both
            a, b = ca_ref[pl.ds(start, both), :], cb_ref[pl.ds(start, both), :]
            ends = ((1 + k, jnp.where(even_x, b, a)), (REACH + nx + k, jnp.where(even_x, a, b)))
            start += PASSES * both
            a, b = (ref[pl.ds(start, both), :].astype(jnp.int32) for ref in (ca_ref, cb_ref))
            kinds = (jnp.where(even_x, b, a), jnp.where(even_x, a, b))
            for (layer, value), kind in zip(ends, kinds):
                for ref, new in zip((press2, perms2, stores2), (value, *rock_of(kind, tables))):
                    at = c * depth + layer * pitch + PAD
                    ref[pl.ds(at - PASSES, PASSES), :] = new[:PASSES]
                    ref[pl.ds(at + ny, PASSES), :] = new[PASSES:]

    def complete(group, _):
        for first in (PAD - PASSES, PAD + ny - 1):
            def rows(k, by, c):
                return pl.ds(c * depth + (1 + group * 8 + by) * pitch + first + k, 8, stride=pitch)

            perm = {k: [perms2[rows(k, 0, c), :] for c in range(chunks)] for k in range(-1, PASSES + 2)}
            t_s = [transmit(perm[-1][c], perm[0][c]) for c in range(chunks)]
            for c in range(chunks):
                ty2[rows(-1, 0, c), :] = t_s[c]
            for k in range(PASSES + 1):
                deep = deeper(perm[k])
                t_z = [transmit(perm[k][c], deep[c]) for c in range(chunks)]
                t_z[-1] = jnp.where(lane == LANES - 1, 0.0, t_z[-1])
                above = shallower(t_z)
                for c in range(chunks):
                    at = rows(k, 0, c)
                    t_x = transmit(perm[k][c], perms2[rows(k, 1, c), :])
                    t_w = transmit(perm[k][c], perms2[rows(k, -1, c), :])
                    t_n = transmit(perm[k][c], perm[k + 1][c])
                    tx2[at, :], ty2[at, :], tz2[at, :] = t_x, t_n, t_z[c]
                    store = stores2[at, :]
                    factor = OMEGA / (store + ((t_x + t_w) + (t_n + t_s[c]) + (t_z[c] + above[c])))
                    scale2[at, :] = factor
                    drive2[at, :] = factor * (store * press2[at, :] + rates2[at, :])
                    t_s[c] = t_n
        return 0

    lax.fori_loop(0, (layers - 2) // 8, complete, 0)

    def relax(source, target, number):
        def one(layer, _):
            def rows(k, c, by=0):
                return pl.ds(c * depth + (layer + by) * pitch + PAD - PASSES + k, 8, stride=tiles)

            now = {k: [source[rows(k, c), :] for c in range(chunks)] for k in range(-1, tiles + 1)}
            for k in range(tiles):
                here = now[k]
                t_z = [tz2[rows(k, c), :] for c in range(chunks)]
                deep = deeper(here)
                shallow = shallower([t_z[c] * here[c] for c in range(chunks)])
                for c in range(chunks):
                    at = rows(k, c)
                    total = (
                        (tx2[at, :] * source[rows(k, c, 1), :] + tx2[rows(k, c, -1), :] * source[rows(k, c, -1), :])
                        + (ty2[at, :] * now[k + 1][c] + ty2[rows(k - 1, c), :] * now[k - 1][c])
                        + (t_z[c] * deep[c] + shallow[c])
                    )
                    target[at, :] = (1.0 - OMEGA) * here[c] + (drive2[at, :] + scale2[at, :] * total)
            return 0

        lax.fori_loop(min(number + 1, REACH), layers - number, one, 0, unroll=UNROLL)

    for number in range(1, PASSES + 1):
        source, target = (press2, other2) if number % 2 else (other2, press2)
        relax(source, target, number)
    final2 = press2 if PASSES % 2 == 0 else other2

    def send_out(start):
        for c in range(chunks):
            copy = pltpu.make_async_copy(leave.at[c], press_ref.at[:, :, pl.ds(c * LANES, LANES)], sems.at[2, c])
            copy.start() if start else copy.wait()

    def gather(layer, _):
        for c in range(chunks):
            for k in range(step):
                at = pl.ds(c * depth + (REACH + layer) * pitch + PAD + k, 8, stride=step)
                leave2[pl.ds((c * nx + layer) * ny + k, 8, stride=step), :] = final2[at, :]
        return 0

    step = ny // 8
    lax.fori_loop(0, nx, gather, 0)
    send_out(True)
    fetch(flux_ref, flux, sems.at[0], False)
    for c in range(chunks):
        inlet_ref[pl.ds(c * ny, ny), :] = flux[c, 0]

    def fluxes(layer, _):
        def wide(ref, k, by=0):
            return [ref[pl.ds(c * depth + (REACH + layer + by) * pitch + PAD + k, 8, stride=step), :] for c in range(chunks)]

        def own(ref, k):
            return [ref[pl.ds((c * nx + layer) * ny + k, 8, stride=step), :] for c in range(chunks)]

        here = {k: wide(final2, k) for k in range(-1, step + 1)}
        old = {
            k: [frac2[pl.ds((c * nx + layer) * pitch + PAD + k, 8, stride=step), :] for c in range(chunks)]
            for k in range(-1, step + 1)
        }
        south = None
        for k in range(-1, step):
            t_y = wide(ty2, k)
            north = [upwind(t_y[c] * (here[k][c] - here[k + 1][c]), old[k][c], old[k + 1][c]) for c in range(chunks)]
            if k >= 0:
                t_z, below, old_below = wide(tz2, k), deeper(here[k]), deeper(old[k])
                down = [upwind(t_z[c] * (here[k][c] - below[c]), old[k][c], old_below[c]) for c in range(chunks)]
                from_above = shallower(down)
                east, t_x, rate, store = wide(final2, k, 1), wide(tx2, k), wide(rates2, k), wide(stores2, k)
                imposed, water, bend = own(flux2, k), own(sat2, k), own(slope2, k)
                for c in range(chunks):
                    leaving = (north[c] - south[c]) + (down[c] - from_above[c])
                    explicit = jnp.maximum(rate[c], 0.0) + jnp.minimum(rate[c], 0.0) * old[k][c] - leaving
                    through = jnp.maximum(imposed[c] + t_x[c] * (here[k][c] - east[c]), 0.0)
                    volume = store[c] * (1.0 / COMPRESS)
                    gain = 1.0 / (volume + through * bend[c])
                    first = water[c] - (through * old[k][c] - explicit) * gain
                    for i, value in enumerate((first, gain, through, volume, volume * water[c] + explicit)):
                        prep_ref[layer, pl.ds((i * chunks + c) * ny + k, 8, stride=step), :] = value
            south = north
        return 0

    lax.fori_loop(0, nx, fluxes, 0, unroll=2)
    send_out(False)


def flow(block, base_flux, saturation, sides, ends_corner, rates, made, rock_perm, rock_poro):
    nx, ny, nz = block
    chunks = nz // LANES
    *fields, slope = made
    own = pltpu.VMEM((chunks, nx, ny, LANES), jnp.float32)
    inputs = (base_flux, saturation, *sides, *ends_corner, rates, slope, rock_perm, rock_poro, *fields)
    first = len(inputs) - len(fields)
    return pl.pallas_call(
        functools.partial(flow_kernel, block),
        name="flow",
        out_shape=tuple(jax.ShapeDtypeStruct(f.shape, f.dtype) for f in fields) + (
            jax.ShapeDtypeStruct(block, jnp.float32),
            jax.ShapeDtypeStruct((nx, 5 * chunks * ny, LANES), jnp.float32),
            jax.ShapeDtypeStruct((chunks * ny, LANES), jnp.float32),
        ),
        in_specs=[HBM] + [VMEM] * 7 + [SMEM] * 2 + [VMEM] * len(fields),
        out_specs=(VMEM,) * len(fields) + (HBM, VMEM, VMEM),
        input_output_aliases={first + i: i for i in range(len(fields))},
        scratch_shapes=[pltpu.VMEM(wide_shape(block).shape, jnp.float32), own, own, pltpu.SemaphoreType.DMA((3, chunks))],
        compiler_params=pltpu.CompilerParams(vmem_limit_bytes=FLOW_LIMIT),
    )(*inputs)[-3:]


def stage_kernel(stage, last, inflow_ref, prep_ref, *refs):
    nx, rows, _ = prep_ref.shape
    plane = rows // 5
    if last:
        held_ref, out_ref, sat, sems = refs
    else:
        sat, out_ref = refs[-2:]
    chunks, _, ny, _ = sat.shape
    mine = lax.axis_index("gx") == stage

    def send(layer):
        return [
            pltpu.make_async_copy(sat.at[c, layer], out_ref.at[layer, :, pl.ds(c * LANES, LANES)], sems.at[layer, c])
            for c in range(chunks)
        ]

    @pl.when(mine)
    def _():
        def advance(layer, incoming):
            first, gain, through, volume, base = (prep_ref[layer, pl.ds(i * plane, plane), :] for i in range(5))
            known = base + incoming
            water = jnp.clip(first + gain * incoming, 0.0, 1.0)
            for _ in range(NEWTON - 1):
                square = water * water
                part = 1.5 * square
                denom = part + (0.5 - water)
                denom = denom * denom
                top = denom * known + through * (square * (0.5 - part))
                bottom = denom * volume + through * (water - square)
                water = jnp.clip(top / bottom, 0.0, 1.0)
            for c in range(chunks):
                sat[c, layer] = water[c * ny : (c + 1) * ny]
            if last:
                for copy in send(layer):
                    copy.start()
            square = water * water
            return (through * square) / (1.5 * square + (0.5 - water))

        outflow = lax.fori_loop(0, nx, advance, inflow_ref[...], unroll=STAGE_UNROLL)
        if not last:
            out_ref[...] = outflow
        else:
            def finish(layer, _):
                for copy in send(layer):
                    copy.wait()
                return 0

            lax.fori_loop(0, nx, finish, 0)

    if last:
        @pl.when(jnp.logical_not(mine))
        def _():
            copies = [
                pltpu.make_async_copy(held_ref.at[c], out_ref.at[:, :, pl.ds(c * LANES, LANES)], sems.at[0, c])
                for c in range(chunks)
            ]
            for copy in copies:
                copy.start()
            for copy in copies:
                copy.wait()


def run_stage(stage, last, inflow, prep, block, held):
    nx, ny, nz = block
    chunks = nz // LANES
    own = (chunks, nx, ny, LANES)
    return pl.pallas_call(
        functools.partial(stage_kernel, stage, last),
        name="stage",
        out_shape=(
            jax.ShapeDtypeStruct(block, jnp.float32)
            if last
            else (jax.ShapeDtypeStruct(own, jnp.float32), jax.ShapeDtypeStruct(inflow.shape, jnp.float32))
        ),
        in_specs=[VMEM] * (2 + len(held)),
        out_specs=HBM if last else (VMEM, VMEM),
        input_output_aliases={2: 0} if held and not last else {},
        scratch_shapes=[pltpu.VMEM(own, jnp.float32), pltpu.SemaphoreType.DMA((nx, chunks))] if last else [],
        compiler_params=pltpu.CompilerParams(vmem_limit_bytes=4 << 20),
    )(inflow, prep, *held)


def step(rock_type, rock_perm, rock_poro, base_flux, initial_pressure, old_saturation, well_cells, well_rates):
    nx = rock_type.shape[0]
    sides = pack_sides(initial_pressure, rock_type, old_saturation)
    sides_got = swap(*sides, "gy")
    ends = swap(*pack_ends(initial_pressure, rock_type, sides[0]), "gx")
    block = rock_type.shape
    *fields, frac, slope, water, rates = ready_own(initial_pressure, rock_type, old_saturation, well_cells, well_rates, rock_perm, rock_poro)
    ends_corner = swap(*corners(*sides_got, nx, slope), "gx")
    fields = ready_ends(block, ends, rates, rock_perm, rock_poro, fields)
    made = (*fields, frac, slope)
    pressure, prep, inflow = flow(block, base_flux, water, sides_got, ends_corner, rates, made, rock_perm, rock_poro)
    swept = ()
    count = lax.axis_size("gx")
    assert count > 1
    for stage in range(count - 1):
        *swept, outflow = run_stage(stage, False, inflow, prep, block, swept)
        inflow = lax.ppermute(outflow, "gx", [(stage, stage + 1)])
    saturation = run_stage(count - 1, True, inflow, prep, block, swept)
    return pressure, saturation


def solution(mesh):
    return jax.shard_map(
        step,
        mesh=mesh,
        in_specs=(
            P("gx", "gy", None),
            P(),
            P(),
            P("gx", "gy", None),
            P("gx", "gy", None),
            P("gx", "gy", None),
            P(),
            P(),
        ),
        out_specs=(P("gx", "gy", None), P("gx", "gy", None)),
        check_vma=False,
    )
```

```python
import functools
import math

import jax
import jax.numpy as jnp
from jax import lax
from jax.experimental import pallas as pl
from jax.experimental.pallas import tpu as pltpu
from jax.sharding import PartitionSpec as P


PASSES = 4
NEWTON = 3

MOBILITY = 0.5
OMEGA = 0.8
VOLUME = 4.0
COMPRESS = 0.5

LANES = 128
STAGE_UNROLL = 2
UNROLL = 4
ENDS_LIMIT = 59 << 20
SIDES_LIMIT = 62 << 20
OWN_LIMIT = 5 << 20
FLOW_LIMIT = 8 << 20
REACH = PASSES + 1
PAD = REACH + 1
HBM = pl.BlockSpec(memory_space=pltpu.MemorySpace.HBM)
VMEM = pl.BlockSpec(memory_space=pltpu.VMEM)
SMEM = pl.BlockSpec(memory_space=pltpu.SMEM)


def swap_pairs(axis):
    count = lax.axis_size(axis)
    pairs = []
    for first in (0, 1):
        ups = [(i, i + 1) for i in range(first, count - 1, 2)]
        pairs.append(ups + [(j, i) for i, j in ups])
    return pairs


def swap(value_a, value_b, axis):
    pairs_a, pairs_b = swap_pairs(axis)
    got_a = lax.ppermute(value_a, axis, pairs_a)
    got_b = lax.ppermute(value_b, axis, pairs_b)
    return got_a, got_b


def fetch(source, target, sems, start):
    for c in range(target.shape[0]):
        copy = pltpu.make_async_copy(source.at[:, :, pl.ds(c * LANES, LANES)], target.at[c], sems.at[c])
        copy.start() if start else copy.wait()


def pack_sides_kernel(p_ref, rock_ref, sat_ref, ya_ref, yb_ref, p, rock, sat, sems):
    chunks, nx = p.shape[1], p.shape[2]
    ny = p_ref.shape[1]
    even = lax.rem(lax.axis_index("gy"), 2) == 0
    outs = ((ya_ref, even), (yb_ref, jnp.logical_not(even)))

    def copies(i):
        _, high = outs[i]
        tile = pl.ds(pl.multiple_of(jnp.where(high, ny - 8, 0), 8), 8)
        return [
            pltpu.make_async_copy(source.at[:, tile, pl.ds(c * LANES, LANES)], target.at[i, c], sems.at[i, n, c])
            for n, (source, target) in enumerate(((p_ref, p), (rock_ref, rock), (sat_ref, sat)))
            for c in range(chunks)
        ]

    for i in range(2):
        for copy in copies(i):
            copy.start()
    p2, rock2, sat2 = (f.reshape(2 * chunks * nx * 8, LANES) for f in (p, rock, sat))
    rows = (2 * REACH + 1) * nx
    for i, (out, high) in enumerate(outs):
        for copy in copies(i):
            copy.wait()
        first = jnp.where(high, 8 - REACH, 0)
        edge = jnp.where(high, 7, 0)
        for c in range(chunks):
            base = (i * chunks + c) * nx * 8
            for j in range(REACH):
                out[pl.ds(c * rows + j * nx, nx), :] = p2[pl.ds(base + first + j, nx, stride=8), :]
                kinds = rock2[pl.ds(base + first + j, nx, stride=8), :]
                out[pl.ds(c * rows + (REACH + j) * nx, nx), :] = kinds.astype(jnp.float32) + 1.0
            out[pl.ds(c * rows + 2 * REACH * nx, nx), :] = sat2[pl.ds(base + edge, nx, stride=8), :]


def pack_sides(pressure, rock_type, saturation):
    nx, _, nz = pressure.shape
    chunks = nz // LANES
    side = jax.ShapeDtypeStruct((chunks * (2 * REACH + 1) * nx, LANES), jnp.float32)
    block = (2, chunks, nx, 8, LANES)
    return pl.pallas_call(
        pack_sides_kernel,
        name="pack_sides",
        out_shape=(side, side),
        in_specs=[HBM] * 3,
        out_specs=(VMEM,) * 2,
        scratch_shapes=[
            pltpu.VMEM(block, jnp.float32),
            pltpu.VMEM(block, jnp.int32),
            pltpu.VMEM(block, jnp.float32),
            pltpu.SemaphoreType.DMA((2, 3, chunks)),
        ],
        compiler_params=pltpu.CompilerParams(vmem_limit_bytes=SIDES_LIMIT),
    )(pressure, rock_type, saturation)


def pack_ends_kernel(p_ref, rock_ref, _, xa_ref, xb_ref, rock, sems):
    nx = p_ref.shape[0]
    chunks = xa_ref.shape[0]
    even = lax.rem(lax.axis_index("gx"), 2) == 0
    outs = (xa_ref, xb_ref)
    copies = []
    for i, high in enumerate((even, jnp.logical_not(even))):
        layers = pl.ds(jnp.where(high, nx - REACH, 0), REACH)
        for c in range(chunks):
            lanes = pl.ds(c * LANES, LANES)
            copies.append((
                pltpu.make_async_copy(rock_ref.at[layers, :, lanes], rock.at[i, c], sems.at[i, c, 0]),
                pltpu.make_async_copy(p_ref.at[layers, :, lanes], outs[i].at[c, pl.ds(0, REACH)], sems.at[i, c, 1]),
            ))
    for pair in copies:
        for copy in pair:
            copy.start()
    for i in range(2):
        for c in range(chunks):
            copies[i * chunks + c][0].wait()
            outs[i][c, pl.ds(REACH, REACH)] = rock[i, c].astype(jnp.float32) + 1.0
    for pair in copies:
        pair[1].wait()


def pack_ends(pressure, rock_type, after):
    _, ny, nz = pressure.shape
    chunks = nz // LANES
    end = jax.ShapeDtypeStruct((chunks, 2 * REACH, ny, LANES), jnp.float32)
    return pl.pallas_call(
        pack_ends_kernel,
        name="pack_ends",
        out_shape=(end, end),
        in_specs=[HBM] * 2 + [pl.BlockSpec(memory_space=pl.ANY)],
        out_specs=(VMEM,) * 2,
        scratch_shapes=[pltpu.VMEM((2, chunks, REACH, ny, LANES), jnp.int32), pltpu.SemaphoreType.DMA((2, chunks, 2))],
        compiler_params=pltpu.CompilerParams(vmem_limit_bytes=ENDS_LIMIT),
    )(pressure, rock_type, after)


def corner_kernel(nx, ya_ref, yb_ref, _, ca_ref, cb_ref):
    rows = (2 * REACH + 1) * nx
    chunks = ya_ref.shape[0] // rows
    even_y = lax.rem(lax.axis_index("gy"), 2) == 0
    even_x = lax.rem(lax.axis_index("gx"), 2) == 0
    for out, high in ((ca_ref, even_x), (cb_ref, jnp.logical_not(even_x))):
        layer = jnp.where(high, nx - PASSES, 0)
        for c in range(chunks):
            for kind in range(2):
                for i in range(PASSES):
                    for side in range(2):
                        start = c * rows + (kind * REACH + 1 - side) * nx + layer + i
                        from_a = ya_ref[pl.ds(start, PASSES, stride=nx), :]
                        from_b = yb_ref[pl.ds(start, PASSES, stride=nx), :]
                        mine = jnp.where(even_y, from_b, from_a) if side == 0 else jnp.where(even_y, from_a, from_b)
                        at = ((c * 2 + kind) * PASSES + i) * 2 + side
                        out[pl.ds(at * PASSES, PASSES), :] = mine


def corners(side_a, side_b, nx, after):
    chunks = side_a.shape[0] // ((2 * REACH + 1) * nx)
    shape = jax.ShapeDtypeStruct((chunks * 4 * PASSES * PASSES, LANES), jnp.float32)
    return pl.pallas_call(
        functools.partial(corner_kernel, nx),
        name="corners",
        out_shape=(shape, shape),
        in_specs=[VMEM] * 2 + [pl.BlockSpec(memory_space=pl.ANY)],
        out_specs=(VMEM,) * 2,
        compiler_params=pltpu.CompilerParams(vmem_limit_bytes=4 << 20),
    )(side_a, side_b, after)


def fraction(water):
    denom = water * water + MOBILITY * (1.0 - water) ** 2
    return water * water / denom


def transmit(left, right):
    return 2.0 * left * right / jnp.maximum(left + right, 1e-30)


def look_up(table, kinds):
    return jnp.take_along_axis(table, kinds, axis=1, mode="promise_in_bounds")


def deeper(values):
    turned = [pltpu.roll(v, LANES - 1, 1) for v in values]
    last = lax.broadcasted_iota(jnp.int32, turned[0].shape, 1) == LANES - 1
    return [jnp.where(last, turned[(c + 1) % len(values)], turned[c]) for c in range(len(values))]


def shallower(values):
    turned = [pltpu.roll(v, 1, 1) for v in values]
    first = lax.broadcasted_iota(jnp.int32, turned[0].shape, 1) == 0
    return [jnp.where(first, turned[c - 1], turned[c]) for c in range(len(values))]


def upwind(flow, own, far):
    return jnp.maximum(flow, 0.0) * own + jnp.minimum(flow, 0.0) * far


def flat(ref):
    return ref.reshape(math.prod(ref.shape[:-1]), LANES)


def rock_tables(perm_ref, poro_ref):
    lane = lax.broadcasted_iota(jnp.int32, (8, LANES), 1)
    table = jnp.zeros((8, LANES), jnp.float32)
    for kind in range(perm_ref.shape[0]):
        table = jnp.where(lane == kind + 1, perm_ref[kind], table)
    return table, [COMPRESS * (VOLUME * poro_ref[kind]) for kind in range(perm_ref.shape[0])]


def rock_of(kind, tables):
    table, stores = tables
    store = jnp.ones(kind.shape, jnp.float32)
    for i, value in enumerate(stores):
        store = jnp.where(kind == i + 1, value, store)
    return look_up(table, kind), store


def fill_rates(block, cells_ref, rates_ref, out_ref):
    (nx, ny, _), (_, layers, pitch) = block, wide_sizes(block)
    rank_x, rank_y = lax.axis_index("gx"), lax.axis_index("gy")
    sub = lax.broadcasted_iota(jnp.int32, (8, LANES), 0)
    lane = lax.broadcasted_iota(jnp.int32, (8, LANES), 1)
    share = out_ref.shape[0] // layers
    low_x, low_y = rank_x * nx - REACH, rank_y * ny - PAD

    def clear(i, _):
        out_ref[pl.ds(pl.multiple_of(i * share, 8), share), :] = jnp.zeros((share, LANES), jnp.float32)
        return 0

    lax.fori_loop(0, layers, clear, 0)

    def some_wells(first, count):
        def place(w):
            return cells_ref[0, w] - low_x, cells_ref[1, w] - low_y

        near = [(x >= 0) & (x < layers) & (y >= 0) & (y < pitch) for x, y in map(place, (first + i for i in range(count)))]

        @pl.when(functools.reduce(jnp.logical_or, near))
        def _():
            for i in range(count):
                @pl.when(near[i])
                def _(w=first + i):
                    (x, y), z = place(w), cells_ref[2, w]
                    row = (lax.shift_right_logical(z, 7) * layers + x) * pitch + y
                    tile = pl.multiple_of(lax.shift_left(lax.shift_right_logical(row, 3), 3), 8)
                    here = (sub == row - tile) & (lane == lax.bitwise_and(z, LANES - 1))
                    out_ref[pl.ds(tile, 8), :] = out_ref[pl.ds(tile, 8), :] + jnp.where(here, rates_ref[w], 0.0)

    wells, batch = cells_ref.shape[1], 8

    def wells_of(i, _):
        some_wells(i * batch, batch)
        return 0

    lax.fori_loop(0, wells // batch, wells_of, 0)
    if wells % batch:
        some_wells(wells - wells % batch, wells % batch)


def wide_sizes(block):
    nx, ny, nz = block
    return nz // LANES, nx + 2 * REACH, ny + 2 * PAD


def wide_shape(block):
    rows = math.prod(wide_sizes(block))
    assert block[0] % 8 == 0 and block[1] % 8 == 0 and block[2] % LANES == 0
    return jax.ShapeDtypeStruct((rows, LANES), jnp.float32)


def prepare_layers(block, fields, rates, first, last):
    press, perms, stores, trans_x, trans_y, trans_z, scale, drive = fields
    chunks, layers, pitch = wide_sizes(block)
    step = block[1] // 8
    lane = lax.broadcasted_iota(jnp.int32, (8, LANES), 1)

    def rows(layer, k, c):
        return pl.ds((c * layers + layer) * pitch + PAD + k, 8, stride=step)

    def prepare(layer, _):
        perm = {k: [perms[rows(layer, k, c), :] for c in range(chunks)] for k in range(-1, step + 1)}
        t_s = [transmit(perm[-1][c], perm[0][c]) for c in range(chunks)]
        for k in range(step):
            deep = deeper(perm[k])
            t_z = [transmit(perm[k][c], deep[c]) for c in range(chunks)]
            t_z[-1] = jnp.where(lane == LANES - 1, 0.0, t_z[-1])
            above = shallower(t_z)
            for c in range(chunks):
                at = rows(layer, k, c)
                t_x = transmit(perm[k][c], perms[rows(layer + 1, k, c), :])
                t_n = transmit(perm[k][c], perm[k + 1][c])
                t_w = trans_x[rows(jnp.maximum(layer - 1, 0), k, c), :]
                trans_x[at, :], trans_y[at, :], trans_z[at, :] = t_x, t_n, t_z[c]
                store = stores[at, :]
                factor = OMEGA / (store + ((t_x + t_w) + (t_n + t_s[c]) + (t_z[c] + above[c])))
                scale[at, :] = factor
                drive[at, :] = factor * (store * press[at, :] + rates[at, :])
                t_s[c] = t_n
        return 0

    lax.fori_loop(first, last, prepare, 0, unroll=2)


def edge_groups(block):
    nx = block[0]
    inside, outside = [], []
    for group in range((nx + 2 * REACH - 2) // 8):
        low, high = 1 + group * 8, 8 + group * 8
        (inside if low > REACH and high < REACH + nx - 1 else outside).append(group)
    return inside, outside


def complete_rows(block, fields, rates, group):
    press, perms, stores, trans_x, trans_y, trans_z, scale, drive = fields
    chunks, layers, pitch = wide_sizes(block)
    lane = lax.broadcasted_iota(jnp.int32, (8, LANES), 1)
    for first in (PAD - PASSES, PAD + block[1] - 1):
        def rows(k, by, c):
            return pl.ds((c * layers + 1 + group * 8 + by) * pitch + first + k, 8, stride=pitch)

        perm = {k: [perms[rows(k, 0, c), :] for c in range(chunks)] for k in range(-1, PASSES + 2)}
        t_s = [transmit(perm[-1][c], perm[0][c]) for c in range(chunks)]
        for c in range(chunks):
            trans_y[rows(-1, 0, c), :] = t_s[c]
        for k in range(PASSES + 1):
            deep = deeper(perm[k])
            t_z = [transmit(perm[k][c], deep[c]) for c in range(chunks)]
            t_z[-1] = jnp.where(lane == LANES - 1, 0.0, t_z[-1])
            above = shallower(t_z)
            for c in range(chunks):
                at = rows(k, 0, c)
                t_x = transmit(perm[k][c], perms[rows(k, 1, c), :])
                t_w = transmit(perm[k][c], perms[rows(k, -1, c), :])
                t_n = transmit(perm[k][c], perm[k + 1][c])
                trans_x[at, :], trans_y[at, :], trans_z[at, :] = t_x, t_n, t_z[c]
                store = stores[at, :]
                factor = OMEGA / (store + ((t_x + t_w) + (t_n + t_s[c]) + (t_z[c] + above[c])))
                scale[at, :] = factor
                drive[at, :] = factor * (store * press[at, :] + rates[at, :])
                t_s[c] = t_n


def ready_own_kernel(block, rock_ref, p_ref, sat_ref, cells_ref, well_ref, perm_ref, poro_ref, *refs):
    fields, (frac, slope, sat, rates_ref, rock, p, sems) = refs[:8], refs[8:]
    sources = ((rock_ref, rock), (p_ref, p), (sat_ref, sat))
    for i, (source, target) in enumerate(sources):
        fetch(source, target, sems.at[i], True)
    fill_rates(block, cells_ref, well_ref, rates_ref)
    press, perms, stores = fields[:3]
    (nx, ny, _), (chunks, layers, pitch) = block, wide_sizes(block)
    step = ny // 8
    tables = rock_tables(perm_ref, poro_ref)
    p2, rock2, sat2, slope2 = map(flat, (p, rock, sat, slope))
    for i, (source, target) in enumerate(sources):
        fetch(source, target, sems.at[i], False)

    def look(layer, _):
        for c in range(chunks):
            for k in range(step):
                own = pl.ds((c * nx + layer) * ny + k, 8, stride=step)
                at = pl.ds((c * layers + REACH + layer) * pitch + PAD + k, 8, stride=step)
                kind = rock2[own, :] + 1
                perms[at, :], stores[at, :] = rock_of(kind, tables)
                press[at, :] = p2[own, :]
        return 0

    lax.fori_loop(0, nx, look, 0, unroll=4)
    prepare_layers(block, fields, rates_ref, REACH, REACH + nx)

    def old_fraction(layer, _):
        for c in range(chunks):
            for k in range(step):
                own = pl.ds((c * nx + layer) * ny + k, 8, stride=step)
                s = sat2[own, :]
                inverse = 1.0 / (s * s + MOBILITY * (1.0 - s) ** 2)
                frac[pl.ds((c * nx + layer) * pitch + PAD + k, 8, stride=step), :] = s * s * inverse
                slope2[own, :] = 2.0 * MOBILITY * s * (1.0 - s) * (inverse * inverse)
        return 0

    lax.fori_loop(0, nx, old_fraction, 0, unroll=4)


def ready_own(pressure, rock_type, saturation, well_cells, well_rates, rock_perm, rock_poro):
    block = pressure.shape
    (nx, ny, _), (chunks, _, pitch) = block, wide_sizes(block)
    own = (chunks, nx, ny, LANES)
    return pl.pallas_call(
        functools.partial(ready_own_kernel, block),
        name="ready_own",
        out_shape=(wide_shape(block),) * 8
        + tuple(jax.ShapeDtypeStruct(shape, jnp.float32) for shape in ((chunks * nx * pitch, LANES), own, own))
        + (wide_shape(block),),
        in_specs=[HBM] * 3 + [SMEM] * 4,
        out_specs=(VMEM,) * 12,
        scratch_shapes=[
            pltpu.VMEM(own, jnp.int32),
            pltpu.VMEM(own, jnp.float32),
            pltpu.SemaphoreType.DMA((3, chunks)),
        ],
        cost_estimate=pl.CostEstimate(flops=0, bytes_accessed=24 << 20, transcendentals=0),
        compiler_params=pltpu.CompilerParams(vmem_limit_bytes=OWN_LIMIT),
    )(rock_type, pressure, saturation, well_cells, well_rates, rock_perm, rock_poro)


def ready_ends_kernel(block, xa_ref, xb_ref, ya_ref, yb_ref, rates_ref, perm_ref, poro_ref, *refs):
    fields = refs[8:16]
    even_y = lax.rem(lax.axis_index("gy"), 2) == 0
    press, perms, stores = fields[:3]
    (nx, ny, _), (chunks, layers, pitch) = block, wide_sizes(block)
    step = ny // 8
    even = lax.rem(lax.axis_index("gx"), 2) == 0
    tables = rock_tables(perm_ref, poro_ref)
    a2, b2 = flat(xa_ref), flat(xb_ref)

    def look(j, _):
        for c in range(chunks):
            for k in range(step):
                got = pl.ds((c * 2 * REACH + j) * ny + k, 8, stride=step)
                kinds_got = pl.ds((c * 2 * REACH + REACH + j) * ny + k, 8, stride=step)
                for low in (True, False):
                    at = pl.ds((c * layers + j + (0 if low else REACH + nx)) * pitch + PAD + k, 8, stride=step)
                    one, two = (b2, a2) if low else (a2, b2)
                    press[at, :] = jnp.where(even, one[got, :], two[got, :])
                    kind = jnp.where(even, one[kinds_got, :], two[kinds_got, :]).astype(jnp.int32)
                    perms[at, :], stores[at, :] = rock_of(kind, tables)
        return 0

    lax.fori_loop(0, REACH, look, 0, unroll=True)
    prepare_layers(block, fields, rates_ref, 0, REACH + 1)
    prepare_layers(block, fields, rates_ref, REACH + nx - 1, layers - 1)
    for c in range(chunks):
        for j in range(REACH):
            for half in range(nx // 8):
                start = (c * (2 * REACH + 1) + j) * nx + half * 8
                at = (c * layers + REACH + half * 8) * pitch + j
                low = pl.ds(at + PAD - REACH, 8, stride=pitch)
                high = pl.ds(at + PAD + ny, 8, stride=pitch)
                a, b = ya_ref[pl.ds(start, 8), :], yb_ref[pl.ds(start, 8), :]
                press[low, :], press[high, :] = jnp.where(even_y, b, a), jnp.where(even_y, a, b)
                a, b = (ref[pl.ds(start + REACH * nx, 8), :].astype(jnp.int32) for ref in (ya_ref, yb_ref))
                for where, kind in ((low, jnp.where(even_y, b, a)), (high, jnp.where(even_y, a, b))):
                    perms[where, :], stores[where, :] = rock_of(kind, tables)
    for group in edge_groups(block)[0]:
        complete_rows(block, fields, rates_ref, group)


def ready_ends(block, ends, sides, rates, rock_perm, rock_poro, fields):
    inputs = (*ends, *sides, rates, rock_perm, rock_poro, *fields)
    return pl.pallas_call(
        functools.partial(ready_ends_kernel, block),
        name="ready_ends",
        out_shape=tuple(jax.ShapeDtypeStruct(f.shape, f.dtype) for f in fields),
        in_specs=[VMEM] * 5 + [SMEM] * 2 + [VMEM] * len(fields),
        out_specs=(VMEM,) * len(fields),
        input_output_aliases={7 + i: i for i in range(len(fields))},
        cost_estimate=pl.CostEstimate(flops=0, bytes_accessed=9 << 20, transcendentals=0),
        compiler_params=pltpu.CompilerParams(vmem_limit_bytes=4 << 20),
    )(*inputs)


def flow_kernel(
    block, flux_ref, sat, ya_ref, yb_ref, ca_ref, cb_ref, rates_ref, slope_ref, perm_ref, poro_ref, *refs
):
    press, perms, stores, trans_x, trans_y, trans_z, scale, drive, frac = refs[9:18]
    press_ref, prep_ref, inlet_ref, other, leave, flux, sems = refs[18:]
    (nx, ny, _), (chunks, layers, pitch) = block, wide_sizes(block)
    depth, step = layers * pitch, ny // 8
    tiles = (ny + 2 * PASSES) // 8
    side_rows = (2 * REACH + 1) * nx
    even_x, even_y = lax.rem(lax.axis_index("gx"), 2) == 0, lax.rem(lax.axis_index("gy"), 2) == 0
    press2, other2, perms2, stores2, rates2, frac2 = press, other, perms, stores, rates_ref, frac
    tx2, ty2, tz2, scale2, drive2 = trans_x, trans_y, trans_z, scale, drive
    flux2, sat2, slope2, leave2 = map(flat, (flux, sat, slope_ref, leave))
    fetch(flux_ref, flux, sems.at[0], True)
    tables = rock_tables(perm_ref, poro_ref)
    lane = lax.broadcasted_iota(jnp.int32, (8, LANES), 1)

    for c in range(chunks):
        start = c * side_rows + 2 * REACH * nx
        a, b = fraction(ya_ref[pl.ds(start, nx), :]), fraction(yb_ref[pl.ds(start, nx), :])
        at = c * nx * pitch
        frac2[pl.ds(at + PAD - 1, nx, stride=pitch), :] = jnp.where(even_y, b, a)
        frac2[pl.ds(at + PAD + ny, nx, stride=pitch), :] = jnp.where(even_y, a, b)
        both = 2 * PASSES
        for k in range(PASSES):
            start = (c * 2 * PASSES + k) * both
            a, b = ca_ref[pl.ds(start, both), :], cb_ref[pl.ds(start, both), :]
            ends = ((1 + k, jnp.where(even_x, b, a)), (REACH + nx + k, jnp.where(even_x, a, b)))
            start += PASSES * both
            a, b = (ref[pl.ds(start, both), :].astype(jnp.int32) for ref in (ca_ref, cb_ref))
            kinds = (jnp.where(even_x, b, a), jnp.where(even_x, a, b))
            for (layer, value), kind in zip(ends, kinds):
                for ref, new in zip((press2, perms2, stores2), (value, *rock_of(kind, tables))):
                    at = c * depth + layer * pitch + PAD
                    ref[pl.ds(at - PASSES, PASSES), :] = new[:PASSES]
                    ref[pl.ds(at + ny, PASSES), :] = new[PASSES:]

    for group in edge_groups(block)[1]:
        complete_rows(block, (press, perms, stores, trans_x, trans_y, trans_z, scale, drive), rates_ref, group)

    def relax(source, target, number):
        def one(layer, _):
            def rows(k, c, by=0):
                return pl.ds(c * depth + (layer + by) * pitch + PAD - PASSES + k, 8, stride=tiles)

            now = {k: [source[rows(k, c), :] for c in range(chunks)] for k in range(-1, tiles + 1)}
            for k in range(tiles):
                here = now[k]
                t_z = [tz2[rows(k, c), :] for c in range(chunks)]
                deep = deeper(here)
                shallow = shallower([t_z[c] * here[c] for c in range(chunks)])
                for c in range(chunks):
                    at = rows(k, c)
                    total = (
                        (tx2[at, :] * source[rows(k, c, 1), :] + tx2[rows(k, c, -1), :] * source[rows(k, c, -1), :])
                        + (ty2[at, :] * now[k + 1][c] + ty2[rows(k - 1, c), :] * now[k - 1][c])
                        + (t_z[c] * deep[c] + shallow[c])
                    )
                    target[at, :] = (1.0 - OMEGA) * here[c] + (drive2[at, :] + scale2[at, :] * total)
            return 0

        lax.fori_loop(min(number + 1, REACH), layers - number, one, 0, unroll=UNROLL)

    for number in range(1, PASSES + 1):
        source, target = (press2, other2) if number % 2 else (other2, press2)
        relax(source, target, number)
    final2 = press2 if PASSES % 2 == 0 else other2

    def send_out(start):
        for c in range(chunks):
            copy = pltpu.make_async_copy(leave.at[c], press_ref.at[:, :, pl.ds(c * LANES, LANES)], sems.at[2, c])
            copy.start() if start else copy.wait()

    def gather(layer, _):
        for c in range(chunks):
            for k in range(step):
                at = pl.ds(c * depth + (REACH + layer) * pitch + PAD + k, 8, stride=step)
                leave2[pl.ds((c * nx + layer) * ny + k, 8, stride=step), :] = final2[at, :]
        return 0

    step = ny // 8
    lax.fori_loop(0, nx, gather, 0)
    send_out(True)
    fetch(flux_ref, flux, sems.at[0], False)
    for c in range(chunks):
        inlet_ref[pl.ds(c * ny, ny), :] = flux[c, 0]

    def fluxes(layer, _):
        def wide(ref, k, by=0):
            return [ref[pl.ds(c * depth + (REACH + layer + by) * pitch + PAD + k, 8, stride=step), :] for c in range(chunks)]

        def own(ref, k):
            return [ref[pl.ds((c * nx + layer) * ny + k, 8, stride=step), :] for c in range(chunks)]

        here = {k: wide(final2, k) for k in range(-1, step + 1)}
        old = {
            k: [frac2[pl.ds((c * nx + layer) * pitch + PAD + k, 8, stride=step), :] for c in range(chunks)]
            for k in range(-1, step + 1)
        }
        south = None
        for k in range(-1, step):
            t_y = wide(ty2, k)
            north = [upwind(t_y[c] * (here[k][c] - here[k + 1][c]), old[k][c], old[k + 1][c]) for c in range(chunks)]
            if k >= 0:
                t_z, below, old_below = wide(tz2, k), deeper(here[k]), deeper(old[k])
                down = [upwind(t_z[c] * (here[k][c] - below[c]), old[k][c], old_below[c]) for c in range(chunks)]
                from_above = shallower(down)
                east, t_x, rate, store = wide(final2, k, 1), wide(tx2, k), wide(rates2, k), wide(stores2, k)
                imposed, water, bend = own(flux2, k), own(sat2, k), own(slope2, k)
                for c in range(chunks):
                    leaving = (north[c] - south[c]) + (down[c] - from_above[c])
                    explicit = jnp.maximum(rate[c], 0.0) + jnp.minimum(rate[c], 0.0) * old[k][c] - leaving
                    through = jnp.maximum(imposed[c] + t_x[c] * (here[k][c] - east[c]), 0.0)
                    volume = store[c] * (1.0 / COMPRESS)
                    gain = 1.0 / (volume + through * bend[c])
                    first = water[c] - (through * old[k][c] - explicit) * gain
                    for i, value in enumerate((first, gain, through, volume, volume * water[c] + explicit)):
                        prep_ref[layer, pl.ds((i * chunks + c) * ny + k, 8, stride=step), :] = value
            south = north
        return 0

    lax.fori_loop(0, nx, fluxes, 0, unroll=2)
    send_out(False)


def flow(block, base_flux, saturation, sides, ends_corner, rates, made, rock_perm, rock_poro):
    nx, ny, nz = block
    chunks = nz // LANES
    *fields, slope = made
    own = pltpu.VMEM((chunks, nx, ny, LANES), jnp.float32)
    inputs = (base_flux, saturation, *sides, *ends_corner, rates, slope, rock_perm, rock_poro, *fields)
    first = len(inputs) - len(fields)
    return pl.pallas_call(
        functools.partial(flow_kernel, block),
        name="flow",
        out_shape=tuple(jax.ShapeDtypeStruct(f.shape, f.dtype) for f in fields) + (
            jax.ShapeDtypeStruct(block, jnp.float32),
            jax.ShapeDtypeStruct((nx, 5 * chunks * ny, LANES), jnp.float32),
            jax.ShapeDtypeStruct((chunks * ny, LANES), jnp.float32),
        ),
        in_specs=[HBM] + [VMEM] * 7 + [SMEM] * 2 + [VMEM] * len(fields),
        out_specs=(VMEM,) * len(fields) + (HBM, VMEM, VMEM),
        input_output_aliases={first + i: i for i in range(len(fields))},
        scratch_shapes=[pltpu.VMEM(wide_shape(block).shape, jnp.float32), own, own, pltpu.SemaphoreType.DMA((3, chunks))],
        compiler_params=pltpu.CompilerParams(vmem_limit_bytes=FLOW_LIMIT),
    )(*inputs)[-3:]


def stage_kernel(stage, last, inflow_ref, prep_ref, *refs):
    nx, rows, _ = prep_ref.shape
    plane = rows // 5
    if last:
        held_ref, out_ref, sat, sems = refs
    else:
        sat, out_ref = refs[-2:]
    chunks, _, ny, _ = sat.shape
    mine = lax.axis_index("gx") == stage

    def send(first, count, slot):
        return [
            pltpu.make_async_copy(
                sat.at[c, pl.ds(first, count)], out_ref.at[pl.ds(first, count), :, pl.ds(c * LANES, LANES)], sems.at[slot, c]
            )
            for c in range(chunks)
        ]

    @pl.when(mine)
    def _():
        def advance(layer, incoming):
            first, gain, through, volume, base = (prep_ref[layer, pl.ds(i * plane, plane), :] for i in range(5))
            known = base + incoming
            water = jnp.clip(first + gain * incoming, 0.0, 1.0)
            for _ in range(NEWTON - 1):
                square = water * water
                part = 1.5 * square
                denom = part + (0.5 - water)
                denom = denom * denom
                top = denom * known + through * (square * (0.5 - part))
                bottom = denom * volume + through * (water - square)
                water = jnp.clip(top / bottom, 0.0, 1.0)
            for c in range(chunks):
                sat[c, layer] = water[c * ny : (c + 1) * ny]
            square = water * water
            return (through * square) / (1.5 * square + (0.5 - water))

        outflow, parts, done = inflow_ref[...], [], 0
        for slot, count in enumerate((nx // 2, nx // 4, nx - nx // 2 - nx // 4) if last else (nx,)):
            outflow = lax.fori_loop(done, done + count, advance, outflow, unroll=STAGE_UNROLL)
            if last:
                parts.append(send(done, count, slot))
                for copy in parts[-1]:
                    copy.start()
            done += count
        if not last:
            out_ref[...] = outflow
        for part in parts:
            for copy in part:
                copy.wait()

    if last:
        @pl.when(jnp.logical_not(mine))
        def _():
            copies = [
                pltpu.make_async_copy(held_ref.at[c], out_ref.at[:, :, pl.ds(c * LANES, LANES)], sems.at[0, c])
                for c in range(chunks)
            ]
            for copy in copies:
                copy.start()
            for copy in copies:
                copy.wait()


def run_stage(stage, last, inflow, prep, block, held):
    nx, ny, nz = block
    chunks = nz // LANES
    own = (chunks, nx, ny, LANES)
    return pl.pallas_call(
        functools.partial(stage_kernel, stage, last),
        name="stage",
        out_shape=(
            jax.ShapeDtypeStruct(block, jnp.float32)
            if last
            else (jax.ShapeDtypeStruct(own, jnp.float32), jax.ShapeDtypeStruct(inflow.shape, jnp.float32))
        ),
        in_specs=[VMEM] * (2 + len(held)),
        out_specs=HBM if last else (VMEM, VMEM),
        input_output_aliases={2: 0} if held and not last else {},
        scratch_shapes=[pltpu.VMEM(own, jnp.float32), pltpu.SemaphoreType.DMA((3, chunks))] if last else [],
        compiler_params=pltpu.CompilerParams(vmem_limit_bytes=4 << 20),
    )(inflow, prep, *held)


def step(rock_type, rock_perm, rock_poro, base_flux, initial_pressure, old_saturation, well_cells, well_rates):
    nx = rock_type.shape[0]
    sides = pack_sides(initial_pressure, rock_type, old_saturation)
    sides_got = swap(*sides, "gy")
    ends = swap(*pack_ends(initial_pressure, rock_type, sides[0]), "gx")
    block = rock_type.shape
    *fields, frac, slope, water, rates = ready_own(initial_pressure, rock_type, old_saturation, well_cells, well_rates, rock_perm, rock_poro)
    ends_corner = swap(*corners(*sides_got, nx, slope), "gx")
    fields = ready_ends(block, ends, sides_got, rates, rock_perm, rock_poro, fields)
    made = (*fields, frac, slope)
    pressure, prep, inflow = flow(block, base_flux, water, sides_got, ends_corner, rates, made, rock_perm, rock_poro)
    swept = ()
    count = lax.axis_size("gx")
    assert count > 1
    for stage in range(count - 1):
        *swept, outflow = run_stage(stage, False, inflow, prep, block, swept)
        inflow = lax.ppermute(outflow, "gx", [(stage, stage + 1)])
    saturation = run_stage(count - 1, True, inflow, prep, block, swept)
    return pressure, saturation


def solution(mesh):
    return jax.shard_map(
        step,
        mesh=mesh,
        in_specs=(
            P("gx", "gy", None),
            P(),
            P(),
            P("gx", "gy", None),
            P("gx", "gy", None),
            P("gx", "gy", None),
            P(),
            P(),
        ),
        out_specs=(P("gx", "gy", None), P("gx", "gy", None)),
        check_vma=False,
    )
```

```python
import functools
import math

import jax
import jax.numpy as jnp
from jax import lax
from jax.experimental import pallas as pl
from jax.experimental.pallas import tpu as pltpu
from jax.sharding import PartitionSpec as P


PASSES = 4
NEWTON = 3

MOBILITY = 0.5
OMEGA = 0.8
VOLUME = 4.0
COMPRESS = 0.5

LANES = 128
STAGE_UNROLL = 2
UNROLL = 4
ENDS_LIMIT = 4 << 20
SIDES_LIMIT = 6 << 20
OWN_LIMIT = 5 << 20
FLOW_LIMIT = 8 << 20
REACH = PASSES + 1
PAD = REACH + 1
HBM = pl.BlockSpec(memory_space=pltpu.MemorySpace.HBM)
VMEM = pl.BlockSpec(memory_space=pltpu.VMEM)
SMEM = pl.BlockSpec(memory_space=pltpu.SMEM)


def swap_pairs(axis):
    count = lax.axis_size(axis)
    pairs = []
    for first in (0, 1):
        ups = [(i, i + 1) for i in range(first, count - 1, 2)]
        pairs.append(ups + [(j, i) for i, j in ups])
    return pairs


def swap(value_a, value_b, axis):
    pairs_a, pairs_b = swap_pairs(axis)
    got_a = lax.ppermute(value_a, axis, pairs_a)
    got_b = lax.ppermute(value_b, axis, pairs_b)
    return got_a, got_b


def fetch(source, target, sems, start):
    for c in range(target.shape[0]):
        copy = pltpu.make_async_copy(source.at[:, :, pl.ds(c * LANES, LANES)], target.at[c], sems.at[c])
        copy.start() if start else copy.wait()


def pack_sides_kernel(p_ref, rock_ref, sat_ref, ya_ref, yb_ref, p, rock, sat, sems):
    chunks, nx = p.shape[1], p.shape[2]
    ny = p_ref.shape[1]
    even = lax.rem(lax.axis_index("gy"), 2) == 0
    outs = ((ya_ref, even), (yb_ref, jnp.logical_not(even)))

    def copies(i):
        _, high = outs[i]
        tile = pl.ds(pl.multiple_of(jnp.where(high, ny - 8, 0), 8), 8)
        return [
            pltpu.make_async_copy(source.at[:, tile, pl.ds(c * LANES, LANES)], target.at[i, c], sems.at[i, n, c])
            for n, (source, target) in enumerate(((p_ref, p), (rock_ref, rock), (sat_ref, sat)))
            for c in range(chunks)
        ]

    for i in range(2):
        for copy in copies(i):
            copy.start()
    p2, rock2, sat2 = (f.reshape(2 * chunks * nx * 8, LANES) for f in (p, rock, sat))
    rows = (2 * REACH + 1) * nx
    for i, (out, high) in enumerate(outs):
        for copy in copies(i):
            copy.wait()
        first = jnp.where(high, 8 - REACH, 0)
        edge = jnp.where(high, 7, 0)
        for c in range(chunks):
            base = (i * chunks + c) * nx * 8
            for j in range(REACH):
                out[pl.ds(c * rows + j * nx, nx), :] = p2[pl.ds(base + first + j, nx, stride=8), :]
                kinds = rock2[pl.ds(base + first + j, nx, stride=8), :]
                out[pl.ds(c * rows + (REACH + j) * nx, nx), :] = kinds.astype(jnp.float32) + 1.0
            out[pl.ds(c * rows + 2 * REACH * nx, nx), :] = sat2[pl.ds(base + edge, nx, stride=8), :]


def pack_sides(pressure, rock_type, saturation):
    nx, _, nz = pressure.shape
    chunks = nz // LANES
    side = jax.ShapeDtypeStruct((chunks * (2 * REACH + 1) * nx, LANES), jnp.float32)
    block = (2, chunks, nx, 8, LANES)
    return pl.pallas_call(
        pack_sides_kernel,
        name="pack_sides",
        out_shape=(side, side),
        in_specs=[HBM] * 3,
        out_specs=(VMEM,) * 2,
        scratch_shapes=[
            pltpu.VMEM(block, jnp.float32),
            pltpu.VMEM(block, jnp.int32),
            pltpu.VMEM(block, jnp.float32),
            pltpu.SemaphoreType.DMA((2, 3, chunks)),
        ],
        compiler_params=pltpu.CompilerParams(vmem_limit_bytes=SIDES_LIMIT),
    )(pressure, rock_type, saturation)


def pack_ends_kernel(p_ref, rock_ref, _, xa_ref, xb_ref, rock, sems):
    nx = p_ref.shape[0]
    chunks = xa_ref.shape[0]
    even = lax.rem(lax.axis_index("gx"), 2) == 0
    outs = (xa_ref, xb_ref)
    copies = []
    for i, high in enumerate((even, jnp.logical_not(even))):
        layers = pl.ds(jnp.where(high, nx - REACH, 0), REACH)
        for c in range(chunks):
            lanes = pl.ds(c * LANES, LANES)
            copies.append((
                pltpu.make_async_copy(rock_ref.at[layers, :, lanes], rock.at[i, c], sems.at[i, c, 0]),
                pltpu.make_async_copy(p_ref.at[layers, :, lanes], outs[i].at[c, pl.ds(0, REACH)], sems.at[i, c, 1]),
            ))
    for pair in copies:
        for copy in pair:
            copy.start()
    for i in range(2):
        for c in range(chunks):
            copies[i * chunks + c][0].wait()
            outs[i][c, pl.ds(REACH, REACH)] = rock[i, c].astype(jnp.float32) + 1.0
    for pair in copies:
        pair[1].wait()


def pack_ends(pressure, rock_type, after):
    _, ny, nz = pressure.shape
    chunks = nz // LANES
    end = jax.ShapeDtypeStruct((chunks, 2 * REACH, ny, LANES), jnp.float32)
    return pl.pallas_call(
        pack_ends_kernel,
        name="pack_ends",
        out_shape=(end, end),
        in_specs=[HBM] * 2 + [pl.BlockSpec(memory_space=pl.ANY)],
        out_specs=(VMEM,) * 2,
        scratch_shapes=[pltpu.VMEM((2, chunks, REACH, ny, LANES), jnp.int32), pltpu.SemaphoreType.DMA((2, chunks, 2))],
        compiler_params=pltpu.CompilerParams(vmem_limit_bytes=ENDS_LIMIT),
    )(pressure, rock_type, after)


def corner_kernel(nx, ya_ref, yb_ref, _, ca_ref, cb_ref):
    rows = (2 * REACH + 1) * nx
    chunks = ya_ref.shape[0] // rows
    even_y = lax.rem(lax.axis_index("gy"), 2) == 0
    even_x = lax.rem(lax.axis_index("gx"), 2) == 0
    for out, high in ((ca_ref, even_x), (cb_ref, jnp.logical_not(even_x))):
        layer = jnp.where(high, nx - PASSES, 0)
        for c in range(chunks):
            for kind in range(2):
                for i in range(PASSES):
                    for side in range(2):
                        start = c * rows + (kind * REACH + 1 - side) * nx + layer + i
                        from_a = ya_ref[pl.ds(start, PASSES, stride=nx), :]
                        from_b = yb_ref[pl.ds(start, PASSES, stride=nx), :]
                        mine = jnp.where(even_y, from_b, from_a) if side == 0 else jnp.where(even_y, from_a, from_b)
                        at = ((c * 2 + kind) * PASSES + i) * 2 + side
                        out[pl.ds(at * PASSES, PASSES), :] = mine


def corners(side_a, side_b, nx, after):
    chunks = side_a.shape[0] // ((2 * REACH + 1) * nx)
    shape = jax.ShapeDtypeStruct((chunks * 4 * PASSES * PASSES, LANES), jnp.float32)
    return pl.pallas_call(
        functools.partial(corner_kernel, nx),
        name="corners",
        out_shape=(shape, shape),
        in_specs=[VMEM] * 2 + [pl.BlockSpec(memory_space=pl.ANY)],
        out_specs=(VMEM,) * 2,
        compiler_params=pltpu.CompilerParams(vmem_limit_bytes=4 << 20),
    )(side_a, side_b, after)


def fraction(water):
    denom = water * water + MOBILITY * (1.0 - water) ** 2
    return water * water / denom


def transmit(left, right):
    return 2.0 * left * right / jnp.maximum(left + right, 1e-30)


def look_up(table, kinds):
    return jnp.take_along_axis(table, kinds, axis=1, mode="promise_in_bounds")


def deeper(values):
    turned = [pltpu.roll(v, LANES - 1, 1) for v in values]
    last = lax.broadcasted_iota(jnp.int32, turned[0].shape, 1) == LANES - 1
    return [jnp.where(last, turned[(c + 1) % len(values)], turned[c]) for c in range(len(values))]


def shallower(values):
    turned = [pltpu.roll(v, 1, 1) for v in values]
    first = lax.broadcasted_iota(jnp.int32, turned[0].shape, 1) == 0
    return [jnp.where(first, turned[c - 1], turned[c]) for c in range(len(values))]


def upwind(flow, own, far):
    return jnp.maximum(flow, 0.0) * own + jnp.minimum(flow, 0.0) * far


def flat(ref):
    return ref.reshape(math.prod(ref.shape[:-1]), LANES)


def rock_tables(perm_ref, poro_ref):
    lane = lax.broadcasted_iota(jnp.int32, (8, LANES), 1)
    table = jnp.zeros((8, LANES), jnp.float32)
    for kind in range(perm_ref.shape[0]):
        table = jnp.where(lane == kind + 1, perm_ref[kind], table)
    return table, [COMPRESS * (VOLUME * poro_ref[kind]) for kind in range(perm_ref.shape[0])]


def rock_of(kind, tables):
    table, stores = tables
    store = jnp.ones(kind.shape, jnp.float32)
    for i, value in enumerate(stores):
        store = jnp.where(kind == i + 1, value, store)
    return look_up(table, kind), store


def fill_rates(block, cells_ref, rates_ref, out_ref):
    (nx, ny, _), (_, layers, pitch) = block, wide_sizes(block)
    rank_x, rank_y = lax.axis_index("gx"), lax.axis_index("gy")
    sub = lax.broadcasted_iota(jnp.int32, (8, LANES), 0)
    lane = lax.broadcasted_iota(jnp.int32, (8, LANES), 1)
    share = out_ref.shape[0] // layers
    low_x, low_y = rank_x * nx - REACH, rank_y * ny - PAD

    def clear(i, _):
        out_ref[pl.ds(pl.multiple_of(i * share, 8), share), :] = jnp.zeros((share, LANES), jnp.float32)
        return 0

    lax.fori_loop(0, layers, clear, 0)

    def some_wells(first, count):
        def place(w):
            return cells_ref[0, w] - low_x, cells_ref[1, w] - low_y

        near = [(x >= 0) & (x < layers) & (y >= 0) & (y < pitch) for x, y in map(place, (first + i for i in range(count)))]

        @pl.when(functools.reduce(jnp.logical_or, near))
        def _():
            for i in range(count):
                @pl.when(near[i])
                def _(w=first + i):
                    (x, y), z = place(w), cells_ref[2, w]
                    row = (lax.shift_right_logical(z, 7) * layers + x) * pitch + y
                    tile = pl.multiple_of(lax.shift_left(lax.shift_right_logical(row, 3), 3), 8)
                    here = (sub == row - tile) & (lane == lax.bitwise_and(z, LANES - 1))
                    out_ref[pl.ds(tile, 8), :] = out_ref[pl.ds(tile, 8), :] + jnp.where(here, rates_ref[w], 0.0)

    wells, batch = cells_ref.shape[1], 8

    def wells_of(i, _):
        some_wells(i * batch, batch)
        return 0

    lax.fori_loop(0, wells // batch, wells_of, 0)
    if wells % batch:
        some_wells(wells - wells % batch, wells % batch)


def wide_sizes(block):
    nx, ny, nz = block
    return nz // LANES, nx + 2 * REACH, ny + 2 * PAD


def wide_shape(block):
    rows = math.prod(wide_sizes(block))
    assert block[0] % 8 == 0 and block[1] % 8 == 0 and block[2] % LANES == 0
    return jax.ShapeDtypeStruct((rows, LANES), jnp.float32)


def prepare_layers(block, fields, rates, first, last):
    press, perms, stores, trans_x, trans_y, trans_z, scale, drive = fields
    chunks, layers, pitch = wide_sizes(block)
    step = block[1] // 8
    lane = lax.broadcasted_iota(jnp.int32, (8, LANES), 1)

    def rows(layer, k, c):
        return pl.ds((c * layers + layer) * pitch + PAD + k, 8, stride=step)

    def prepare(layer, _):
        perm = {k: [perms[rows(layer, k, c), :] for c in range(chunks)] for k in range(-1, step + 1)}
        t_s = [transmit(perm[-1][c], perm[0][c]) for c in range(chunks)]
        for k in range(step):
            deep = deeper(perm[k])
            t_z = [transmit(perm[k][c], deep[c]) for c in range(chunks)]
            t_z[-1] = jnp.where(lane == LANES - 1, 0.0, t_z[-1])
            above = shallower(t_z)
            for c in range(chunks):
                at = rows(layer, k, c)
                t_x = transmit(perm[k][c], perms[rows(layer + 1, k, c), :])
                t_n = transmit(perm[k][c], perm[k + 1][c])
                t_w = trans_x[rows(jnp.maximum(layer - 1, 0), k, c), :]
                trans_x[at, :], trans_y[at, :], trans_z[at, :] = t_x, t_n, t_z[c]
                store = stores[at, :]
                factor = OMEGA / (store + ((t_x + t_w) + (t_n + t_s[c]) + (t_z[c] + above[c])))
                scale[at, :] = factor
                drive[at, :] = factor * (store * press[at, :] + rates[at, :])
                t_s[c] = t_n
        return 0

    lax.fori_loop(first, last, prepare, 0, unroll=2)


def edge_groups(block):
    nx = block[0]
    inside, outside = [], []
    for group in range((nx + 2 * REACH - 2) // 8):
        low, high = 1 + group * 8, 8 + group * 8
        (inside if low > REACH and high < REACH + nx - 1 else outside).append(group)
    return inside, outside


def complete_rows(block, fields, rates, group):
    press, perms, stores, trans_x, trans_y, trans_z, scale, drive = fields
    chunks, layers, pitch = wide_sizes(block)
    lane = lax.broadcasted_iota(jnp.int32, (8, LANES), 1)
    for first in (PAD - PASSES, PAD + block[1] - 1):
        def rows(k, by, c):
            return pl.ds((c * layers + 1 + group * 8 + by) * pitch + first + k, 8, stride=pitch)

        perm = {k: [perms[rows(k, 0, c), :] for c in range(chunks)] for k in range(-1, PASSES + 2)}
        t_s = [transmit(perm[-1][c], perm[0][c]) for c in range(chunks)]
        for c in range(chunks):
            trans_y[rows(-1, 0, c), :] = t_s[c]
        for k in range(PASSES + 1):
            deep = deeper(perm[k])
            t_z = [transmit(perm[k][c], deep[c]) for c in range(chunks)]
            t_z[-1] = jnp.where(lane == LANES - 1, 0.0, t_z[-1])
            above = shallower(t_z)
            for c in range(chunks):
                at = rows(k, 0, c)
                t_x = transmit(perm[k][c], perms[rows(k, 1, c), :])
                t_w = transmit(perm[k][c], perms[rows(k, -1, c), :])
                t_n = transmit(perm[k][c], perm[k + 1][c])
                trans_x[at, :], trans_y[at, :], trans_z[at, :] = t_x, t_n, t_z[c]
                store = stores[at, :]
                factor = OMEGA / (store + ((t_x + t_w) + (t_n + t_s[c]) + (t_z[c] + above[c])))
                scale[at, :] = factor
                drive[at, :] = factor * (store * press[at, :] + rates[at, :])
                t_s[c] = t_n


def ready_own_kernel(block, rock_ref, p_ref, sat_ref, cells_ref, well_ref, perm_ref, poro_ref, *refs):
    fields, (frac, slope, sat, rates_ref, rock, p, sems) = refs[:8], refs[8:]
    sources = ((rock_ref, rock), (p_ref, p), (sat_ref, sat))
    for i, (source, target) in enumerate(sources):
        fetch(source, target, sems.at[i], True)
    fill_rates(block, cells_ref, well_ref, rates_ref)
    press, perms, stores = fields[:3]
    (nx, ny, _), (chunks, layers, pitch) = block, wide_sizes(block)
    step = ny // 8
    tables = rock_tables(perm_ref, poro_ref)
    p2, rock2, sat2, slope2 = map(flat, (p, rock, sat, slope))
    for i, (source, target) in enumerate(sources):
        fetch(source, target, sems.at[i], False)

    def look(layer, _):
        for c in range(chunks):
            for k in range(step):
                own = pl.ds((c * nx + layer) * ny + k, 8, stride=step)
                at = pl.ds((c * layers + REACH + layer) * pitch + PAD + k, 8, stride=step)
                kind = rock2[own, :] + 1
                perms[at, :], stores[at, :] = rock_of(kind, tables)
                press[at, :] = p2[own, :]
        return 0

    lax.fori_loop(0, nx, look, 0, unroll=4)
    prepare_layers(block, fields, rates_ref, REACH, REACH + nx)

    def old_fraction(layer, _):
        for c in range(chunks):
            for k in range(step):
                own = pl.ds((c * nx + layer) * ny + k, 8, stride=step)
                s = sat2[own, :]
                inverse = 1.0 / (s * s + MOBILITY * (1.0 - s) ** 2)
                frac[pl.ds((c * nx + layer) * pitch + PAD + k, 8, stride=step), :] = s * s * inverse
                slope2[own, :] = 2.0 * MOBILITY * s * (1.0 - s) * (inverse * inverse)
        return 0

    lax.fori_loop(0, nx, old_fraction, 0, unroll=4)


def ready_own(pressure, rock_type, saturation, well_cells, well_rates, rock_perm, rock_poro):
    block = pressure.shape
    (nx, ny, _), (chunks, _, pitch) = block, wide_sizes(block)
    own = (chunks, nx, ny, LANES)
    return pl.pallas_call(
        functools.partial(ready_own_kernel, block),
        name="ready_own",
        out_shape=(wide_shape(block),) * 8
        + tuple(jax.ShapeDtypeStruct(shape, jnp.float32) for shape in ((chunks * nx * pitch, LANES), own, own))
        + (wide_shape(block),),
        in_specs=[HBM] * 3 + [SMEM] * 4,
        out_specs=(VMEM,) * 12,
        scratch_shapes=[
            pltpu.VMEM(own, jnp.int32),
            pltpu.VMEM(own, jnp.float32),
            pltpu.SemaphoreType.DMA((3, chunks)),
        ],
        cost_estimate=pl.CostEstimate(flops=0, bytes_accessed=24 << 20, transcendentals=0),
        compiler_params=pltpu.CompilerParams(vmem_limit_bytes=OWN_LIMIT),
    )(rock_type, pressure, saturation, well_cells, well_rates, rock_perm, rock_poro)


def ready_ends_kernel(block, xa_ref, xb_ref, ya_ref, yb_ref, rates_ref, perm_ref, poro_ref, *refs):
    fields = refs[8:16]
    even_y = lax.rem(lax.axis_index("gy"), 2) == 0
    press, perms, stores = fields[:3]
    (nx, ny, _), (chunks, layers, pitch) = block, wide_sizes(block)
    step = ny // 8
    even = lax.rem(lax.axis_index("gx"), 2) == 0
    tables = rock_tables(perm_ref, poro_ref)
    a2, b2 = flat(xa_ref), flat(xb_ref)

    def look(j, _):
        for c in range(chunks):
            for k in range(step):
                got = pl.ds((c * 2 * REACH + j) * ny + k, 8, stride=step)
                kinds_got = pl.ds((c * 2 * REACH + REACH + j) * ny + k, 8, stride=step)
                for low in (True, False):
                    at = pl.ds((c * layers + j + (0 if low else REACH + nx)) * pitch + PAD + k, 8, stride=step)
                    one, two = (b2, a2) if low else (a2, b2)
                    press[at, :] = jnp.where(even, one[got, :], two[got, :])
                    kind = jnp.where(even, one[kinds_got, :], two[kinds_got, :]).astype(jnp.int32)
                    perms[at, :], stores[at, :] = rock_of(kind, tables)
        return 0

    lax.fori_loop(0, REACH, look, 0, unroll=True)
    prepare_layers(block, fields, rates_ref, 0, REACH + 1)
    prepare_layers(block, fields, rates_ref, REACH + nx - 1, layers - 1)
    for c in range(chunks):
        for j in range(REACH):
            for half in range(nx // 8):
                start = (c * (2 * REACH + 1) + j) * nx + half * 8
                at = (c * layers + REACH + half * 8) * pitch + j
                low = pl.ds(at + PAD - REACH, 8, stride=pitch)
                high = pl.ds(at + PAD + ny, 8, stride=pitch)
                a, b = ya_ref[pl.ds(start, 8), :], yb_ref[pl.ds(start, 8), :]
                press[low, :], press[high, :] = jnp.where(even_y, b, a), jnp.where(even_y, a, b)
                a, b = (ref[pl.ds(start + REACH * nx, 8), :].astype(jnp.int32) for ref in (ya_ref, yb_ref))
                for where, kind in ((low, jnp.where(even_y, b, a)), (high, jnp.where(even_y, a, b))):
                    perms[where, :], stores[where, :] = rock_of(kind, tables)
    for group in edge_groups(block)[0]:
        complete_rows(block, fields, rates_ref, group)


def ready_ends(block, ends, sides, rates, rock_perm, rock_poro, fields):
    inputs = (*ends, *sides, rates, rock_perm, rock_poro, *fields)
    return pl.pallas_call(
        functools.partial(ready_ends_kernel, block),
        name="ready_ends",
        out_shape=tuple(jax.ShapeDtypeStruct(f.shape, f.dtype) for f in fields),
        in_specs=[VMEM] * 5 + [SMEM] * 2 + [VMEM] * len(fields),
        out_specs=(VMEM,) * len(fields),
        input_output_aliases={7 + i: i for i in range(len(fields))},
        cost_estimate=pl.CostEstimate(flops=0, bytes_accessed=9 << 20, transcendentals=0),
        compiler_params=pltpu.CompilerParams(vmem_limit_bytes=4 << 20),
    )(*inputs)


def flow_kernel(
    block, flux_ref, sat, ya_ref, yb_ref, ca_ref, cb_ref, rates_ref, slope_ref, perm_ref, poro_ref, *refs
):
    press, perms, stores, trans_x, trans_y, trans_z, scale, drive, frac = refs[9:18]
    press_ref, prep_ref, inlet_ref, other, leave, flux, sems = refs[18:]
    (nx, ny, _), (chunks, layers, pitch) = block, wide_sizes(block)
    depth, step = layers * pitch, ny // 8
    tiles = (ny + 2 * PASSES) // 8
    side_rows = (2 * REACH + 1) * nx
    even_x, even_y = lax.rem(lax.axis_index("gx"), 2) == 0, lax.rem(lax.axis_index("gy"), 2) == 0
    press2, other2, perms2, stores2, rates2, frac2 = press, other, perms, stores, rates_ref, frac
    tx2, ty2, tz2, scale2, drive2 = trans_x, trans_y, trans_z, scale, drive
    flux2, sat2, slope2, leave2 = map(flat, (flux, sat, slope_ref, leave))
    fetch(flux_ref, flux, sems.at[0], True)
    tables = rock_tables(perm_ref, poro_ref)
    lane = lax.broadcasted_iota(jnp.int32, (8, LANES), 1)

    for c in range(chunks):
        start = c * side_rows + 2 * REACH * nx
        a, b = fraction(ya_ref[pl.ds(start, nx), :]), fraction(yb_ref[pl.ds(start, nx), :])
        at = c * nx * pitch
        frac2[pl.ds(at + PAD - 1, nx, stride=pitch), :] = jnp.where(even_y, b, a)
        frac2[pl.ds(at + PAD + ny, nx, stride=pitch), :] = jnp.where(even_y, a, b)
        both = 2 * PASSES
        for k in range(PASSES):
            start = (c * 2 * PASSES + k) * both
            a, b = ca_ref[pl.ds(start, both), :], cb_ref[pl.ds(start, both), :]
            ends = ((1 + k, jnp.where(even_x, b, a)), (REACH + nx + k, jnp.where(even_x, a, b)))
            start += PASSES * both
            a, b = (ref[pl.ds(start, both), :].astype(jnp.int32) for ref in (ca_ref, cb_ref))
            kinds = (jnp.where(even_x, b, a), jnp.where(even_x, a, b))
            for (layer, value), kind in zip(ends, kinds):
                for ref, new in zip((press2, perms2, stores2), (value, *rock_of(kind, tables))):
                    at = c * depth + layer * pitch + PAD
                    ref[pl.ds(at - PASSES, PASSES), :] = new[:PASSES]
                    ref[pl.ds(at + ny, PASSES), :] = new[PASSES:]

    for group in edge_groups(block)[1]:
        complete_rows(block, (press, perms, stores, trans_x, trans_y, trans_z, scale, drive), rates_ref, group)

    def relax(source, target, number):
        def one(layer, _):
            def rows(k, c, by=0):
                return pl.ds(c * depth + (layer + by) * pitch + PAD - PASSES + k, 8, stride=tiles)

            now = {k: [source[rows(k, c), :] for c in range(chunks)] for k in range(-1, tiles + 1)}
            for k in range(tiles):
                here = now[k]
                t_z = [tz2[rows(k, c), :] for c in range(chunks)]
                deep = deeper(here)
                shallow = shallower([t_z[c] * here[c] for c in range(chunks)])
                for c in range(chunks):
                    at = rows(k, c)
                    total = (
                        (tx2[at, :] * source[rows(k, c, 1), :] + tx2[rows(k, c, -1), :] * source[rows(k, c, -1), :])
                        + (ty2[at, :] * now[k + 1][c] + ty2[rows(k - 1, c), :] * now[k - 1][c])
                        + (t_z[c] * deep[c] + shallow[c])
                    )
                    target[at, :] = (1.0 - OMEGA) * here[c] + (drive2[at, :] + scale2[at, :] * total)
            return 0

        lax.fori_loop(min(number + 1, REACH), layers - number, one, 0, unroll=UNROLL)

    for number in range(1, PASSES + 1):
        source, target = (press2, other2) if number % 2 else (other2, press2)
        relax(source, target, number)
    final2 = press2 if PASSES % 2 == 0 else other2

    def send_out(start):
        for c in range(chunks):
            copy = pltpu.make_async_copy(leave.at[c], press_ref.at[:, :, pl.ds(c * LANES, LANES)], sems.at[2, c])
            copy.start() if start else copy.wait()

    def gather(layer, _):
        for c in range(chunks):
            for k in range(step):
                at = pl.ds(c * depth + (REACH + layer) * pitch + PAD + k, 8, stride=step)
                leave2[pl.ds((c * nx + layer) * ny + k, 8, stride=step), :] = final2[at, :]
        return 0

    step = ny // 8
    lax.fori_loop(0, nx, gather, 0)
    send_out(True)
    fetch(flux_ref, flux, sems.at[0], False)
    for c in range(chunks):
        inlet_ref[pl.ds(c * ny, ny), :] = flux[c, 0]

    def fluxes(layer, _):
        def wide(ref, k, by=0):
            return [ref[pl.ds(c * depth + (REACH + layer + by) * pitch + PAD + k, 8, stride=step), :] for c in range(chunks)]

        def own(ref, k):
            return [ref[pl.ds((c * nx + layer) * ny + k, 8, stride=step), :] for c in range(chunks)]

        here = {k: wide(final2, k) for k in range(-1, step + 1)}
        old = {
            k: [frac2[pl.ds((c * nx + layer) * pitch + PAD + k, 8, stride=step), :] for c in range(chunks)]
            for k in range(-1, step + 1)
        }
        south = None
        for k in range(-1, step):
            t_y = wide(ty2, k)
            north = [upwind(t_y[c] * (here[k][c] - here[k + 1][c]), old[k][c], old[k + 1][c]) for c in range(chunks)]
            if k >= 0:
                t_z, below, old_below = wide(tz2, k), deeper(here[k]), deeper(old[k])
                down = [upwind(t_z[c] * (here[k][c] - below[c]), old[k][c], old_below[c]) for c in range(chunks)]
                from_above = shallower(down)
                east, t_x, rate, store = wide(final2, k, 1), wide(tx2, k), wide(rates2, k), wide(stores2, k)
                imposed, water, bend = own(flux2, k), own(sat2, k), own(slope2, k)
                for c in range(chunks):
                    leaving = (north[c] - south[c]) + (down[c] - from_above[c])
                    explicit = jnp.maximum(rate[c], 0.0) + jnp.minimum(rate[c], 0.0) * old[k][c] - leaving
                    through = jnp.maximum(imposed[c] + t_x[c] * (here[k][c] - east[c]), 0.0)
                    volume = store[c] * (1.0 / COMPRESS)
                    gain = 1.0 / (volume + through * bend[c])
                    first = water[c] - (through * old[k][c] - explicit) * gain
                    for i, value in enumerate((first, gain, through, volume, volume * water[c] + explicit)):
                        prep_ref[layer, pl.ds((i * chunks + c) * ny + k, 8, stride=step), :] = value
            south = north
        return 0

    lax.fori_loop(0, nx, fluxes, 0, unroll=2)
    send_out(False)


def flow(block, base_flux, saturation, sides, ends_corner, rates, made, rock_perm, rock_poro):
    nx, ny, nz = block
    chunks = nz // LANES
    *fields, slope = made
    own = pltpu.VMEM((chunks, nx, ny, LANES), jnp.float32)
    inputs = (base_flux, saturation, *sides, *ends_corner, rates, slope, rock_perm, rock_poro, *fields)
    first = len(inputs) - len(fields)
    return pl.pallas_call(
        functools.partial(flow_kernel, block),
        name="flow",
        out_shape=tuple(jax.ShapeDtypeStruct(f.shape, f.dtype) for f in fields) + (
            jax.ShapeDtypeStruct(block, jnp.float32),
            jax.ShapeDtypeStruct((nx, 5 * chunks * ny, LANES), jnp.float32),
            jax.ShapeDtypeStruct((chunks * ny, LANES), jnp.float32),
        ),
        in_specs=[HBM] + [VMEM] * 7 + [SMEM] * 2 + [VMEM] * len(fields),
        out_specs=(VMEM,) * len(fields) + (HBM, VMEM, VMEM),
        input_output_aliases={first + i: i for i in range(len(fields))},
        scratch_shapes=[pltpu.VMEM(wide_shape(block).shape, jnp.float32), own, own, pltpu.SemaphoreType.DMA((3, chunks))],
        compiler_params=pltpu.CompilerParams(vmem_limit_bytes=FLOW_LIMIT),
    )(*inputs)[-3:]


def stage_kernel(stage, last, inflow_ref, prep_ref, *refs):
    nx, rows, _ = prep_ref.shape
    plane = rows // 5
    if last:
        held_ref, out_ref, sat, sems = refs
    else:
        sat, out_ref = refs[-2:]
    chunks, _, ny, _ = sat.shape
    mine = lax.axis_index("gx") == stage

    def send(first, count, slot):
        return [
            pltpu.make_async_copy(
                sat.at[c, pl.ds(first, count)], out_ref.at[pl.ds(first, count), :, pl.ds(c * LANES, LANES)], sems.at[slot, c]
            )
            for c in range(chunks)
        ]

    @pl.when(mine)
    def _():
        def advance(layer, incoming):
            first, gain, through, volume, base = (prep_ref[layer, pl.ds(i * plane, plane), :] for i in range(5))
            known = base + incoming
            water = jnp.clip(first + gain * incoming, 0.0, 1.0)
            for _ in range(NEWTON - 1):
                square = water * water
                part = 1.5 * square
                denom = part + (0.5 - water)
                denom = denom * denom
                top = denom * known + through * (square * (0.5 - part))
                bottom = denom * volume + through * (water - square)
                water = jnp.clip(top / bottom, 0.0, 1.0)
            for c in range(chunks):
                sat[c, layer] = water[c * ny : (c + 1) * ny]
            square = water * water
            return (through * square) / (1.5 * square + (0.5 - water))

        outflow, parts, done = inflow_ref[...], [], 0
        for slot, count in enumerate((nx // 2, nx // 4, nx - nx // 2 - nx // 4) if last else (nx,)):
            outflow = lax.fori_loop(done, done + count, advance, outflow, unroll=STAGE_UNROLL)
            if last:
                parts.append(send(done, count, slot))
                for copy in parts[-1]:
                    copy.start()
            done += count
        if not last:
            out_ref[...] = outflow
        for part in parts:
            for copy in part:
                copy.wait()

    if last:
        @pl.when(jnp.logical_not(mine))
        def _():
            copies = [
                pltpu.make_async_copy(held_ref.at[c], out_ref.at[:, :, pl.ds(c * LANES, LANES)], sems.at[0, c])
                for c in range(chunks)
            ]
            for copy in copies:
                copy.start()
            for copy in copies:
                copy.wait()


def run_stage(stage, last, inflow, prep, block, held):
    nx, ny, nz = block
    chunks = nz // LANES
    own = (chunks, nx, ny, LANES)
    return pl.pallas_call(
        functools.partial(stage_kernel, stage, last),
        name="stage",
        out_shape=(
            jax.ShapeDtypeStruct(block, jnp.float32)
            if last
            else (jax.ShapeDtypeStruct(own, jnp.float32), jax.ShapeDtypeStruct(inflow.shape, jnp.float32))
        ),
        in_specs=[VMEM] * (2 + len(held)),
        out_specs=HBM if last else (VMEM, VMEM),
        input_output_aliases={2: 0} if held and not last else {},
        scratch_shapes=[pltpu.VMEM(own, jnp.float32), pltpu.SemaphoreType.DMA((3, chunks))] if last else [],
        compiler_params=pltpu.CompilerParams(vmem_limit_bytes=4 << 20),
    )(inflow, prep, *held)


def step(rock_type, rock_perm, rock_poro, base_flux, initial_pressure, old_saturation, well_cells, well_rates):
    nx = rock_type.shape[0]
    initial_pressure, rock_type, old_saturation, base_flux = (
        pltpu.with_memory_space_constraint(f, pltpu.MemorySpace.HBM)
        for f in (initial_pressure, rock_type, old_saturation, base_flux)
    )
    sides = pack_sides(initial_pressure, rock_type, old_saturation)
    sides_got = swap(*sides, "gy")
    ends = swap(*pack_ends(initial_pressure, rock_type, sides[0]), "gx")
    block = rock_type.shape
    *fields, frac, slope, water, rates = ready_own(initial_pressure, rock_type, old_saturation, well_cells, well_rates, rock_perm, rock_poro)
    ends_corner = swap(*corners(*sides_got, nx, slope), "gx")
    fields = ready_ends(block, ends, sides_got, rates, rock_perm, rock_poro, fields)
    made = (*fields, frac, slope)
    pressure, prep, inflow = flow(block, base_flux, water, sides_got, ends_corner, rates, made, rock_perm, rock_poro)
    swept = ()
    count = lax.axis_size("gx")
    assert count > 1
    for stage in range(count - 1):
        *swept, outflow = run_stage(stage, False, inflow, prep, block, swept)
        inflow = lax.ppermute(outflow, "gx", [(stage, stage + 1)])
    saturation = run_stage(count - 1, True, inflow, prep, block, swept)
    return pressure, saturation


def solution(mesh):
    return jax.shard_map(
        step,
        mesh=mesh,
        in_specs=(
            P("gx", "gy", None),
            P(),
            P(),
            P("gx", "gy", None),
            P("gx", "gy", None),
            P("gx", "gy", None),
            P(),
            P(),
        ),
        out_specs=(P("gx", "gy", None), P("gx", "gy", None)),
        check_vma=False,
    )
```
